128 devices in a mesh: dp: 32 (over x, z, core), mp: 4 (over y).
Axes of the slice: x: 4, y: 4, z: 4, core: 2. Of those that a mesh axis runs over, the one named last changes fastest.
Arguments:
- hidden_in: bfloat16 [32768, 2048], P('dp', 'mp'), may hold values from -6 to 6
- token_ids: int32 [32768], P('dp'), may hold values from 0 to 128001, as said below
- passage_counts: int32 [64], P('dp'), may hold values from 1 to 4, as said below
- positive_doc: int32 [4096], P('dp'), may hold values from 0 to 63
- queries: bfloat16 [4096, 2048], P('dp', 'mp'), may hold values from -6 to 6
- norm_gain: float32 [2048], replicated, may hold values from 0.5 to 1.5
- w_gate: bfloat16 [2048, 7168], P(None, 'mp'), may hold values from -0.125 to 0.125
- w_up: bfloat16 [2048, 7168], P(None, 'mp'), may hold values from -0.125 to 0.125
- w_down: bfloat16 [7168, 2048], P('mp'), may hold values from -0.0625 to 0.0625
Outputs:
- query_loss: float32 [4096], P('dp')
- hidden_grad: bfloat16 [32768, 2048], P('dp', 'mp')
The draws below stay inside these ranges and needn't reach their ends.
Inputs may be any that keep to these rules, and one draw needn't show every extreme that they name: `passage_counts`: A document has 1 to 4 passages; every draw has a dp index whose documents all have 4. The live passages hold 160 passages in all. `token_ids`: 128001 marks padding; it stands only at the tail of a document's last live passage, and every live passage has a token that is not padding.
All inputs are finite; a program needn't handle non-finite values.
Results may differ from the reference program's by a relative error of at most 0.023.
Values may be sent and summed in bfloat16 or wider, within the bound.
No kernel may reach another device: no remote copies, remote signals or barrier semaphores. Data moves between devices by JAX's collectives and lax.ppermute only.
A program may use at most 128 MiB of HBM per device.

```python
import jax
import jax.numpy as jnp
from jax import lax

D = 2048
FF = 7168
L = 128
PMAX = 4
DOC_DEV = 2
CAP = 20
DOCS = 64
PASSAGES = 256
QUERIES = 4096
ROWS = 32768
N_DP = 32


pad_token = 128001


def make_counts(key):
    half = DOCS // 2
    order = jax.random.permutation(jax.random.fold_in(key, 101), half)
    base = 1 + order % PMAX
    heavy = jax.random.randint(jax.random.fold_in(key, 102), (), 0, half // DOC_DEV)
    base = jnp.where(jnp.arange(half) // DOC_DEV == heavy, PMAX, base)
    return jnp.concatenate([base, PMAX + 1 - base]).astype(jnp.int32)


def draw_passage_counts(key, part):
    return make_counts(key)


def draw_token_ids(key, part):
    counts = make_counts(key)
    passage_total = DOCS * PMAX
    passage_index = jnp.arange(passage_total, dtype=jnp.int32)
    last_live = passage_index % PMAX == jnp.repeat(counts, PMAX) - 1
    length = jax.random.randint(jax.random.fold_in(key, 106), (passage_total,), 1, L + 1)
    length = jnp.where(last_live, length, L)
    position = jnp.arange(L, dtype=jnp.int32)
    words = jax.random.randint(jax.random.fold_in(key, 107), (passage_total, L), 0, 128000)
    tokens = jnp.where(position[None, :] < length[:, None], words, pad_token)
    return tokens.reshape(passage_total * L).astype(jnp.int32)


def touch_ends(drawn, key, least, largest):
    place = [jax.random.randint(jax.random.fold_in(key, axis), (), 0, length) for axis, length in enumerate(drawn.shape)]
    widest = drawn.shape.index(max(drawn.shape))
    next_to = place[:widest] + [(place[widest] + 1) % drawn.shape[widest]] + place[widest + 1:]
    return drawn.at[tuple(place)].set(least).at[tuple(next_to)].set(largest)


def levels(own_key, extent, pieces, low, largest):
    def one(dim, shards_of):
        draws = jax.random.uniform(jax.random.fold_in(jax.random.fold_in(own_key, 6), dim), (shards_of,), jnp.float32, low / len(pieces), largest / len(pieces))
        return jnp.repeat(jnp.exp(draws), extent[dim] // shards_of).reshape((-1,) + (1,) * (len(extent) - dim - 1))

    level = one(*pieces[0])
    for cut in pieces[1:]:
        level = level * one(*cut)
    return level


def scatter_about(rng, dims, deviation, reach, cuts=(), kind=jnp.bfloat16):
    drawn = jax.random.normal(rng, dims, jnp.float32) * deviation
    if len(cuts) > 0:
        drawn = levels(rng, dims, cuts, -0.22, 0.18) * drawn
    return jnp.clip(drawn, min=-reach, max=reach).astype(kind)


def setup_inputs(seed: int = 0) -> dict:
    key_of = jax.random.split(jax.random.key(seed), 10)
    return {
        "hidden_in": scatter_about(key_of[0], (ROWS, D), 1.0, 6.0, ((0, 32), (1, 4))),
        "token_ids": draw_token_ids(jax.random.fold_in(key_of[9], 71), 0),
        "passage_counts": draw_passage_counts(jax.random.fold_in(key_of[9], 71), 0),
        "positive_doc": touch_ends(jax.random.randint(key_of[3], (QUERIES,), 0, DOCS), jax.random.fold_in(key_of[3], 1), 0, DOCS - 1).astype(jnp.int32),
        "queries": scatter_about(key_of[4], (QUERIES, D), 1.0, 6.0, ((0, 32), (1, 4))),
        "norm_gain": jnp.clip(1.0 + 0.1 * jax.random.normal(key_of[5], (D,), jnp.float32), 0.5, 1.5),
        "w_gate": scatter_about(key_of[6], (D, FF), D ** -0.5, 0.125, ((1, 4),)),
        "w_up": scatter_about(key_of[7], (D, FF), D ** -0.5, 0.125, ((1, 4),)),
        "w_down": scatter_about(key_of[8], (FF, D), FF ** -0.5, 0.0625, ((0, 4),)),
    }


pad_token = 128001
score_scale = 20.0
loss_seed = 4096.0
norm_epsilon = 1e-05
unit_epsilon = 1e-06

def layer_forward(rows, norm_gain, w_gate, w_up, w_down):
    row_float = rows.astype(jnp.float32)
    rms_scale = lax.rsqrt(lax.optimization_barrier(jnp.mean(row_float * row_float, axis=1, keepdims=True)) + norm_epsilon)
    normed = (row_float * rms_scale * norm_gain[None, :]).astype(jnp.bfloat16)
    gate = jnp.dot(normed, w_gate, preferred_element_type=jnp.float32)
    up = jnp.dot(normed, w_up, preferred_element_type=jnp.float32)
    sigmoid_gate = jax.nn.sigmoid(gate)
    hidden = (gate * sigmoid_gate * up).astype(jnp.bfloat16)
    branch = jnp.dot(hidden, w_down, preferred_element_type=jnp.float32)
    return (row_float, rms_scale, gate, up, sigmoid_gate, branch)

def reference(hidden_in, token_ids, passage_counts, positive_doc, queries, norm_gain, w_gate, w_up, w_down):
    block_len = L // 4
    block_total = DOCS * PMAX * 4
    block_index = jnp.arange(block_total, dtype=jnp.int32)
    live_block = block_index // 4 % PMAX < jnp.repeat(passage_counts, PMAX * 4)
    token_live = (token_ids.reshape(block_total, block_len) != pad_token) & live_block[:, None]
    chosen = jnp.nonzero(live_block, size=N_DP * CAP)[0].astype(jnp.int32)
    task_rows = hidden_in.reshape(block_total, block_len, D)[chosen].reshape(N_DP, CAP * block_len, D)
    task_row_mask = token_live[chosen].astype(jnp.float32).reshape(N_DP, CAP, block_len)

    def pool_group(pair):
        rows, mask = pair
        row_float, rms_scale, gate, up, sigmoid_gate, branch = layer_forward(rows, norm_gain, w_gate, w_up, w_down)
        output = (row_float + branch).reshape(CAP, block_len, D)
        return lax.optimization_barrier(jnp.sum(output * mask[:, :, None], axis=1))
    pooled = lax.map(pool_group, (task_rows, task_row_mask)).reshape(N_DP * CAP, D)
    block_sums = jnp.zeros((block_total, D), jnp.float32).at[chosen].set(pooled)
    passage_sum = block_sums.reshape(PASSAGES, 4, D).sum(axis=1)
    token_total = lax.optimization_barrier(jnp.sum(token_live.reshape(PASSAGES, L).astype(jnp.float32), axis=1))
    divisor = jnp.maximum(token_total, 1.0)
    passage_vec = (passage_sum / divisor[:, None]).astype(jnp.bfloat16)
    passage_live = live_block.reshape(PASSAGES, 4)[:, 0].astype(jnp.float32)
    vec_float = passage_vec.astype(jnp.float32)
    query_float = queries.astype(jnp.float32)
    raw_score = lax.dot_general(queries, passage_vec, (((1,), (1,)), ((), ())), preferred_element_type=jnp.float32)
    query_scale = lax.rsqrt(lax.optimization_barrier(jnp.sum(query_float * query_float, axis=1)) + unit_epsilon)
    passage_scale = lax.rsqrt(lax.optimization_barrier(jnp.sum(vec_float * vec_float, axis=1)) + unit_epsilon)
    scores = score_scale * raw_score * query_scale[:, None] * passage_scale[None, :]
    weights = passage_live[None, :] * jnp.exp(scores)
    doc_mass = weights.reshape(QUERIES, DOCS, PMAX).sum(axis=2)
    total_mass = doc_mass.sum(axis=1)
    positive_hit = (positive_doc[:, None] == jnp.arange(DOCS, dtype=jnp.int32)[None, :]).astype(jnp.float32)
    positive_mass = lax.optimization_barrier(jnp.sum(doc_mass * positive_hit, axis=1))
    query_loss = jnp.log(total_mass) - jnp.log(positive_mass)
    positive_pass = jnp.repeat(positive_hit, PMAX, axis=1)
    coefficient = loss_seed * score_scale * query_scale[:, None] * (weights / total_mass[:, None] - positive_pass * weights / positive_mass[:, None])
    weighted_queries = lax.dot_general(coefficient.astype(jnp.bfloat16), queries, (((0,), (0,)), ((), ())), preferred_element_type=jnp.float32)
    norm_term = lax.optimization_barrier(jnp.sum(coefficient * raw_score, axis=0))
    vec_change = passage_scale[:, None] * weighted_queries - vec_float * (passage_scale ** 3 * norm_term)[:, None]
    token_grad = (vec_change / divisor[:, None]).astype(jnp.bfloat16)
    block_grad = jnp.repeat(token_grad, 4, axis=0)[chosen].reshape(N_DP, CAP, D)

    def grad_group(triple):
        rows, mask, grad = triple
        row_float, rms_scale, gate, up, sigmoid_gate, branch = layer_forward(rows, norm_gain, w_gate, w_up, w_down)
        out_float = (mask[:, :, None] * grad[:, None, :].astype(jnp.float32)).reshape(CAP * block_len, D)
        out_grad = out_float.astype(jnp.bfloat16)
        hidden_grad = lax.dot_general(out_grad, w_down, (((1,), (1,)), ((), ())), preferred_element_type=jnp.float32)
        gate_grad = (hidden_grad * up * sigmoid_gate * (1.0 + gate * (1.0 - sigmoid_gate))).astype(jnp.bfloat16)
        up_grad = (hidden_grad * gate * sigmoid_gate).astype(jnp.bfloat16)
        normed_grad = lax.dot_general(gate_grad, w_gate, (((1,), (1,)), ((), ())), preferred_element_type=jnp.float32)
        normed_grad = normed_grad + lax.dot_general(up_grad, w_up, (((1,), (1,)), ((), ())), preferred_element_type=jnp.float32)
        inner = lax.optimization_barrier(jnp.mean(row_float * norm_gain[None, :] * normed_grad, axis=1))
        input_grad = out_float + rms_scale * norm_gain[None, :] * normed_grad - row_float * rms_scale ** 3 * inner[:, None]
        return input_grad.astype(jnp.bfloat16).reshape(CAP, block_len * D)
    task_grads = lax.map(grad_group, (task_rows, task_row_mask, block_grad)).reshape(N_DP * CAP, block_len * D)
    grad_rows = jnp.zeros((block_total, block_len * D), jnp.bfloat16).at[chosen].set(task_grads)
    return (query_loss, grad_rows.reshape(ROWS, D))
```

```python
import functools

import jax
import jax.numpy as jnp
from jax import lax
from jax.experimental import pallas as pl
from jax.experimental.pallas import tpu as pltpu
from jax.sharding import Mesh, PartitionSpec as P

L = 128
pad_token = 128001
score_scale = 20.0
loss_seed = 4096.0
norm_epsilon = 1e-05
unit_epsilon = 1e-06
MP = 4
FT = 256
CHUNKS = (640, 384)
bf16 = jnp.bfloat16
f32 = jnp.float32


def shifted(x, by):
    return lax.ppermute(x, "mp", [(i, (i + by) % MP) for i in range(MP)])


def swapped(x):
    return lax.ppermute(x, "core", [(0, 1), (1, 0)])


def copies_to_all(x, axes, count):
    return lax.all_to_all(
        jnp.broadcast_to(x, (count, *x.shape)), axes, split_axis=0, concat_axis=0, tiled=True
    )


def encode_kernel(
    m_ref, own_ref, left_ref, right_ref, opp_ref, mask_ref, gain_ref, wg_ref, wu_ref,
    a_ref, b_ref, c_ref, pool_ref, rms_ref, xpool_ref, xs,
):
    passes = pool_ref.shape[0]
    m = m_ref[0]

    @pl.when(pl.program_id(0) == 0)
    def _():
        pieces = [own_ref, right_ref, opp_ref, left_ref]
        total = None
        for piece in pieces:
            v = piece[...].astype(f32)
            part = jnp.sum(v * v, axis=1, keepdims=True)
            total = part if total is None else total + part
        width = MP * own_ref.shape[1]
        rms = lax.rsqrt(total / width + norm_epsilon)
        rms_ref[...] = rms
        mask = mask_ref[...]
        for k, piece in enumerate(pieces):
            j = lax.rem(m + k, MP)
            v = piece[...].astype(f32)
            xs[j] = (v * rms * gain_ref[j]).astype(bf16)
            live = v * mask
            for p in range(passes):
                xpool_ref[j, p : p + 1] = jnp.sum(live[p * L : (p + 1) * L], axis=0, keepdims=True)

    part = own_ref.shape[1]
    gate = None
    up = None
    for j in range(MP):
        rows = slice(j * part, (j + 1) * part)
        g = jnp.dot(xs[j], wg_ref[rows], preferred_element_type=f32)
        u = jnp.dot(xs[j], wu_ref[rows], preferred_element_type=f32)
        gate = g if gate is None else gate + g
        up = u if up is None else up + u
    sig = jax.nn.sigmoid(gate)
    b = gate * sig
    act = (b * up).astype(bf16).astype(f32) * mask_ref[...]
    for p in range(passes):
        pool_ref[p : p + 1] = jnp.sum(act[p * L : (p + 1) * L], axis=0, keepdims=True)
    a = up * sig * (1.0 + gate * (1.0 - sig))
    a_ref[...] = a.astype(bf16)
    b_ref[...] = b.astype(bf16)
    c_ref[...] = (a * gate + b * up).astype(bf16)


def encode(m, own, left, right, opp, mask, gain, w_gate, w_up):
    rows, part = own.shape
    width, ff = w_gate.shape
    passes = rows // L
    whole = lambda n, m_: (0, 0)
    piece = pl.BlockSpec((rows, part), whole)
    column = pl.BlockSpec((rows, 1), whole)
    weight = pl.BlockSpec((width, FT), lambda n, m_: (0, n))
    tile = pl.BlockSpec((rows, FT), lambda n, m_: (0, n))
    return pl.pallas_call(
        encode_kernel,
        grid_spec=pltpu.PrefetchScalarGridSpec(
            num_scalar_prefetch=1,
            grid=(ff // FT,),
            in_specs=[piece] * 4
            + [column, pl.BlockSpec((MP, 1, part), lambda n, m_: (0, 0, 0)), weight, weight],
            out_specs=[tile, tile, tile]
            + [
                pl.BlockSpec((passes, FT), lambda n, m_: (0, n)),
                column,
                pl.BlockSpec((MP, passes, part), lambda n, m_: (0, 0, 0)),
            ],
            scratch_shapes=[pltpu.VMEM((MP, rows, part), bf16)],
        ),
        out_shape=[jax.ShapeDtypeStruct((rows, ff), bf16)] * 3
        + [
            jax.ShapeDtypeStruct((passes, ff), f32),
            jax.ShapeDtypeStruct((rows, 1), f32),
            jax.ShapeDtypeStruct((MP, passes, part), f32),
        ],
        compiler_params=pltpu.CompilerParams(vmem_limit_bytes=48 << 20),
        cost_estimate=pl.CostEstimate(
            flops=4 * rows * width * ff,
            transcendentals=rows * ff,
            bytes_accessed=4 * width * ff + 2 * rows * width + 6 * rows * ff,
        ),
        name="encode",
    )(m, own, left, right, opp, mask, gain, w_gate, w_up)


def back_kernel(with_sum, m_ref, a_ref, b_ref, *refs):
    if with_sum:
        c_ref, g_ref, mask_ref, wg_ref, wu_ref, out_ref, s_ref = refs
    else:
        g_ref, mask_ref, wg_ref, wu_ref, out_ref = refs
    rows = a_ref.shape[0]
    base = pl.program_id(1) * (rows // L)
    dg = []
    du = []
    for p in range(rows // L):
        part = slice(p * L, (p + 1) * L)
        dact = g_ref[pl.ds(base + p, 1)] * mask_ref[part]
        dg.append((dact * a_ref[part].astype(f32)).astype(bf16))
        du.append((dact * b_ref[part].astype(f32)).astype(bf16))
        if with_sum:
            s_ref[part] = jnp.sum(dact * c_ref[part].astype(f32), axis=1, keepdims=True)
    contract = (((1,), (1,)), ((), ()))
    out = lax.dot_general(jnp.concatenate(dg, 0), wg_ref[...], contract, preferred_element_type=f32)
    out += lax.dot_general(jnp.concatenate(du, 0), wu_ref[...], contract, preferred_element_type=f32)
    out_ref[0] = out.astype(bf16)


def back(m, steps, a, b, c, g, mask, w_gate, w_up):
    rows, ff = a.shape
    width = w_gate.shape[0]
    part = width // MP
    rt = 256
    first, stride = steps[0], (steps[1] - steps[0]) if len(steps) > 1 else 0
    with_sum = c is not None
    tile = pl.BlockSpec((rt, ff), lambda k, r, m_: (r, 0))
    column = pl.BlockSpec((rt, 1), lambda k, r, m_: (r, 0))
    weight = pl.BlockSpec((part, ff), lambda k, r, m_: (lax.rem(m_[0] + first + stride * k, MP), 0))
    out_specs = [pl.BlockSpec((1, rt, part), lambda k, r, m_: (k, r, 0))]
    out_shape = [jax.ShapeDtypeStruct((len(steps), rows, part), bf16)]
    if with_sum:
        out_specs.append(column)
        out_shape.append(jax.ShapeDtypeStruct((rows, 1), f32))
    return pl.pallas_call(
        functools.partial(back_kernel, with_sum),
        grid_spec=pltpu.PrefetchScalarGridSpec(
            num_scalar_prefetch=1,
            grid=(len(steps), rows // rt),
            in_specs=[tile, tile]
            + ([tile] if with_sum else [])
            + [pl.BlockSpec((g.shape[0], ff), lambda k, r, m_: (0, 0)), column, weight, weight],
            out_specs=out_specs,
        ),
        out_shape=out_shape,
        compiler_params=pltpu.CompilerParams(vmem_limit_bytes=48 << 20),
        cost_estimate=pl.CostEstimate(
            flops=4 * rows * part * len(steps) * ff,
            transcendentals=0,
            bytes_accessed=(4 * part * ff + 4 * rows * ff + 2 * rows * part) * len(steps),
        ),
        name="back",
    )(m, a, b, *([c] if with_sum else []), g, mask, w_gate, w_up)


def per_device(
    hidden_in, token_ids, passage_counts, positive_doc, queries, norm_gain, w_gate, w_up, w_down
):
    row_count, part = hidden_in.shape
    width = norm_gain.shape[0]
    docs = passage_counts.shape[0]
    passes = row_count // L
    most = passes // docs
    query_rows = queries.shape[0]
    share = query_rows // MP
    chips = lax.axis_size(("x", "z"))
    mi = lax.axis_index("mp")
    core = lax.axis_index("core")
    chip = lax.axis_index(("x", "z"))
    m = mi.astype(jnp.int32).reshape(1)

    chunks = []
    at = 0
    for rows in CHUNKS:
        own = hidden_in[at : at + rows]
        chunks.append((at, rows, own, shifted(own, 1), shifted(own, -1)))
        at += rows

    mine = lax.all_to_all(
        queries.reshape(MP, share, part), "mp", split_axis=0, concat_axis=0, tiled=True
    )
    mine = jnp.moveaxis(mine, 0, 1).reshape(share, width)
    own_positive = lax.dynamic_slice_in_dim(positive_doc, mi * share, share)
    extra = jnp.pad(own_positive.astype(bf16)[:, None], ((0, 0), (0, L - 1)))
    all_q = copies_to_all(jnp.concatenate([mine, extra], axis=1), ("x", "z"), chips)
    all_q = all_q.reshape(chips * share, width + L)
    q = all_q[:, :width]
    positive = all_q[:, width].astype(f32)
    q_float = q.astype(f32)
    query_scale = lax.rsqrt(jnp.sum(q_float * q_float, axis=1) + unit_epsilon)

    live_pass = jnp.arange(passes, dtype=jnp.int32) % most < jnp.repeat(passage_counts, most)
    token_live = (token_ids.reshape(passes, L) != pad_token) & live_pass[:, None]
    live_float = token_live.astype(f32)
    mask = live_float.reshape(row_count, 1)
    divisor = jnp.maximum(jnp.sum(live_float, axis=1), 1.0)[:, None]
    gain = norm_gain.reshape(MP, 1, part)

    done = []
    for at, rows, own, left, right in chunks:
        half = rows // 2
        opp = jnp.concatenate([shifted(left[:half], 1), shifted(right[half:], -1)], axis=0)
        done.append(
            encode(m, own, left, right, opp, mask[at : at + rows], gain, w_gate, w_up)
        )
    a, b, c, pool, rms = (jnp.concatenate([d[k] for d in done], axis=0) for k in range(5))
    xpool = jnp.concatenate([d[5] for d in done], axis=1)
    xpool = jnp.moveaxis(xpool, 0, 1).reshape(passes, width)

    high = pool.astype(bf16)
    low = (pool - high.astype(f32)).astype(bf16)
    branch = jnp.dot(jnp.concatenate([high, low], 0), w_down, preferred_element_type=f32)
    branch = (branch[:passes] + branch[passes:]).astype(bf16)
    branch = copies_to_all(branch, "mp", MP).astype(f32).sum(axis=0)
    vec = ((xpool + branch) / divisor).astype(bf16)

    flag = jnp.broadcast_to(live_pass.astype(bf16)[:, None], (passes, L))
    packed = jnp.concatenate([vec, flag], axis=1)
    packed = jnp.concatenate([packed, swapped(packed)], axis=0)
    vecs = packed[:, :width]
    live = packed[:, width].astype(f32)[:, None]
    vec_float = vecs.astype(f32)
    vec_scale = lax.rsqrt(jnp.sum(vec_float * vec_float, axis=1, keepdims=True) + unit_epsilon)

    raw = lax.dot_general(vecs, q, (((1,), (1,)), ((), ())), preferred_element_type=f32)
    weights = live * jnp.exp(score_scale * raw * query_scale[None, :] * vec_scale)
    first_doc = (chip * 2 + core) * docs
    other_doc = (chip * 2 + 1 - core) * docs
    k = jnp.arange(2 * passes, dtype=jnp.int32)
    doc = jnp.where(k < passes, first_doc + k // most, other_doc + (k - passes) // most)
    hit = (positive[None, :] == doc.astype(f32)[:, None]).astype(f32)
    mass = jnp.stack([jnp.sum(weights, axis=0), jnp.sum(weights * hit, axis=0)])
    mass = copies_to_all(mass.reshape(8, -1), ("x", "z"), chips).sum(axis=0).reshape(2, -1)
    total, held = mass[0], mass[1]
    loss = jnp.log(total) - jnp.log(held)
    own_loss = lax.dynamic_slice_in_dim(loss, chip * share, share)

    coef = (loss_seed * score_scale) * query_scale[None, :] * (
        weights / total[None, :] - hit * weights / held[None, :]
    )
    grad = jnp.dot(coef.astype(bf16), q, preferred_element_type=f32)
    term = jnp.sum(coef * raw, axis=1, keepdims=True)
    grad = jnp.concatenate([grad, jnp.broadcast_to(term, (2 * passes, L))], axis=1)
    grad = grad[:passes] + swapped(grad[passes:])
    grad = copies_to_all(grad.astype(bf16), "mp", MP).astype(f32).sum(axis=0)
    scale = vec_scale[:passes]
    change = scale * grad[:, :width] - vec_float[:passes] * (scale**3 * grad[:, width : width + 1])
    token_grad = (change / divisor).astype(bf16)
    dact = lax.dot_general(token_grad, w_down, (((1,), (1,)), ((), ())), preferred_element_type=f32)

    half = row_count // 2
    opp, s = back(m, (2,), a, b, c, dact, mask, w_gate, w_up)
    opp = opp[0]
    from_right = shifted(opp[:half], -1)
    from_left = shifted(opp[half:], 1)
    sides = back(m, (1, 3), a, b, None, dact, mask, w_gate, w_up)[0]
    right, left = sides[0], sides[1]
    left_low = shifted(left[half:], -1)
    right_high = shifted(right[:half], 1)
    left_high = shifted((left[:half].astype(f32) + from_right.astype(f32)).astype(bf16), -1)
    right_low = shifted((right[half:].astype(f32) + from_left.astype(f32)).astype(bf16), 1)
    own = back(m, (0,), a, b, None, dact, mask, w_gate, w_up)[0][0]
    small = jnp.concatenate(
        [s.reshape(passes, L), jnp.pad(own_loss[None, :], ((0, 7), (0, L - share)))], axis=0
    )
    small = copies_to_all(small, "mp", MP)
    inner = small[:, :passes].sum(axis=0).reshape(row_count, 1) / width
    query_loss = small[:, passes, :share].reshape(MP * share)
    normed_grad = own.astype(f32) + jnp.concatenate(
        [
            left_high.astype(f32) + right_high.astype(f32),
            left_low.astype(f32) + right_low.astype(f32),
        ],
        axis=0,
    )
    own_gain = lax.dynamic_slice_in_dim(norm_gain, mi * part, part)
    own_token = lax.dynamic_slice_in_dim(token_grad, mi * part, part, axis=1).astype(f32)
    own_out = (live_float[:, :, None] * own_token[:, None, :]).reshape(row_count, part)
    hidden_grad = (
        own_out
        + rms * own_gain[None, :] * normed_grad
        - hidden_in.astype(f32) * (rms * rms * inner)
    )
    return query_loss, hidden_grad.astype(bf16)


def solution(mesh):
    shape = (4, 4, 2, MP)
    split = Mesh(mesh.devices.reshape(shape), ("x", "z", "core", "mp"))
    dp = ("x", "z", "core")
    return jax.shard_map(
        per_device,
        mesh=split,
        in_specs=(
            P(dp, "mp"),
            P(dp),
            P(dp),
            P(dp),
            P(dp, "mp"),
            P(),
            P(None, "mp"),
            P(None, "mp"),
            P("mp", None),
        ),
        out_specs=(P(dp), P(dp, "mp")),
        check_vma=False,
    )
```

```python
import functools

import jax
import jax.numpy as jnp
from jax import lax
from jax.experimental import pallas as pl
from jax.experimental.pallas import tpu as pltpu
from jax.sharding import Mesh, PartitionSpec as P

L = 128
pad_token = 128001
score_scale = 20.0
loss_seed = 4096.0
norm_epsilon = 1e-05
unit_epsilon = 1e-06
MP = 4
FT = 256
CHUNKS = (512, 512)
bf16 = jnp.bfloat16
f32 = jnp.float32


def shifted(x, by):
    return lax.ppermute(x, "mp", [(i, (i + by) % MP) for i in range(MP)])


def swapped(x):
    return lax.ppermute(x, "core", [(0, 1), (1, 0)])


def copies_to_all(x, axes, count):
    return lax.all_to_all(
        jnp.broadcast_to(x, (count, *x.shape)), axes, split_axis=0, concat_axis=0, tiled=True
    )


def in_hbm(x):
    return pltpu.with_memory_space_constraint(x, pltpu.HBM)


def encode_kernel(
    chunk, count, m_ref, own_ref, right_ref, left_ref, high_ref, low_ref, mask_ref, gain_ref, wg_ref, wu_ref, *refs
):
    a_out, b_out, c_out, pool_ref, rms_ref, xpool_ref = refs[count : count + 6]
    xin, xs, w, a_buf, b_buf, c_buf, in_sem, w_sem, out_sem = refs[count + 6 :]
    rows, part = own_ref.shape
    half = rows // 2
    tiles = w.shape[0]
    m = m_ref[0]
    sources = [
        (own_ref, xin.at[0]),
        (right_ref, xin.at[1]),
        (left_ref, xin.at[3]),
        (high_ref, xin.at[2, pl.ds(0, half)]),
        (low_ref, xin.at[2, pl.ds(half, half)]),
    ]
    arriving = [pltpu.make_async_copy(a, b, in_sem.at[k]) for k, (a, b) in enumerate(sources)]
    for copy in arriving:
        copy.start()
    weights = []
    for n in range(tiles):
        columns = pl.ds(n * FT, FT)
        for k in range(MP):
            at = pl.multiple_of(lax.rem(m + k, MP) * part, part)
            for i, ref in enumerate((wg_ref, wu_ref)):
                weights.append(
                    pltpu.make_async_copy(
                        ref.at[pl.ds(at, part), columns],
                        w.at[n, pl.ds(k * part, part), pl.ds(i * FT, FT)],
                        w_sem.at[n, 2 * k + i],
                    )
                )
    for copy in weights:
        copy.start()
    for copy in arriving:
        copy.wait()

    total = None
    for k in range(MP):
        v = xin[k].astype(f32)
        square = jnp.sum(v * v, axis=1, keepdims=True)
        total = square if total is None else total + square
    rms = lax.rsqrt(total / (MP * part) + norm_epsilon)
    rms_ref[...] = rms
    mask = mask_ref[...]
    for k in range(MP):
        j = lax.rem(m + k, MP)
        v = xin[k].astype(f32)
        xs[:, k * part : (k + 1) * part] = (v * rms * gain_ref[j]).astype(bf16)
        live = v * mask
        for p in range(rows // L):
            xpool_ref[j, p : p + 1] = jnp.sum(live[p * L : (p + 1) * L], axis=0, keepdims=True)

    def product(n):
        for copy in weights[n * 2 * MP : (n + 1) * 2 * MP]:
            copy.wait()
        return jnp.dot(xs[...], w[n], preferred_element_type=f32)

    leaving = []
    both = product(0)
    for n in range(tiles):
        gate, up = both[:, :FT], both[:, FT:]
        if n + 1 < tiles:
            both = product(n + 1)
        columns = slice(n * FT, (n + 1) * FT)
        sig = jax.nn.sigmoid(gate)
        b = gate * sig
        bu = b * up
        act = bu.astype(bf16).astype(f32) * mask
        for p in range(rows // L):
            pool_ref[p : p + 1, columns] = jnp.sum(act[p * L : (p + 1) * L], axis=0, keepdims=True)
        a = up * (sig + b * (1.0 - sig))
        a_buf[:, columns] = a.astype(bf16)
        b_buf[:, columns] = b.astype(bf16)
        c_buf[:, columns] = (a * gate + bu).astype(bf16)
        for i, (buf, out) in enumerate(((a_buf, a_out), (b_buf, b_out), (c_buf, c_out))):
            copy = pltpu.make_async_copy(
                buf.at[:, pl.ds(n * FT, FT)],
                out.at[pl.ds(chunk * rows, rows), pl.ds(n * FT, FT)],
                out_sem.at[n, i],
            )
            copy.start()
            leaving.append(copy)
    for copy in leaving:
        copy.wait()


def encode(m, chunk, total, before, own, right, left, high, low, mask, gain, w_gate, w_up):
    rows, part = own.shape
    width, ff = w_gate.shape
    passes = rows // L
    tiles = ff // FT
    anywhere = pl.BlockSpec(memory_space=pl.ANY)
    vmem = pl.BlockSpec(memory_space=pltpu.VMEM)
    return pl.pallas_call(
        functools.partial(encode_kernel, chunk, len(before)),
        in_specs=[pl.BlockSpec(memory_space=pltpu.SMEM)]
        + [anywhere] * 5
        + [vmem, vmem, anywhere, anywhere]
        + [anywhere] * len(before),
        out_specs=[anywhere] * 3 + [vmem] * 3,
        out_shape=[pltpu.HBM((total, ff), bf16)] * 3
        + [
            jax.ShapeDtypeStruct((passes, ff), f32),
            jax.ShapeDtypeStruct((rows, 1), f32),
            jax.ShapeDtypeStruct((MP, passes, part), f32),
        ],
        scratch_shapes=[
            pltpu.VMEM((MP, rows, part), bf16),
            pltpu.VMEM((rows, width), bf16),
            pltpu.VMEM((tiles, width, 2 * FT), bf16),
        ]
        + [pltpu.VMEM((rows, ff), bf16)] * 3
        + [
            pltpu.SemaphoreType.DMA((5,)),
            pltpu.SemaphoreType.DMA((tiles, 2 * MP)),
            pltpu.SemaphoreType.DMA((tiles, 3)),
        ],
        compiler_params=pltpu.CompilerParams(vmem_limit_bytes=44 << 20),
        cost_estimate=pl.CostEstimate(
            flops=4 * rows * width * ff,
            transcendentals=rows * ff,
            bytes_accessed=4 * width * ff + 2 * rows * width + 6 * rows * ff,
        ),
        input_output_aliases={10 + k: k for k in range(len(before))},
        name="encode",
    )(
        m, *map(in_hbm, (own, right, left, high, low)), mask, gain,
        in_hbm(w_gate), in_hbm(w_up), *map(in_hbm, before),
    )


def contract_rows(left, right):
    return lax.dot_general(
        left, right, (((1,), (1,)), ((), ())), preferred_element_type=f32
    )


def load_weights(m, steps, wg_ref, wu_ref, w, sem):
    part, ff = w.shape[1], wg_ref.shape[1]
    copies = []
    for k, step in enumerate(steps):
        at = pl.multiple_of(lax.rem(m + step, MP) * part, part)
        for i, ref in enumerate((wg_ref, wu_ref)):
            copies.append(
                pltpu.make_async_copy(
                    ref.at[pl.ds(at, part)], w.at[k, :, pl.ds(i * ff, ff)], sem.at[k, i]
                )
            )
    return copies


def back_far_kernel(m_ref, a_ref, b_ref, c_ref, g_ref, mask_ref, wg_ref, wu_ref, *refs):
    high_ref, low_ref, s_ref, d_out = refs[:4]
    abc, d, w, in_sem, w_sem, out_sem = refs[4:]
    ff = a_ref.shape[1]
    tiles, _, rt, _ = abc.shape
    weights = load_weights(m_ref[0], (2,), wg_ref, wu_ref, w, w_sem)
    arriving = [
        [
            pltpu.make_async_copy(ref.at[pl.ds(r * rt, rt)], abc.at[r, i], in_sem.at[r, i])
            for i, ref in enumerate((a_ref, b_ref, c_ref))
        ]
        for r in range(tiles)
    ]
    for copy in arriving[0] + weights + sum(arriving[1:], []):
        copy.start()

    def scaled(r):
        for copy in arriving[r]:
            copy.wait()
        for p in range(rt // L):
            part = slice(p * L, (p + 1) * L)
            at = r * rt + p * L
            dact = g_ref[at // L : at // L + 1] * mask_ref[at : at + L]
            d[r, part, :ff] = (dact * abc[r, 0, part].astype(f32)).astype(bf16)
            d[r, part, ff:] = (dact * abc[r, 1, part].astype(f32)).astype(bf16)
            s_ref[at : at + L] = jnp.sum(dact * abc[r, 2, part].astype(f32), axis=1, keepdims=True)
        copy = pltpu.make_async_copy(d.at[r], d_out.at[pl.ds(r * rt, rt)], out_sem.at[r])
        copy.start()
        return copy

    leaving = [scaled(0)]
    for copy in weights:
        copy.wait()
    for r in range(tiles):
        out = contract_rows(d[r], w[0]).astype(bf16)
        if r + 1 < tiles:
            leaving.append(scaled(r + 1))
        half = tiles // 2
        target, at = (high_ref, r) if r < half else (low_ref, r - half)
        target[at * rt : (at + 1) * rt] = out
    for copy in leaving:
        copy.wait()


def back_far(m, a, b, c, g, mask, w_gate, w_up):
    rows, ff = a.shape
    part = w_gate.shape[0] // MP
    rt = 256
    tiles = rows // rt
    anywhere = pl.BlockSpec(memory_space=pl.ANY)
    vmem = pl.BlockSpec(memory_space=pltpu.VMEM)
    return pl.pallas_call(
        back_far_kernel,
        in_specs=[pl.BlockSpec(memory_space=pltpu.SMEM)]
        + [anywhere] * 3
        + [vmem, vmem, anywhere, anywhere],
        out_specs=[vmem, vmem, vmem, anywhere],
        out_shape=[
            jax.ShapeDtypeStruct((rows // 2, part), bf16),
            jax.ShapeDtypeStruct((rows // 2, part), bf16),
            jax.ShapeDtypeStruct((rows, 1), f32),
            pltpu.HBM((rows, 2 * ff), bf16),
        ],
        scratch_shapes=[
            pltpu.VMEM((tiles, 3, rt, ff), bf16),
            pltpu.VMEM((tiles, rt, 2 * ff), bf16),
            pltpu.VMEM((1, part, 2 * ff), bf16),
            pltpu.SemaphoreType.DMA((tiles, 3)),
            pltpu.SemaphoreType.DMA((1, 2)),
            pltpu.SemaphoreType.DMA((tiles,)),
        ],
        compiler_params=pltpu.CompilerParams(vmem_limit_bytes=44 << 20),
        cost_estimate=pl.CostEstimate(flops=1, transcendentals=0, bytes_accessed=1),
        name="back_far",
    )(m, *map(in_hbm, (a, b, c)), g, mask, in_hbm(w_gate), in_hbm(w_up))


def back_near_kernel(m_ref, d_ref, wg_ref, wu_ref, *refs):
    outs = refs[:6]
    d, w, in_sem, w_sem = refs[6:]
    tiles, rt, _ = d.shape
    weights = load_weights(m_ref[0], (1, 3, 0), wg_ref, wu_ref, w, w_sem)
    arriving = [
        pltpu.make_async_copy(d_ref.at[pl.ds(r * rt, rt)], d.at[r], in_sem.at[r])
        for r in range(tiles)
    ]
    for copy in weights[:2] + arriving + weights[2:]:
        copy.start()
    for k in range(3):
        for copy in weights[2 * k : 2 * k + 2]:
            copy.wait()
        for r in range(tiles):
            if k == 0:
                arriving[r].wait()
            outs[2 * k + r][...] = contract_rows(d[r], w[k]).astype(bf16)


def back_near(m, d, w_gate, w_up):
    rows, ff2 = d.shape
    part = w_gate.shape[0] // MP
    tiles = 2
    rt = rows // tiles
    anywhere = pl.BlockSpec(memory_space=pl.ANY)
    return pl.pallas_call(
        back_near_kernel,
        in_specs=[pl.BlockSpec(memory_space=pltpu.SMEM)] + [anywhere] * 3,
        out_specs=[pl.BlockSpec(memory_space=pltpu.VMEM)] * 6,
        out_shape=[jax.ShapeDtypeStruct((rt, part), bf16)] * 6,
        scratch_shapes=[
            pltpu.VMEM((tiles, rt, ff2), bf16),
            pltpu.VMEM((3, part, ff2), bf16),
            pltpu.SemaphoreType.DMA((tiles,)),
            pltpu.SemaphoreType.DMA((3, 2)),
        ],
        compiler_params=pltpu.CompilerParams(vmem_limit_bytes=44 << 20),
        cost_estimate=pl.CostEstimate(flops=1, transcendentals=0, bytes_accessed=1),
        name="back_near",
    )(m, in_hbm(d), in_hbm(w_gate), in_hbm(w_up))


def finish_kernel(
    count, x_ref, own_ref, one_ref, two_ref, rms_ref, inner_ref, mask_ref, token_ref, gain_ref, *refs
):
    out_ref = refs[count]
    rms = rms_ref[...]
    normed = own_ref[...].astype(f32) + one_ref[...].astype(f32) + two_ref[...].astype(f32)
    grad = rms * gain_ref[...] * normed - x_ref[...].astype(f32) * (rms * rms * inner_ref[...])
    mask = mask_ref[...]
    for p in range(out_ref.shape[0] // L):
        part = slice(p * L, (p + 1) * L)
        out_ref[part] = (grad[part] + mask[part] * token_ref[0, p : p + 1]).astype(bf16)


def finish(chunk, before, x, own, one, two, rms, inner, mask, token, gain):
    rows, part = own.shape
    rt = 256
    steps = rows // rt
    here = pl.BlockSpec((rt, part), lambda r: (r, 0))
    whole = pl.BlockSpec((rt, part), lambda r: (chunk * steps + r, 0))
    column = pl.BlockSpec((rt, 1), lambda r: (chunk * steps + r, 0))
    return pl.pallas_call(
        functools.partial(finish_kernel, len(before)),
        grid=(steps,),
        in_specs=[whole, here, here, here, column, column, column]
        + [
            pl.BlockSpec((1, rt // L, part), lambda r: (chunk * steps + r, 0, 0)),
            pl.BlockSpec((1, part), lambda r: (0, 0)),
        ]
        + [pl.BlockSpec(memory_space=pl.ANY)] * len(before),
        out_specs=whole,
        out_shape=jax.ShapeDtypeStruct(x.shape, bf16),
        input_output_aliases={9 + k: k for k in range(len(before))},
        name="finish",
    )(x, own, one, two, rms, inner, mask, token.reshape(-1, rt // L, part), gain, *before)


def per_device(
    hidden_in, token_ids, passage_counts, positive_doc, queries, norm_gain, w_gate, w_up, w_down
):
    row_count, part = hidden_in.shape
    width = norm_gain.shape[0]
    docs = passage_counts.shape[0]
    passes = row_count // L
    most = passes // docs
    query_rows = queries.shape[0]
    share = query_rows // MP
    chips = lax.axis_size(("x", "z"))
    mi = lax.axis_index("mp")
    core = lax.axis_index("core")
    chip = lax.axis_index(("x", "z"))
    m = mi.astype(jnp.int32).reshape(1)

    mine = lax.all_to_all(
        queries.reshape(MP, share, part), "mp", split_axis=0, concat_axis=0, tiled=True
    )
    mine, hidden_in = lax.optimization_barrier((mine, hidden_in))

    chunks = []
    at = 0
    for rows in CHUNKS:
        own = hidden_in[at : at + rows]
        chunks.append((at, rows, own, shifted(own, 1), shifted(own, -1)))
        at += rows

    mine = jnp.moveaxis(mine, 0, 1).reshape(share, width)
    own_positive = lax.dynamic_slice_in_dim(positive_doc, mi * share, share)
    extra = jnp.pad(own_positive.astype(bf16)[:, None], ((0, 0), (0, L - 1)))
    all_q = lax.all_gather(jnp.concatenate([mine, extra], axis=1), ("x", "z"), axis=0)

    live_pass = jnp.arange(passes, dtype=jnp.int32) % most < jnp.repeat(passage_counts, most)
    token_live = (token_ids.reshape(passes, L) != pad_token) & live_pass[:, None]
    live_float = token_live.astype(f32)
    mask = live_float.reshape(row_count, 1)
    divisor = jnp.maximum(jnp.sum(live_float, axis=1), 1.0)[:, None]
    gain = norm_gain.reshape(MP, 1, part)

    done = []
    before = ()
    for k, (at, rows, own, left, right) in enumerate(chunks):
        half = rows // 2
        high, low = shifted(left[:half], 1), shifted(right[half:], -1)
        part_mask = mask[at : at + rows]
        done.append(
            encode(
                m, k, row_count, before, own, right, left, high, low, part_mask, gain, w_gate, w_up
            )
        )
        before = done[-1][:3]
    a, b, c = before
    all_q = all_q.reshape(chips * share, width + L)
    q = all_q[:, :width]
    positive = all_q[:, width].astype(f32)
    q_float = q.astype(f32)
    query_scale = lax.rsqrt(jnp.sum(q_float * q_float, axis=1) + unit_epsilon)
    pool, rms = (jnp.concatenate([d[k] for d in done], axis=0) for k in (3, 4))
    xpool = jnp.concatenate([d[5] for d in done], axis=1)
    xpool = jnp.moveaxis(xpool, 0, 1).reshape(passes, width)

    high = pool.astype(bf16)
    low = (pool - high.astype(f32)).astype(bf16)
    branch = jnp.dot(jnp.concatenate([high, low], 0), w_down, preferred_element_type=f32)
    branch = (branch[:passes] + branch[passes:]).astype(bf16)
    branch = copies_to_all(branch, "mp", MP).astype(f32).sum(axis=0)
    vec = ((xpool + branch) / divisor).astype(bf16)

    flag = jnp.broadcast_to(live_pass.astype(bf16)[:, None], (passes, L))
    packed = jnp.concatenate([vec, flag], axis=1)
    packed = jnp.concatenate([packed, swapped(packed)], axis=0)
    vecs = packed[:, :width]
    live = packed[:, width].astype(f32)[:, None]
    vec_float = vecs.astype(f32)
    vec_scale = lax.rsqrt(jnp.sum(vec_float * vec_float, axis=1, keepdims=True) + unit_epsilon)

    raw = lax.dot_general(vecs, q, (((1,), (1,)), ((), ())), preferred_element_type=f32)
    weights = live * jnp.exp(score_scale * raw * query_scale[None, :] * vec_scale)
    first_doc = (chip * 2 + core) * docs
    other_doc = (chip * 2 + 1 - core) * docs
    k = jnp.arange(2 * passes, dtype=jnp.int32)
    doc = jnp.where(k < passes, first_doc + k // most, other_doc + (k - passes) // most)
    hit = (positive[None, :] == doc.astype(f32)[:, None]).astype(f32)
    mass = jnp.stack([jnp.sum(weights, axis=0), jnp.sum(weights * hit, axis=0)])
    mass = copies_to_all(mass.reshape(8, -1), ("x", "z"), chips).sum(axis=0).reshape(2, -1)
    total, held = mass[0], mass[1]
    loss = jnp.log(total) - jnp.log(held)
    own_loss = lax.dynamic_slice_in_dim(loss, chip * share, share)

    coef = (loss_seed * score_scale) * query_scale[None, :] * (
        weights / total[None, :] - hit * weights / held[None, :]
    )
    grad = jnp.dot(coef.astype(bf16), q, preferred_element_type=f32)
    term = jnp.sum(coef * raw, axis=1, keepdims=True)
    grad = jnp.concatenate([grad, jnp.broadcast_to(term, (2 * passes, L))], axis=1)
    grad = grad[:passes] + swapped(grad[passes:])
    grad = copies_to_all(grad.astype(bf16), "mp", MP).astype(f32).sum(axis=0)
    scale = vec_scale[:passes]
    change = scale * grad[:, :width] - vec_float[:passes] * (scale**3 * grad[:, width : width + 1])
    token_grad = (change / divisor).astype(bf16)
    dact = lax.dot_general(token_grad, w_down, (((1,), (1,)), ((), ())), preferred_element_type=f32)

    high, low, s, d = back_far(m, a, b, c, dact, mask, w_gate, w_up)
    from_right = shifted(high, -1)
    from_left = shifted(low, 1)
    right_high, right_low, left_high, left_low, own_high, own_low = back_near(m, d, w_gate, w_up)
    left_low = shifted(left_low, -1)
    right_low = shifted((right_low.astype(f32) + from_left.astype(f32)).astype(bf16), 1)
    left_high = shifted((left_high.astype(f32) + from_right.astype(f32)).astype(bf16), -1)
    right_high = shifted(right_high, 1)
    small = jnp.concatenate(
        [s.reshape(passes, L), jnp.pad(own_loss[None, :], ((0, 7), (0, L - share)))], axis=0
    )
    left_low, small = lax.optimization_barrier((left_low, small))
    small = copies_to_all(small, "mp", MP)
    inner = small[:, :passes].sum(axis=0).reshape(row_count, 1) / width
    query_loss = small[:, passes, :share].reshape(MP * share)
    own_gain = lax.dynamic_slice_in_dim(norm_gain, mi * part, part)[None, :]
    own_token = lax.dynamic_slice_in_dim(token_grad, mi * part, part, axis=1).astype(f32)
    rest = (rms, inner, mask, own_token, own_gain)
    hidden_grad = finish(1, (), hidden_in, own_low, left_low, right_low, *rest)
    hidden_grad = finish(0, (hidden_grad,), hidden_in, own_high, left_high, right_high, *rest)
    return query_loss, hidden_grad


def solution(mesh):
    shape = (4, 4, 2, MP)
    split = Mesh(mesh.devices.reshape(shape), ("x", "z", "core", "mp"))
    dp = ("x", "z", "core")
    return jax.shard_map(
        per_device,
        mesh=split,
        in_specs=(
            P(dp, "mp"),
            P(dp),
            P(dp),
            P(dp),
            P(dp, "mp"),
            P(),
            P(None, "mp"),
            P(None, "mp"),
            P("mp", None),
        ),
        out_specs=(P(dp), P(dp, "mp")),
        check_vma=False,
    )
```

```python
import functools

import jax
import jax.numpy as jnp
from jax import lax
from jax.experimental import pallas as pl
from jax.experimental.pallas import tpu as pltpu
from jax.sharding import Mesh, PartitionSpec as P

L = 128
pad_token = 128001
score_scale = 20.0
loss_seed = 4096.0
norm_epsilon = 1e-05
unit_epsilon = 1e-06
MP = 4
FT = 256
ROW_STEP = 512
CHUNKS = (512, 512)
bf16 = jnp.bfloat16
f32 = jnp.float32


def shifted(x, by):
    return lax.ppermute(x, "mp", [(i, (i + by) % MP) for i in range(MP)])


def swapped(x):
    return lax.ppermute(x, "core", [(0, 1), (1, 0)])


def copies_to_all(x, axes, count):
    return lax.all_to_all(
        jnp.broadcast_to(x, (count, *x.shape)), axes, split_axis=0, concat_axis=0, tiled=True
    )


def in_hbm(x):
    return pltpu.with_memory_space_constraint(x, pltpu.HBM)


def encode_kernel(
    chunk, count, m_ref, own_ref, right_ref, left_ref, high_ref, low_ref, mask_ref, gain_ref, wg_ref, wu_ref, *refs
):
    a_out, b_out, c_out, pool_ref, rms_ref, xpool_ref = refs[count : count + 6]
    xin, xs, w, results, in_sem, w_sem, out_sem = refs[count + 6 :]
    rows, part = own_ref.shape
    half = rows // 2
    tiles = w.shape[0]
    m = m_ref[0]
    sources = [
        (own_ref, xin.at[0]),
        (right_ref, xin.at[1]),
        (left_ref, xin.at[3]),
        (high_ref, xin.at[2, pl.ds(0, half)]),
        (low_ref, xin.at[2, pl.ds(half, half)]),
    ]
    arriving = [pltpu.make_async_copy(a, b, in_sem.at[k]) for k, (a, b) in enumerate(sources)]
    for copy in arriving:
        copy.start()
    def weight_copies(n):
        columns = pl.ds(pl.multiple_of(n * FT, FT), FT)
        copies = []
        for k in range(MP):
            at = pl.multiple_of(lax.rem(m + k, MP) * part, part)
            for i, ref in enumerate((wg_ref, wu_ref)):
                copies.append(
                    pltpu.make_async_copy(
                        ref.at[pl.ds(at, part), columns],
                        w.at[n, pl.ds(k * part, part), pl.ds(i * FT, FT)],
                        w_sem.at[n, 2 * k + i],
                    )
                )
        return copies

    def result_copies(n):
        return [
            pltpu.make_async_copy(
                results.at[n, i],
                out.at[pl.ds(chunk * rows, rows), pl.ds(pl.multiple_of(n * FT, FT), FT)],
                out_sem.at[n, i],
            )
            for i, out in enumerate((a_out, b_out, c_out))
        ]

    def each(count, body):
        def step(n, carry):
            body(n)
            return carry

        lax.fori_loop(0, count, step, 0)

    def start_weights(n):
        for copy in weight_copies(n):
            copy.start()

    each(tiles, start_weights)
    for copy in arriving:
        copy.wait()

    def normalise(p):
        at = pl.ds(pl.multiple_of(p * L, L), L)
        mask = mask_ref[at]
        total = None
        for k in range(MP):
            v = xin[k, at].astype(f32)
            square = jnp.sum(v * v, axis=1, keepdims=True)
            total = square if total is None else total + square
        rms = lax.rsqrt(total / (MP * part) + norm_epsilon)
        rms_ref[at] = rms
        for k in range(MP):
            j = lax.rem(m + k, MP)
            v = xin[k, at].astype(f32)
            xs[at, k * part : (k + 1) * part] = (v * rms * gain_ref[j]).astype(bf16)
            xpool_ref[p, pl.ds(j, 1)] = jnp.sum(v * mask, axis=0, keepdims=True)

    each(rows // L, normalise)

    def multiply(n):
        for copy in weight_copies(n):
            copy.wait()
        for r in range(0, rows, ROW_STEP):
            at = slice(r, r + ROW_STEP)
            both = jnp.dot(xs[at], w[n], preferred_element_type=f32)
            gate, up = both[:, :FT], both[:, FT:]
            mask = mask_ref[at]
            sig = jax.nn.sigmoid(gate)
            up = up * mask
            b = gate * sig
            bu = b * up
            act = bu.astype(bf16).astype(f32)
            for p in range(ROW_STEP // L):
                q = r // L + p
                pool_ref[n, q : q + 1] = jnp.sum(act[p * L : (p + 1) * L], axis=0, keepdims=True)
            a = up * (sig + b * (1.0 - sig))
            results[n, 0, at] = a.astype(bf16)
            results[n, 1, at] = (b * mask).astype(bf16)
            results[n, 2, at] = (a * gate + bu).astype(bf16)
        for copy in result_copies(n):
            copy.start()

    each(tiles, multiply)

    def wait_results(n):
        for copy in result_copies(n):
            copy.wait()

    each(tiles, wait_results)


def encode(m, chunk, total, before, own, right, left, high, low, mask, gain, w_gate, w_up):
    rows, part = own.shape
    width, ff = w_gate.shape
    passes = rows // L
    tiles = ff // FT
    anywhere = pl.BlockSpec(memory_space=pl.ANY)
    vmem = pl.BlockSpec(memory_space=pltpu.VMEM)
    return pl.pallas_call(
        functools.partial(encode_kernel, chunk, len(before)),
        in_specs=[pl.BlockSpec(memory_space=pltpu.SMEM)]
        + [anywhere] * 5
        + [vmem, vmem, anywhere, anywhere]
        + [anywhere] * len(before),
        out_specs=[anywhere] * 3 + [vmem] * 3,
        out_shape=[pltpu.HBM((total, ff), bf16)] * 3
        + [
            jax.ShapeDtypeStruct((tiles, passes, FT), f32),
            jax.ShapeDtypeStruct((rows, 1), f32),
            jax.ShapeDtypeStruct((passes, MP, part), f32),
        ],
        scratch_shapes=[
            pltpu.VMEM((MP, rows, part), bf16),
            pltpu.VMEM((rows, width), bf16),
            pltpu.VMEM((tiles, width, 2 * FT), bf16),
            pltpu.VMEM((tiles, 3, rows, FT), bf16),
            pltpu.SemaphoreType.DMA((5,)),
            pltpu.SemaphoreType.DMA((tiles, 2 * MP)),
            pltpu.SemaphoreType.DMA((tiles, 3)),
        ],
        compiler_params=pltpu.CompilerParams(vmem_limit_bytes=44 << 20),
        cost_estimate=pl.CostEstimate(
            flops=4 * rows * width * ff,
            transcendentals=rows * ff,
            bytes_accessed=4 * width * ff + 2 * rows * width + 6 * rows * ff,
        ),
        input_output_aliases={10 + k: k for k in range(len(before))},
        name="encode",
    )(
        m, *map(in_hbm, (own, right, left, high, low)), mask, gain,
        in_hbm(w_gate), in_hbm(w_up), *map(in_hbm, before),
    )


def contract_rows(left, right):
    return lax.dot_general(
        left, right, (((1,), (1,)), ((), ())), preferred_element_type=f32
    )


def load_weights(m, steps, wg_ref, wu_ref, w, sem):
    part, ff = w.shape[1], wg_ref.shape[1]
    copies = []
    for k, step in enumerate(steps):
        at = pl.multiple_of(lax.rem(m + step, MP) * part, part)
        for i, ref in enumerate((wg_ref, wu_ref)):
            copies.append(
                pltpu.make_async_copy(
                    ref.at[pl.ds(at, part)], w.at[k, :, pl.ds(i * ff, ff)], sem.at[k, i]
                )
            )
    return copies


def back_far_kernel(m_ref, a_ref, b_ref, c_ref, g_ref, wg_ref, wu_ref, *refs):
    high_ref, low_ref, s_ref, d_out = refs[:4]
    abc, d, w, in_sem, w_sem, out_sem = refs[4:]
    ff = a_ref.shape[1]
    tiles, _, rt, _ = abc.shape
    weights = load_weights(m_ref[0], (2,), wg_ref, wu_ref, w, w_sem)
    half = tiles // 2
    passes = g_ref.shape[0] // 2

    def arriving(r):
        at = pl.ds(pl.multiple_of(r * rt, rt), rt)
        return [
            pltpu.make_async_copy(ref.at[at], abc.at[r, i], in_sem.at[r, i])
            for i, ref in enumerate((a_ref, b_ref, c_ref))
        ]

    def leaving(r):
        at = pl.ds(pl.multiple_of(r * rt, rt), rt)
        return pltpu.make_async_copy(d.at[r], d_out.at[at], out_sem.at[r])

    for copy in arriving(0) + weights + sum((arriving(r) for r in range(1, tiles)), []):
        copy.start()
    for copy in weights:
        copy.wait()

    def step(r, carry):
        for copy in arriving(r):
            copy.wait()
        sums = contract_rows(abc[r, 2], g_ref[...].astype(bf16))
        lane = lax.broadcasted_iota(jnp.int32, (L, 2 * passes), 1)
        for p in range(rt // L):
            part = slice(p * L, (p + 1) * L)
            q = r * (rt // L) + p
            dact = g_ref[pl.ds(q, 1)].astype(bf16)
            d[r, part, :ff] = dact * abc[r, 0, part]
            d[r, part, ff:] = dact * abc[r, 1, part]
            mine = (lane == q) | (lane == q + passes)
            s_ref[pl.ds(pl.multiple_of(q * L, L), L)] = jnp.sum(
                jnp.where(mine, sums[part], 0.0), axis=1, keepdims=True
            )
        leaving(r).start()
        out = contract_rows(d[r], w[0]).astype(bf16)

        @pl.when(r < half)
        def _():
            high_ref[pl.ds(pl.multiple_of(r * rt, rt), rt)] = out

        @pl.when(r >= half)
        def _():
            low_ref[pl.ds(pl.multiple_of((r - half) * rt, rt), rt)] = out

        return carry

    lax.fori_loop(0, tiles, step, 0)
    for r in range(tiles):
        leaving(r).wait()


def back_far(m, a, b, c, g, w_gate, w_up):
    rows, ff = a.shape
    part = w_gate.shape[0] // MP
    rt = 256
    tiles = rows // rt
    anywhere = pl.BlockSpec(memory_space=pl.ANY)
    vmem = pl.BlockSpec(memory_space=pltpu.VMEM)
    return pl.pallas_call(
        back_far_kernel,
        in_specs=[pl.BlockSpec(memory_space=pltpu.SMEM)]
        + [anywhere] * 3
        + [vmem, anywhere, anywhere],
        out_specs=[vmem, vmem, vmem, anywhere],
        out_shape=[
            jax.ShapeDtypeStruct((rows // 2, part), bf16),
            jax.ShapeDtypeStruct((rows // 2, part), bf16),
            jax.ShapeDtypeStruct((rows, 1), f32),
            pltpu.HBM((rows, 2 * ff), bf16),
        ],
        scratch_shapes=[
            pltpu.VMEM((tiles, 3, rt, ff), bf16),
            pltpu.VMEM((tiles, rt, 2 * ff), bf16),
            pltpu.VMEM((1, part, 2 * ff), bf16),
            pltpu.SemaphoreType.DMA((tiles, 3)),
            pltpu.SemaphoreType.DMA((1, 2)),
            pltpu.SemaphoreType.DMA((tiles,)),
        ],
        compiler_params=pltpu.CompilerParams(vmem_limit_bytes=44 << 20),
        cost_estimate=pl.CostEstimate(flops=1, transcendentals=0, bytes_accessed=1),
        name="back_far",
    )(m, *map(in_hbm, (a, b, c)), g, in_hbm(w_gate), in_hbm(w_up))


def back_near_kernel(steps, m_ref, d_ref, wg_ref, wu_ref, *refs):
    count = 2 * len(steps)
    outs = refs[:count]
    d, w, out, in_sem, w_sem, out_sem = refs[count:]
    tiles, rt, _ = d.shape
    half = wg_ref.shape[1]
    weights = load_weights(m_ref[0], steps, wg_ref, wu_ref, w, w_sem)

    def arriving(r):
        at = pl.ds(pl.multiple_of(r * rt, rt), rt)
        return pltpu.make_async_copy(d_ref.at[at], d.at[r], in_sem.at[r])

    for copy in weights[:2] + [arriving(r) for r in range(tiles)] + weights[2:]:
        copy.start()

    def step(j, carry):
        k, r = j // tiles, lax.rem(j, tiles)

        @pl.when(r == 0)
        def _():
            for i in range(2):
                pltpu.make_async_copy(
                    wg_ref.at[pl.ds(0, w.shape[1])], w.at[k, :, pl.ds(i * half, half)], w_sem.at[k, i]
                ).wait()

        @pl.when(k == 0)
        def _():
            arriving(r).wait()

        out[j] = contract_rows(d[r], w[k]).astype(bf16)
        for i, ref in enumerate(outs):

            @pl.when(j == i)
            def _():
                pltpu.make_async_copy(out.at[j], ref, out_sem.at[i]).start()

        return carry

    lax.fori_loop(0, count, step, 0)
    for i, ref in enumerate(outs):
        pltpu.make_async_copy(out.at[i], ref, out_sem.at[i]).wait()


def back_near(m, steps, d, w_gate, w_up, flops):
    rows, ff2 = d.shape
    part = w_gate.shape[0] // MP
    tiles = 2
    count = tiles * len(steps)
    rt = rows // tiles
    anywhere = pl.BlockSpec(memory_space=pl.ANY)
    return pl.pallas_call(
        functools.partial(back_near_kernel, steps),
        in_specs=[pl.BlockSpec(memory_space=pltpu.SMEM)] + [anywhere] * 3,
        out_specs=[anywhere] * count,
        out_shape=[pltpu.HBM((rt, part), bf16)] * count,
        scratch_shapes=[
            pltpu.VMEM((tiles, rt, ff2), bf16),
            pltpu.VMEM((len(steps), part, ff2), bf16),
            pltpu.VMEM((count, rt, part), bf16),
            pltpu.SemaphoreType.DMA((tiles,)),
            pltpu.SemaphoreType.DMA((len(steps), 2)),
            pltpu.SemaphoreType.DMA((count,)),
        ],
        compiler_params=pltpu.CompilerParams(vmem_limit_bytes=44 << 20),
        cost_estimate=pl.CostEstimate(flops=flops, transcendentals=0, bytes_accessed=1),
        name="back_near",
    )(m, in_hbm(d), in_hbm(w_gate), in_hbm(w_up))


def finish_kernel(
    count, x_ref, own_ref, one_ref, two_ref, rms_ref, inner_ref, mask_ref, token_ref, gain_ref, *refs
):
    out_ref = refs[count]
    rms = rms_ref[...]
    normed = own_ref[...].astype(f32) + one_ref[...].astype(f32) + two_ref[...].astype(f32)
    grad = rms * gain_ref[...] * normed - x_ref[...].astype(f32) * (rms * rms * inner_ref[...])
    mask = mask_ref[...]
    for p in range(out_ref.shape[0] // L):
        part = slice(p * L, (p + 1) * L)
        out_ref[part] = (grad[part] + mask[part] * token_ref[0, p : p + 1]).astype(bf16)


def finish(chunk, before, x, own, one, two, rms, inner, mask, token, gain):
    rows, part = own.shape
    rt = 256
    steps = rows // rt
    here = pl.BlockSpec((rt, part), lambda r: (r, 0))
    whole = pl.BlockSpec((rt, part), lambda r: (chunk * steps + r, 0))
    column = pl.BlockSpec((rt, 1), lambda r: (chunk * steps + r, 0))
    return pl.pallas_call(
        functools.partial(finish_kernel, len(before)),
        grid=(steps,),
        in_specs=[whole, here, here, here, column, column, column]
        + [
            pl.BlockSpec((1, rt // L, part), lambda r: (chunk * steps + r, 0, 0)),
            pl.BlockSpec((1, part), lambda r: (0, 0)),
        ]
        + [pl.BlockSpec(memory_space=pl.ANY)] * len(before),
        out_specs=whole,
        out_shape=jax.ShapeDtypeStruct(x.shape, bf16),
        input_output_aliases={9 + k: k for k in range(len(before))},
        name="finish",
    )(x, own, one, two, rms, inner, mask, token.reshape(-1, rt // L, part), gain, *before)


def per_device(
    hidden_in, token_ids, passage_counts, positive_doc, queries, norm_gain, w_gate, w_up, w_down
):
    row_count, part = hidden_in.shape
    width = norm_gain.shape[0]
    docs = passage_counts.shape[0]
    passes = row_count // L
    most = passes // docs
    share = queries.shape[0] // MP
    chips = lax.axis_size(("x", "z"))
    cores = lax.axis_size("core")
    mi = lax.axis_index("mp")
    core = lax.axis_index("core")
    chip = lax.axis_index(("x", "z"))
    m = mi.astype(jnp.int32).reshape(1)

    mine = lax.all_to_all(
        queries.reshape(MP, share, part), "mp", split_axis=0, concat_axis=0, tiled=True
    )
    mine = jnp.moveaxis(mine, 0, 1).reshape(share, width)
    own_positive = lax.dynamic_slice_in_dim(positive_doc, mi * share, share)
    square = jnp.sum(mine.astype(f32) ** 2, axis=1)
    square_high = square.astype(bf16)
    square_low = (square - square_high.astype(f32)).astype(bf16)
    extra = jnp.stack([own_positive.astype(bf16), square_high, square_low], axis=1)
    extra = jnp.pad(extra, ((0, 0), (0, L - 3)))
    sent = jnp.concatenate([mine, extra], axis=1)

    chunks = []
    at = 0
    for k, rows in enumerate(CHUNKS):
        own = hidden_in[at : at + rows]
        if k == 1:
            own, sent = lax.optimization_barrier((own, sent))
        chunks.append((at, rows, own, shifted(own, 1), shifted(own, -1)))
        at += rows
    all_q = lax.all_gather(sent, ("x", "z"), axis=0)

    live_pass = jnp.arange(passes, dtype=jnp.int32) % most < jnp.repeat(passage_counts, most)
    other_live = swapped(live_pass.astype(jnp.int32)) > 0
    live = jnp.where(
        core == 0,
        jnp.concatenate([live_pass, other_live]),
        jnp.concatenate([other_live, live_pass]),
    ).astype(f32)[:, None]
    token_live = (token_ids.reshape(passes, L) != pad_token) & live_pass[:, None]
    live_float = token_live.astype(f32)
    mask = live_float.reshape(row_count, 1)
    divisor = jnp.maximum(jnp.sum(live_float, axis=1), 1.0)[:, None]
    gain = norm_gain.reshape(MP, 1, part)

    done = []
    before = ()
    for k, (at, rows, own, left, right) in enumerate(chunks):
        half = rows // 2
        high, low = shifted(left[:half], 1), shifted(right[half:], -1)
        part_mask = mask[at : at + rows]
        done.append(
            encode(
                m, k, row_count, before, own, right, left, high, low, part_mask, gain, w_gate, w_up
            )
        )
        before = done[-1][:3]
    a, b, c = before
    pool = jnp.concatenate([d[3] for d in done], axis=1)
    pool = jnp.moveaxis(pool, 0, 1).reshape(passes, -1)
    rms = jnp.concatenate([d[4] for d in done], axis=0)
    xpool = jnp.concatenate([d[5] for d in done], axis=0)

    high = pool.astype(bf16)
    low = (pool - high.astype(f32)).astype(bf16)
    branch = jnp.dot(jnp.concatenate([high, low], 0), w_down, preferred_element_type=f32)
    own_x = (jnp.arange(MP) == mi)[None, :, None].astype(f32) * xpool
    summed = (branch[:passes] + branch[passes:] + own_x.reshape(passes, width)) / divisor
    summed = copies_to_all(summed.astype(bf16), ("core", "mp"), cores * MP)
    summed = summed.reshape(cores, MP, passes, width).astype(f32).sum(axis=1)
    vecs = summed.reshape(cores * passes, width).astype(bf16)
    vec_float = vecs.astype(f32)
    vec_scale = lax.rsqrt(jnp.sum(vec_float * vec_float, axis=1, keepdims=True) + unit_epsilon)

    all_q = all_q.reshape(chips * share, width + L)
    q = all_q[:, :width]
    extra = all_q[:, width:].astype(f32)
    positive = extra[:, 0]
    query_scale = lax.rsqrt(extra[:, 1] + extra[:, 2] + unit_epsilon)
    raw = contract_rows(vecs, q)
    weights = live * jnp.exp(score_scale * raw * query_scale[None, :] * vec_scale)
    k = jnp.arange(cores * passes, dtype=jnp.int32)
    doc = chip * (cores * docs) + k // most
    hit = (positive[None, :] == doc.astype(f32)[:, None]).astype(f32)
    mass = jnp.stack([jnp.sum(weights, axis=0), jnp.sum(weights * hit, axis=0)])
    mass = copies_to_all(mass.reshape(8, -1), ("x", "z"), chips).sum(axis=0).reshape(2, -1)
    total, held = mass[0], mass[1]
    loss = jnp.log(total) - jnp.log(held)
    own_loss = lax.dynamic_slice_in_dim(loss, chip * share, share)

    coef = (loss_seed * score_scale) * query_scale[None, :] * (
        weights / total[None, :] - hit * weights / held[None, :]
    )
    grad = jnp.dot(coef.astype(bf16), q, preferred_element_type=f32)
    term = jnp.sum(coef * raw, axis=1, keepdims=True)
    grad = jnp.concatenate([grad, jnp.broadcast_to(term, (cores * passes, L))], axis=1).astype(bf16)
    grad = jnp.broadcast_to(
        grad.reshape(cores, 1, passes, width + L), (cores, MP, passes, width + L)
    ).reshape(cores * MP, passes, width + L)
    grad = lax.all_to_all(grad, ("core", "mp"), split_axis=0, concat_axis=0, tiled=True)
    grad = grad.astype(f32).sum(axis=0)
    own_vec = lax.dynamic_slice_in_dim(vec_float, core * passes, passes)
    scale = lax.dynamic_slice_in_dim(vec_scale, core * passes, passes)
    change = scale * grad[:, :width] - own_vec * (scale**3 * grad[:, width : width + 1])
    token_grad = (change / divisor).astype(bf16)
    dact = contract_rows(token_grad, w_down)
    dact_high = dact.astype(bf16).astype(f32)
    dact = jnp.concatenate([dact_high, dact - dact_high], axis=0)

    high, low, s, d = back_far(m, a, b, c, dact, w_gate, w_up)
    from_right = shifted(high, -1)
    from_left = shifted(low, 1)
    right_high, right_low, left_high, left_low = back_near(m, (1, 3), d, w_gate, w_up, 1)
    left_low = shifted(left_low, -1)
    right_high = shifted(right_high, 1)
    right_low = (right_low.astype(f32) + from_left.astype(f32)).astype(bf16)
    left_high = (left_high.astype(f32) + from_right.astype(f32)).astype(bf16)
    right_low, left_high, d = lax.optimization_barrier((right_low, left_high, d))
    right_low = shifted(right_low, 1)
    left_high = shifted(left_high, -1)
    own_high, own_low = back_near(m, (0,), d, w_gate, w_up, 1 << 38)
    small = jnp.concatenate(
        [s.reshape(passes, L), jnp.pad(own_loss[None, :], ((0, 7), (0, L - share)))], axis=0
    )
    own_high, small = lax.optimization_barrier((own_high, small))
    small = copies_to_all(small, "mp", MP)
    inner = small[:, :passes].sum(axis=0).reshape(row_count, 1) / width
    query_loss = small[:, passes, :share].reshape(MP * share)
    own_gain = lax.dynamic_slice_in_dim(norm_gain, mi * part, part)[None, :]
    own_token = lax.dynamic_slice_in_dim(token_grad, mi * part, part, axis=1).astype(f32)
    rest = (rms, inner, mask, own_token, own_gain)
    hidden_grad = finish(1, (), hidden_in, own_low, left_low, right_low, *rest)
    hidden_grad = finish(0, (hidden_grad,), hidden_in, own_high, left_high, right_high, *rest)
    return query_loss, hidden_grad


def solution(mesh):
    shape = (4, 4, 2, MP)
    split = Mesh(mesh.devices.reshape(shape), ("x", "z", "core", "mp"))
    dp = ("x", "z", "core")
    return jax.shard_map(
        per_device,
        mesh=split,
        in_specs=(
            P(dp, "mp"),
            P(dp),
            P(dp),
            P(dp),
            P(dp, "mp"),
            P(),
            P(None, "mp"),
            P(None, "mp"),
            P("mp", None),
        ),
        out_specs=(P(dp), P(dp, "mp")),
        check_vma=False,
    )
```

```python
import functools

import jax
import jax.numpy as jnp
from jax import lax
from jax.experimental import pallas as pl
from jax.experimental.pallas import tpu as pltpu
from jax.sharding import Mesh, PartitionSpec as P

L = 128
pad_token = 128001
score_scale = 20.0
loss_seed = 4096.0
norm_epsilon = 1e-05
unit_epsilon = 1e-06
MP = 4
FT = 256
SCOPED = 40 << 20
CHUNKS = (512, 512)
bf16 = jnp.bfloat16
f32 = jnp.float32


def shifted(x, by):
    return lax.ppermute(x, "mp", [(i, (i + by) % MP) for i in range(MP)])


def across(left, right):
    half = left.shape[0] // 2
    return shifted(left[:half], 1), shifted(right[half:], -1)


def swapped(x):
    return lax.ppermute(x, "core", [(0, 1), (1, 0)])


def copies_to_all(x, axes, count):
    return lax.all_to_all(
        jnp.broadcast_to(x, (count, *x.shape)), axes, split_axis=0, concat_axis=0, tiled=True
    )


def in_hbm(x):
    return pltpu.with_memory_space_constraint(x, pltpu.HBM)


def contract_rows(left, right):
    return lax.dot_general(
        left, right, (((1,), (1,)), ((), ())), preferred_element_type=f32
    )


def each(count, body):
    def step(n, carry):
        body(n)
        return carry

    lax.fori_loop(0, count, step, 0)


anywhere = pl.BlockSpec(memory_space=pl.ANY)
vmem = pl.BlockSpec(memory_space=pltpu.VMEM)
smem = pl.BlockSpec(memory_space=pltpu.SMEM)


def encode_kernel(
    chunk, count, m_ref, own_ref, right_ref, left_ref, high_ref, low_ref, mask_ref, gain_ref, wg_ref, wu_ref, *refs
):
    a_out, b_out, c_out, pool_ref, rms_ref, xpool_ref = refs[count : count + 6]
    xin, xs, w, results, in_sem, w_sem, out_sem = refs[count + 6 :]
    rows, part = own_ref.shape
    half = rows // 2
    tiles = w.shape[0]
    m = m_ref[0]
    sources = [
        (own_ref, xin.at[0]),
        (right_ref, xin.at[1]),
        (left_ref, xin.at[3]),
        (high_ref, xin.at[2, pl.ds(0, half)]),
        (low_ref, xin.at[2, pl.ds(half, half)]),
    ]
    arriving = [pltpu.make_async_copy(a, b, in_sem.at[k]) for k, (a, b) in enumerate(sources)]
    for copy in arriving:
        copy.start()
    def weight_copies(n):
        columns = pl.ds(pl.multiple_of(n * FT, FT), FT)
        copies = []
        for k in range(MP):
            at = pl.multiple_of(lax.rem(m + k, MP) * part, part)
            for i, ref in enumerate((wg_ref, wu_ref)):
                copies.append(
                    pltpu.make_async_copy(
                        ref.at[pl.ds(at, part), columns],
                        w.at[n, pl.ds(k * part, part), pl.ds(i * FT, FT)],
                        w_sem.at[n, 2 * k + i],
                    )
                )
        return copies

    def result_copies(n):
        return [
            pltpu.make_async_copy(
                results.at[n, i],
                out.at[pl.ds(chunk * rows, rows), pl.ds(pl.multiple_of(n * FT, FT), FT)],
                out_sem.at[n, i],
            )
            for i, out in enumerate((a_out, b_out, c_out))
        ]

    def start_weights(n):
        for copy in weight_copies(n):
            copy.start()

    each(tiles, start_weights)
    for copy in arriving:
        copy.wait()

    def normalise(p):
        at = pl.ds(pl.multiple_of(p * L, L), L)
        mask = mask_ref[at]
        total = None
        for k in range(MP):
            v = xin[k, at].astype(f32)
            square = jnp.sum(v * v, axis=1, keepdims=True)
            total = square if total is None else total + square
        rms = lax.rsqrt(total / (MP * part) + norm_epsilon)
        rms_ref[at] = rms
        for k in range(MP):
            j = lax.rem(m + k, MP)
            v = xin[k, at].astype(f32)
            xs[at, k * part : (k + 1) * part] = (v * rms * gain_ref[j]).astype(bf16)
            xpool_ref[p, pl.ds(j, 1)] = jnp.sum(v * mask, axis=0, keepdims=True)

    each(rows // L, normalise)

    def multiply(n):
        for copy in weight_copies(n):
            copy.wait()
        for r in range(0, rows, rows):
            at = slice(r, r + rows)
            both = jnp.dot(xs[at], w[n], preferred_element_type=f32)
            gate, up = both[:, :FT], both[:, FT:]
            mask = mask_ref[at]
            sig = jax.nn.sigmoid(gate)
            up = up * mask
            b = gate * sig
            bu = b * up
            act = bu.astype(bf16).astype(f32)
            for p in range(rows // L):
                q = r // L + p
                pool_ref[n, q : q + 1] = jnp.sum(act[p * L : (p + 1) * L], axis=0, keepdims=True)
            a = up * (sig + b * (1.0 - sig))
            results[n, 0, at] = a.astype(bf16)
            results[n, 1, at] = (b * mask).astype(bf16)
            results[n, 2, at] = (a * gate + bu).astype(bf16)
        for copy in result_copies(n):
            copy.start()

    each(tiles, multiply)

    def wait_results(n):
        for copy in result_copies(n):
            copy.wait()

    each(tiles, wait_results)


def encode(m, chunk, total, before, own, right, left, high, low, mask, gain, w_gate, w_up):
    rows, part = own.shape
    width, ff = w_gate.shape
    passes = rows // L
    tiles = ff // FT
    return pl.pallas_call(
        functools.partial(encode_kernel, chunk, len(before)),
        in_specs=[smem]
        + [anywhere] * 5
        + [vmem, vmem, anywhere, anywhere]
        + [anywhere] * len(before),
        out_specs=[anywhere] * 3 + [vmem] * 3,
        out_shape=[pltpu.HBM((total, ff), bf16)] * 3
        + [
            jax.ShapeDtypeStruct((tiles, passes, FT), f32),
            jax.ShapeDtypeStruct((rows, 1), f32),
            jax.ShapeDtypeStruct((passes, MP, part), f32),
        ],
        scratch_shapes=[
            pltpu.VMEM((MP, rows, part), bf16),
            pltpu.VMEM((rows, width), bf16),
            pltpu.VMEM((tiles, width, 2 * FT), bf16),
            pltpu.VMEM((tiles, 3, rows, FT), bf16),
            pltpu.SemaphoreType.DMA((5,)),
            pltpu.SemaphoreType.DMA((tiles, 2 * MP)),
            pltpu.SemaphoreType.DMA((tiles, 3)),
        ],
        compiler_params=pltpu.CompilerParams(vmem_limit_bytes=44 << 20),
        cost_estimate=pl.CostEstimate(
            flops=4 * rows * width * ff,
            transcendentals=rows * ff,
            bytes_accessed=4 * width * ff + 2 * rows * width + 6 * rows * ff,
        ),
        input_output_aliases={10 + k: k for k in range(len(before))},
        name="encode",
    )(
        m, *map(in_hbm, (own, right, left, high, low)), mask, gain,
        in_hbm(w_gate), in_hbm(w_up), *map(in_hbm, before),
    )


def load_weights(m, steps, wg_ref, wu_ref, w, sem):
    part, ff = w.shape[1], wg_ref.shape[1]
    copies = []
    for k, step in enumerate(steps):
        at = pl.multiple_of(lax.rem(m + step, MP) * part, part)
        for i, ref in enumerate((wg_ref, wu_ref)):
            copies.append(
                pltpu.make_async_copy(
                    ref.at[pl.ds(at, part)], w.at[k, :, pl.ds(i * ff, ff)], sem.at[k, i]
                )
            )
    return copies


def back_kernel(steps, first, m_ref, a_ref, b_ref, c_ref, g_in, gs_ref, wg_ref, wu_ref, *refs):
    if first:
        wd_ref, *refs = refs
    count = 2 * len(steps)
    outs = refs[:count]
    last = not first and len(steps) == 1
    if first:
        g_ref, ab, w, in_sem, w_sem = refs[count:]
    elif last:
        s_ref, c, ab, w, in_sem, w_sem = refs[count:]
    else:
        ab, w, in_sem, w_sem = refs[count:]
    part = outs[0].shape[1]
    ff = a_ref.shape[1]
    tiles, rt, _ = ab.shape
    here = tiles // 2
    weights = load_weights(m_ref[0], steps, wg_ref, wu_ref, w, w_sem)
    passes = g_in.shape[0]

    def arriving(r):
        at = pl.ds(pl.multiple_of(r * rt, rt), rt)
        copies = [
            pltpu.make_async_copy(ref.at[at], ab.at[r, :, pl.ds(i * ff, ff)], in_sem.at[r, i])
            for i, ref in enumerate((a_ref, b_ref))
        ]
        if last:
            copies.append(pltpu.make_async_copy(c_ref.at[at], c.at[r], in_sem.at[r, 2]))
        return copies

    for copy in arriving(0) + weights[:2]:
        copy.start()
    for r in range(1, tiles):
        for copy in arriving(r):
            copy.start()
    for copy in weights[2:]:
        copy.start()

    if first:

        def dact_tile(n):
            at = pl.ds(pl.multiple_of(n * FT, FT), FT)
            g_ref[:, at] = contract_rows(wd_ref[at], g_in[...]).T

        each(ff // FT, dact_tile)
        source = g_ref
    else:
        source = g_in

    def scale(r):
        for copy in arriving(r):
            copy.wait()
        lane = lax.broadcasted_iota(jnp.int32, (L, 2 * passes), 1)
        for p in range(rt // L):
            at = slice(p * L, (p + 1) * L)
            q = r * (rt // L) + p
            dact = source[pl.ds(q, 1)].astype(bf16)
            ab[r, at, :ff] = dact * ab[r, at, :ff]
            ab[r, at, ff:] = dact * ab[r, at, ff:]
            if last:
                sums = contract_rows(c[r, at], gs_ref[...])
                mine = (lane == q) | (lane == q + passes)
                s_ref[pl.ds(pl.multiple_of(q * L, L), L)] = jnp.sum(
                    jnp.where(mine, sums, 0.0), axis=1, keepdims=True
                )

    def multiply(j):
        k, r = j // tiles, lax.rem(j, tiles)

        @pl.when(k == 0)
        def _():
            scale(r)

        @pl.when(r == 0)
        def _():
            for i in range(2):
                pltpu.make_async_copy(
                    wg_ref.at[pl.ds(0, part)], w.at[k, :, pl.ds(i * ff, ff)], w_sem.at[k, i]
                ).wait()

        out = contract_rows(ab[r], w[k]).astype(bf16)
        at = pl.ds(pl.multiple_of(lax.rem(j, here) * rt, rt), rt)
        for i, ref in enumerate(outs):

            @pl.when(j // here == i)
            def _():
                ref[at] = out

    each(len(steps) * tiles, multiply)


def back(m, steps, rt, first, a, b, c, g, gs, w_gate, w_up, w_down):
    rows, ff = a.shape
    width = w_gate.shape[0]
    part = width // MP
    tiles = rows // rt
    last = not first and len(steps) == 1
    out = pltpu.HBM((rows // 2, part), bf16)
    more = []
    scratch = []
    if first:
        more = [jax.ShapeDtypeStruct((g.shape[0], ff), f32)]
    elif last:
        more = [jax.ShapeDtypeStruct((rows, 1), f32)]
        scratch = [pltpu.VMEM((tiles, rt, ff), bf16)]
    return pl.pallas_call(
        functools.partial(back_kernel, steps, first),
        in_specs=[smem] + [anywhere] * 3 + [vmem] * 2 + [anywhere] * 2 + [vmem] * first,
        out_specs=[vmem] * (2 * len(steps) + len(more)),
        out_shape=[out] * (2 * len(steps)) + more,
        scratch_shapes=scratch
        + [
            pltpu.VMEM((tiles, rt, 2 * ff), bf16),
            pltpu.VMEM((len(steps), part, 2 * ff), bf16),
            pltpu.SemaphoreType.DMA((tiles, 3)),
            pltpu.SemaphoreType.DMA((len(steps), 2)),
        ],
        compiler_params=pltpu.CompilerParams(vmem_limit_bytes=SCOPED),
        cost_estimate=pl.CostEstimate(flops=1, transcendentals=0, bytes_accessed=1),
        name="back",
    )(m, *map(in_hbm, (a, b, c)), g, gs, in_hbm(w_gate), in_hbm(w_up), *([w_down] if first else []))


def finish_kernel(
    x_ref, high_ref, low_ref, one_ref, two_ref, rms_ref, inner_ref, mask_ref, token_ref, gain_ref, out_ref
):
    half = pl.num_programs(0) // 2
    rms = rms_ref[...]
    eye = lax.broadcasted_iota(jnp.int32, (L, L), 0) == lax.broadcasted_iota(jnp.int32, (L, L), 1)
    inner = jnp.concatenate(
        [
            jnp.sum(jnp.where(eye, inner_ref[0, p : p + 1], 0.0), axis=1, keepdims=True)
            for p in range(out_ref.shape[0] // L)
        ],
        axis=0,
    )
    own = jnp.where(pl.program_id(0) < half, high_ref[...], low_ref[...]).astype(f32)
    normed = own + one_ref[...].astype(f32) + two_ref[...].astype(f32)
    grad = rms * gain_ref[...] * normed - x_ref[...].astype(f32) * (rms * rms * inner)
    mask = mask_ref[...]
    for p in range(out_ref.shape[0] // L):
        part = slice(p * L, (p + 1) * L)
        out_ref[part] = (grad[part] + mask[part] * token_ref[0, p : p + 1]).astype(bf16)


def finish(x, high, low, one, two, rms, inner, mask, token, gain):
    rows, part = x.shape
    rt = 256
    half = rows // (2 * rt)
    whole = pl.BlockSpec((rt, part), lambda r: (r, 0))
    column = pl.BlockSpec((rt, 1), lambda r: (r, 0))
    return pl.pallas_call(
        finish_kernel,
        grid=(rows // rt,),
        in_specs=[
            whole,
            pl.BlockSpec((rt, part), lambda r: (jnp.minimum(r, half - 1), 0)),
            pl.BlockSpec((rt, part), lambda r: (jnp.maximum(r - half, 0), 0)),
            whole,
            whole,
            column,
            pl.BlockSpec((1, rt // L, L), lambda r: (r, 0, 0)),
            column,
            pl.BlockSpec((1, rt // L, part), lambda r: (r, 0, 0)),
            pl.BlockSpec((1, part), lambda r: (0, 0)),
        ],
        out_specs=whole,
        out_shape=jax.ShapeDtypeStruct(x.shape, bf16),
        compiler_params=pltpu.CompilerParams(vmem_limit_bytes=16 << 20),
        name="finish",
    )(*map(in_hbm, (x, high, low, one, two)), rms, inner, mask, token.reshape(-1, rt // L, part), gain)


def per_device(
    hidden_in, token_ids, passage_counts, positive_doc, queries, norm_gain, w_gate, w_up, w_down
):
    row_count, part = hidden_in.shape
    width = norm_gain.shape[0]
    docs = passage_counts.shape[0]
    passes = row_count // L
    most = passes // docs
    share = queries.shape[0] // MP
    chips = lax.axis_size(("x", "z"))
    cores = lax.axis_size("core")
    mi = lax.axis_index("mp")
    core = lax.axis_index("core")
    chip = lax.axis_index(("x", "z"))
    m = mi.astype(jnp.int32).reshape(1)

    mine = lax.all_to_all(
        queries.reshape(MP, share, part), "mp", split_axis=0, concat_axis=0, tiled=True
    )
    mine = jnp.moveaxis(mine, 0, 1).reshape(share, width)
    own_positive = lax.dynamic_slice_in_dim(positive_doc, mi * share, share)
    square = jnp.sum(mine.astype(f32) ** 2, axis=1)
    square_high = square.astype(bf16)
    square_low = (square - square_high.astype(f32)).astype(bf16)
    extra = jnp.stack([own_positive.astype(bf16), square_high, square_low], axis=1)
    extra = jnp.pad(extra, ((0, 0), (0, L - 3)))
    sent = jnp.concatenate([mine, extra], axis=1)

    chunks = []
    at = 0
    for rows in CHUNKS:
        own = hidden_in[at : at + rows]
        if chunks:
            own, sent, *last = lax.optimization_barrier((own, sent, *chunks[-1][1:]))
            chunks[-1] = (chunks[-1][0], *last)
        left, right = shifted(own, 1), shifted(own, -1)
        chunks.append((at, own, right, left, *(across(left, right) if at == 0 else ())))
        at += rows
    all_q = lax.all_gather(sent, ("x", "z"), axis=0)

    live_pass = jnp.arange(passes, dtype=jnp.int32) % most < jnp.repeat(passage_counts, most)
    other_live = swapped(live_pass.astype(jnp.int32)) > 0
    live = jnp.where(
        core == 0,
        jnp.concatenate([live_pass, other_live]),
        jnp.concatenate([other_live, live_pass]),
    ).astype(f32)[:, None]
    token_live = (token_ids.reshape(passes, L) != pad_token) & live_pass[:, None]
    live_float = token_live.astype(f32)
    mask = live_float.reshape(row_count, 1)
    divisor = jnp.maximum(jnp.sum(live_float, axis=1), 1.0)[:, None]
    gain = norm_gain.reshape(MP, 1, part)

    done = []
    before = ()
    for k, (at, *pieces) in enumerate(chunks):
        if k > 0:
            pool, right, left = lax.optimization_barrier((done[-1][3], *pieces[1:]))
            done[-1] = (*done[-1][:3], pool, *done[-1][4:])
            pieces = (pieces[0], right, left, *across(left, right))
        part_mask = mask[at : at + CHUNKS[k]]
        done.append(encode(m, k, row_count, before, *pieces, part_mask, gain, w_gate, w_up))
        before = done[-1][:3]
    a, b, c = before
    pool = jnp.concatenate([d[3] for d in done], axis=1)
    pool = jnp.moveaxis(pool, 0, 1).reshape(passes, -1)
    rms = jnp.concatenate([d[4] for d in done], axis=0)
    xpool = jnp.concatenate([d[5] for d in done], axis=0)

    high = pool.astype(bf16)
    low = (pool - high.astype(f32)).astype(bf16)
    branch = jnp.dot(jnp.concatenate([high, low], 0), w_down, preferred_element_type=f32)
    own_x = (jnp.arange(MP) == mi)[None, :, None].astype(f32) * xpool
    summed = (branch[:passes] + branch[passes:] + own_x.reshape(passes, width)) / divisor
    summed = copies_to_all(summed.astype(bf16), ("core", "mp"), cores * MP)
    summed = summed.reshape(cores, MP, passes, width).astype(f32).sum(axis=1)
    vecs = summed.reshape(cores * passes, width).astype(bf16)
    vec_float = vecs.astype(f32)
    vec_scale = lax.rsqrt(jnp.sum(vec_float * vec_float, axis=1, keepdims=True) + unit_epsilon)

    all_q = all_q.reshape(chips * share, width + L)
    q = all_q[:, :width]
    extra = all_q[:, width:].astype(f32)
    positive = extra[:, 0]
    query_scale = lax.rsqrt(extra[:, 1] + extra[:, 2] + unit_epsilon)
    raw = contract_rows(vecs, q)
    weights = live * jnp.exp(score_scale * raw * query_scale[None, :] * vec_scale)
    k = jnp.arange(cores * passes, dtype=jnp.int32)
    doc = chip * (cores * docs) + k // most
    hit = (positive[None, :] == doc.astype(f32)[:, None]).astype(f32)
    mass = jnp.stack([jnp.sum(weights, axis=0), jnp.sum(weights * hit, axis=0)])
    mass = copies_to_all(mass.reshape(8, -1), ("x", "z"), chips).sum(axis=0).reshape(2, -1)
    total, held = mass[0], mass[1]
    loss = jnp.log(total) - jnp.log(held)
    own_loss = lax.dynamic_slice_in_dim(loss, chip * share, share)

    coef = (loss_seed * score_scale) * query_scale[None, :] * (
        weights / total[None, :] - hit * weights / held[None, :]
    )
    grad = jnp.dot(coef.astype(bf16), q, preferred_element_type=f32)
    term = jnp.sum(coef * raw, axis=1, keepdims=True)
    grad = jnp.concatenate([grad, jnp.broadcast_to(term, (cores * passes, L))], axis=1).astype(bf16)
    grad = jnp.broadcast_to(
        grad.reshape(cores, 1, passes, width + L), (cores, MP, passes, width + L)
    ).reshape(cores * MP, passes, width + L)
    grad = lax.all_to_all(grad, ("core", "mp"), split_axis=0, concat_axis=0, tiled=True)
    grad = grad.astype(f32).sum(axis=0)
    own_vec = lax.dynamic_slice_in_dim(vec_float, core * passes, passes)
    scale = lax.dynamic_slice_in_dim(vec_scale, core * passes, passes)
    change = scale * grad[:, :width] - own_vec * (scale**3 * grad[:, width : width + 1])
    token_grad = (change / divisor).astype(bf16)

    tensors = (w_gate, w_up, w_down)
    none = jnp.zeros((2 * passes, pool.shape[1]), bf16)
    high, low, g = back(m, (2,), 256, True, a, b, c, token_grad, none, *tensors)
    from_right = shifted(high, -1)
    from_left = shifted(low, 1)
    right_high, right_low, left_high, left_low = back(
        m, (1, 3), 512, False, a, b, c, g, none, *tensors
    )
    right_low = (right_low.astype(f32) + from_left.astype(f32)).astype(bf16)
    left_high = (left_high.astype(f32) + from_right.astype(f32)).astype(bf16)
    right = jnp.concatenate([right_high, right_low], axis=0)
    left = jnp.concatenate([left_high, left_low], axis=0)
    right, left, g = lax.optimization_barrier((right, left, g))
    right = shifted(right, 1)
    left = shifted(left, -1)
    g_high = g.astype(bf16)
    gs = jnp.concatenate([g_high, (g - g_high.astype(f32)).astype(bf16)], axis=0)
    own_high, own_low, s = back(m, (0,), 512, False, a, b, c, g, gs, *tensors)
    small = jnp.concatenate(
        [s.reshape(passes, L), jnp.pad(own_loss[None, :], ((0, 7), (0, L - share)))], axis=0
    )
    small = copies_to_all(small, "mp", MP)
    inner = small[:, :passes].sum(axis=0).reshape(passes // 2, 2, L) / width
    query_loss = small[:, passes, :share].reshape(MP * share)
    own_gain = lax.dynamic_slice_in_dim(norm_gain, mi * part, part)[None, :]
    own_token = lax.dynamic_slice_in_dim(token_grad, mi * part, part, axis=1).astype(f32)
    rest = (rms, inner, mask, own_token, own_gain)
    hidden_grad = finish(hidden_in, own_high, own_low, right, left, *rest)
    return query_loss, hidden_grad


def solution(mesh):
    shape = (4, 4, 2, MP)
    split = Mesh(mesh.devices.reshape(shape), ("x", "z", "core", "mp"))
    dp = ("x", "z", "core")
    return jax.shard_map(
        per_device,
        mesh=split,
        in_specs=(
            P(dp, "mp"),
            P(dp),
            P(dp),
            P(dp),
            P(dp, "mp"),
            P(),
            P(None, "mp"),
            P(None, "mp"),
            P("mp", None),
        ),
        out_specs=(P(dp), P(dp, "mp")),
        check_vma=False,
    )
```

```python
import functools

import jax
import jax.numpy as jnp
from jax import lax
from jax.experimental import pallas as pl
from jax.experimental.pallas import tpu as pltpu
from jax.sharding import Mesh, PartitionSpec as P

L = 128
pad_token = 128001
score_scale = 20.0
loss_seed = 4096.0
norm_epsilon = 1e-05
unit_epsilon = 1e-06
MP = 4
FT = 256
SCOPED = 40 << 20
bf16 = jnp.bfloat16
f32 = jnp.float32


def shifted(x, by):
    return lax.ppermute(x, "mp", [(i, (i + by) % MP) for i in range(MP)])


def across(left, right):
    half = left.shape[0] // 2
    return shifted(left[:half], 1), shifted(right[half:], -1)


def swapped(x):
    return lax.ppermute(x, "core", [(0, 1), (1, 0)])


def copies_to_all(x, axes, count):
    return lax.all_to_all(
        jnp.broadcast_to(x, (count, *x.shape)), axes, split_axis=0, concat_axis=0, tiled=True
    )


def in_hbm(x):
    return pltpu.with_memory_space_constraint(x, pltpu.HBM)


def contract_rows(left, right):
    return lax.dot_general(
        left, right, (((1,), (1,)), ((), ())), preferred_element_type=f32
    )


def each(count, body):
    def step(n, carry):
        body(n)
        return carry

    lax.fori_loop(0, count, step, 0)


anywhere = pl.BlockSpec(memory_space=pl.ANY)
vmem = pl.BlockSpec(memory_space=pltpu.VMEM)
smem = pl.BlockSpec(memory_space=pltpu.SMEM)


def loop_copies(copies, count):
    def start(n):
        for copy in copies(n):
            copy.start()

    each(count, start)


def weight_tiles(m, steps, part, wg_ref, wu_ref, w, sem):
    def copies(n):
        columns = pl.ds(pl.multiple_of(n * FT, FT), FT)
        return [
            pltpu.make_async_copy(
                ref.at[pl.ds(pl.multiple_of(lax.rem(m + step, MP) * part, part), part), columns],
                w.at[n, pl.ds(k * part, part), pl.ds(i * FT, FT)],
                sem.at[n, 2 * k + i],
            )
            for k, step in enumerate(steps)
            for i, ref in enumerate((wg_ref, wu_ref))
        ]

    return copies


NEAR = (0, 1, 3)


def encode_near_kernel(
    m_ref, own_ref, right_ref, left_ref, mask_ref, gain_ref, wg_ref, wu_ref,
    acc_out, square_ref, xpool_ref, xin, xs, w, acc, in_sem, w_sem, out_sem,
):
    rows, part = own_ref.shape
    tiles = w.shape[0]
    m = m_ref[0]
    arriving = [
        pltpu.make_async_copy(ref, xin.at[k], in_sem.at[k])
        for k, ref in enumerate((own_ref, right_ref, left_ref))
    ]
    for copy in arriving:
        copy.start()
    weights = weight_tiles(m, NEAR, part, wg_ref, wu_ref, w, w_sem)
    loop_copies(weights, tiles)
    for copy in arriving:
        copy.wait()

    def scale(p):
        at = pl.ds(pl.multiple_of(p * L, L), L)
        total = None
        for k, step in enumerate(NEAR):
            v = xin[k, at].astype(f32)
            square = jnp.sum(v * v, axis=1, keepdims=True)
            total = square if total is None else total + square
            xs[at, k * part : (k + 1) * part] = (v * gain_ref[lax.rem(m + step, MP)]).astype(bf16)
            if k == 0:
                xpool_ref[pl.ds(p, 1)] = jnp.sum(v * mask_ref[at], axis=0, keepdims=True)
        square_ref[at] = total

    each(rows // L, scale)

    def leaving(n):
        return pltpu.make_async_copy(acc.at[lax.rem(n, 2)], acc_out.at[n], out_sem.at[n])

    def multiply(n):
        for copy in weights(n):
            copy.wait()

        @pl.when(n >= 2)
        def _():
            leaving(n - 2).wait()

        acc[lax.rem(n, 2)] = jnp.dot(xs[...], w[n], preferred_element_type=f32)
        leaving(n).start()

    each(tiles, multiply)
    leaving(tiles - 2).wait()
    leaving(tiles - 1).wait()


def encode_near(m, own, right, left, mask, gain, w_gate, w_up):
    rows, part = own.shape
    width, ff = w_gate.shape
    tiles = ff // FT
    return pl.pallas_call(
        encode_near_kernel,
        in_specs=[smem] + [anywhere] * 3 + [vmem, vmem, anywhere, anywhere],
        out_specs=[anywhere, vmem, vmem],
        out_shape=[
            pltpu.HBM((tiles, rows, 2 * FT), f32),
            jax.ShapeDtypeStruct((rows, 1), f32),
            jax.ShapeDtypeStruct((rows // L, part), f32),
        ],
        scratch_shapes=[
            pltpu.VMEM((len(NEAR), rows, part), bf16),
            pltpu.VMEM((rows, len(NEAR) * part), bf16),
            pltpu.VMEM((tiles, len(NEAR) * part, 2 * FT), bf16),
            pltpu.VMEM((2, rows, 2 * FT), f32),
            pltpu.SemaphoreType.DMA((len(NEAR),)),
            pltpu.SemaphoreType.DMA((tiles, 2 * len(NEAR))),
            pltpu.SemaphoreType.DMA((tiles,)),
        ],
        compiler_params=pltpu.CompilerParams(vmem_limit_bytes=SCOPED),
        cost_estimate=pl.CostEstimate(
            flops=3 * rows * width * ff, transcendentals=0, bytes_accessed=4 * rows * width
        ),
        name="encode_near",
    )(m, *map(in_hbm, (own, right, left)), mask, gain, in_hbm(w_gate), in_hbm(w_up))


def encode_far_kernel(
    m_ref, high_ref, low_ref, acc_ref, square_ref, mask_ref, gain_ref, wg_ref, wu_ref,
    a_out, b_out, c_out, pool_ref, rms_ref, xin, xs, w, acc, results, in_sem, w_sem, acc_sem, out_sem,
):
    rows, part = xin.shape
    half = rows // 2
    tiles = w.shape[0]
    m = m_ref[0]
    arriving = [
        pltpu.make_async_copy(ref, xin.at[pl.ds(k * half, half)], in_sem.at[k])
        for k, ref in enumerate((high_ref, low_ref))
    ]
    for copy in arriving:
        copy.start()
    weights = weight_tiles(m, (2,), part, wg_ref, wu_ref, w, w_sem)

    def inputs(n):
        return [*weights(n), pltpu.make_async_copy(acc_ref.at[n], acc.at[n], acc_sem.at[n])]

    loop_copies(inputs, tiles)
    for copy in arriving:
        copy.wait()

    def scale(p):
        at = pl.ds(pl.multiple_of(p * L, L), L)
        v = xin[at].astype(f32)
        total = square_ref[at] + jnp.sum(v * v, axis=1, keepdims=True)
        rms_ref[at] = lax.rsqrt(total / (MP * part) + norm_epsilon)
        xs[at] = (v * gain_ref[lax.rem(m + 2, MP)]).astype(bf16)

    each(rows // L, scale)

    def leaving(n):
        return [
            pltpu.make_async_copy(
                results.at[n, i],
                out.at[:, pl.ds(pl.multiple_of(n * FT, FT), FT)],
                out_sem.at[n, i],
            )
            for i, out in enumerate((a_out, b_out, c_out))
        ]

    def multiply(n):
        for copy in inputs(n):
            copy.wait()
        for r in range(2):
            at = slice(r * half, (r + 1) * half)
            both = acc[n, at] + jnp.dot(xs[at], w[n], preferred_element_type=f32)
            both *= rms_ref[at]
            gate, up = both[:, :FT], both[:, FT:]
            mask = mask_ref[at]
            sig = jax.nn.sigmoid(gate)
            up = up * mask
            b = gate * sig
            bu = b * up
            act = bu.astype(bf16).astype(f32)
            for p in range(half // L):
                q = r * (half // L) + p
                pool_ref[n, q : q + 1] = jnp.sum(act[p * L : (p + 1) * L], axis=0, keepdims=True)
            a = up * (sig + b * (1.0 - sig))
            results[n, 0, at] = a.astype(bf16)
            results[n, 1, at] = (b * mask).astype(bf16)
            results[n, 2, at] = (a * gate + bu).astype(bf16)
        for copy in leaving(n):
            copy.start()

    each(tiles, multiply)

    def wait(n):
        for copy in leaving(n):
            copy.wait()

    each(tiles, wait)


def encode_far(m, high, low, acc, square, mask, gain, w_gate, w_up):
    half, part = high.shape
    rows = 2 * half
    width, ff = w_gate.shape
    tiles = ff // FT
    return pl.pallas_call(
        encode_far_kernel,
        in_specs=[smem] + [anywhere] * 3 + [vmem] * 3 + [anywhere] * 2,
        out_specs=[anywhere] * 3 + [vmem] * 2,
        out_shape=[pltpu.HBM((rows, ff), bf16)] * 3
        + [
            jax.ShapeDtypeStruct((tiles, rows // L, FT), f32),
            jax.ShapeDtypeStruct((rows, 1), f32),
        ],
        scratch_shapes=[
            pltpu.VMEM((rows, part), bf16),
            pltpu.VMEM((rows, part), bf16),
            pltpu.VMEM((tiles, part, 2 * FT), bf16),
            pltpu.VMEM((tiles, rows, 2 * FT), f32),
            pltpu.VMEM((tiles, 3, rows, FT), bf16),
            pltpu.SemaphoreType.DMA((2,)),
            pltpu.SemaphoreType.DMA((tiles, 2)),
            pltpu.SemaphoreType.DMA((tiles,)),
            pltpu.SemaphoreType.DMA((tiles, 3)),
        ],
        compiler_params=pltpu.CompilerParams(vmem_limit_bytes=SCOPED),
        cost_estimate=pl.CostEstimate(
            flops=rows * width * ff, transcendentals=rows * ff, bytes_accessed=6 * rows * ff
        ),
        name="encode_far",
    )(m, *map(in_hbm, (high, low, acc)), square, mask, gain, in_hbm(w_gate), in_hbm(w_up))


def load_weights(m, steps, wg_ref, wu_ref, w, sem):
    part, ff = w.shape[1], wg_ref.shape[1]
    copies = []
    for k, step in enumerate(steps):
        at = pl.multiple_of(lax.rem(m + step, MP) * part, part)
        for i, ref in enumerate((wg_ref, wu_ref)):
            copies.append(
                pltpu.make_async_copy(
                    ref.at[pl.ds(at, part)], w.at[k, :, pl.ds(i * ff, ff)], sem.at[k, i]
                )
            )
    return copies


def back_kernel(steps, first, m_ref, a_ref, b_ref, c_ref, g_in, gs_ref, wg_ref, wu_ref, *refs):
    if first:
        wd_ref, *refs = refs
    count = 2 if first else len(steps)
    outs = refs[:count]
    last = not first and len(steps) == 1
    if first:
        g_ref, ab, w, in_sem, w_sem = refs[count:]
    elif last:
        s_ref, c, ab, w, in_sem, w_sem = refs[count:]
    else:
        ab, w, in_sem, w_sem = refs[count:]
    part = outs[0].shape[1]
    ff = a_ref.shape[1]
    tiles, rt, _ = ab.shape
    here = tiles // 2 if first else tiles
    weights = load_weights(m_ref[0], steps, wg_ref, wu_ref, w, w_sem)
    passes = g_in.shape[0]

    def arriving(r):
        at = pl.ds(pl.multiple_of(r * rt, rt), rt)
        copies = [
            pltpu.make_async_copy(ref.at[at], ab.at[r, :, pl.ds(i * ff, ff)], in_sem.at[r, i])
            for i, ref in enumerate((a_ref, b_ref))
        ]
        if last:
            copies.append(pltpu.make_async_copy(c_ref.at[at], c.at[r], in_sem.at[r, 2]))
        return copies

    for copy in arriving(0) + weights[:2]:
        copy.start()
    for r in range(1, tiles):
        for copy in arriving(r):
            copy.start()
    for copy in weights[2:]:
        copy.start()

    if first:

        def dact_tile(n):
            at = pl.ds(pl.multiple_of(n * FT, FT), FT)
            g_ref[:, at] = contract_rows(wd_ref[at], g_in[...]).T

        each(ff // FT, dact_tile)
        source = g_ref
    else:
        source = g_in

    def scale(r):
        for copy in arriving(r):
            copy.wait()
        lane = lax.broadcasted_iota(jnp.int32, (L, 2 * passes), 1)
        for p in range(rt // L):
            at = slice(p * L, (p + 1) * L)
            q = r * (rt // L) + p
            dact = source[pl.ds(q, 1)].astype(bf16)
            ab[r, at, :ff] = dact * ab[r, at, :ff]
            ab[r, at, ff:] = dact * ab[r, at, ff:]
            if last:
                sums = contract_rows(c[r, at], gs_ref[...])
                mine = (lane == q) | (lane == q + passes)
                s_ref[pl.ds(pl.multiple_of(q * L, L), L)] = jnp.sum(
                    jnp.where(mine, sums, 0.0), axis=1, keepdims=True
                )

    def multiply(j):
        k, r = j // tiles, lax.rem(j, tiles)

        @pl.when(k == 0)
        def _():
            scale(r)

        @pl.when(r == 0)
        def _():
            for i in range(2):
                pltpu.make_async_copy(
                    wg_ref.at[pl.ds(0, part)], w.at[k, :, pl.ds(i * ff, ff)], w_sem.at[k, i]
                ).wait()

        out = contract_rows(ab[r], w[k]).astype(bf16)
        at = pl.ds(pl.multiple_of(lax.rem(j, here) * rt, rt), rt)
        for i, ref in enumerate(outs):

            @pl.when(j // here == i)
            def _():
                ref[at] = out

    each(len(steps) * tiles, multiply)


def back(m, steps, rt, first, a, b, c, g, gs, w_gate, w_up, w_down):
    rows, ff = a.shape
    width = w_gate.shape[0]
    part = width // MP
    tiles = rows // rt
    last = not first and len(steps) == 1
    outs = [pltpu.HBM((rows // 2, part), bf16)] * 2
    if not first:
        outs = [pltpu.HBM((rows, part), bf16)] * len(steps)
    more = []
    scratch = []
    if first:
        more = [jax.ShapeDtypeStruct((g.shape[0], ff), f32)]
    elif last:
        more = [jax.ShapeDtypeStruct((rows, 1), f32)]
        scratch = [pltpu.VMEM((tiles, rt, ff), bf16)]
    return pl.pallas_call(
        functools.partial(back_kernel, steps, first),
        in_specs=[smem] + [anywhere] * 3 + [vmem] * 2 + [anywhere] * 2 + [vmem] * first,
        out_specs=[vmem] * (len(outs) + len(more)),
        out_shape=outs + more,
        scratch_shapes=scratch
        + [
            pltpu.VMEM((tiles, rt, 2 * ff), bf16),
            pltpu.VMEM((len(steps), part, 2 * ff), bf16),
            pltpu.SemaphoreType.DMA((tiles, 3)),
            pltpu.SemaphoreType.DMA((len(steps), 2)),
        ],
        compiler_params=pltpu.CompilerParams(vmem_limit_bytes=SCOPED),
        cost_estimate=pl.CostEstimate(flops=1, transcendentals=0, bytes_accessed=1),
        name="back",
    )(m, *map(in_hbm, (a, b, c)), g, gs, in_hbm(w_gate), in_hbm(w_up), *([w_down] if first else []))


def finish_kernel(
    x_ref, own_ref, one_ref, two_ref, rms_ref, inner_ref, mask_ref, token_ref, gain_ref, out_ref
):
    rms = rms_ref[...]
    eye = lax.broadcasted_iota(jnp.int32, (L, L), 0) == lax.broadcasted_iota(jnp.int32, (L, L), 1)
    inner = jnp.concatenate(
        [
            jnp.sum(jnp.where(eye, inner_ref[0, p : p + 1], 0.0), axis=1, keepdims=True)
            for p in range(out_ref.shape[0] // L)
        ],
        axis=0,
    )
    normed = own_ref[...].astype(f32) + one_ref[...].astype(f32) + two_ref[...].astype(f32)
    grad = rms * gain_ref[...] * normed - x_ref[...].astype(f32) * (rms * rms * inner)
    mask = mask_ref[...]
    for p in range(out_ref.shape[0] // L):
        part = slice(p * L, (p + 1) * L)
        out_ref[part] = (grad[part] + mask[part] * token_ref[0, p : p + 1]).astype(bf16)


def finish(x, own, one, two, rms, inner, mask, token, gain):
    rows, part = x.shape
    rt = 256
    whole = pl.BlockSpec((rt, part), lambda r: (r, 0))
    column = pl.BlockSpec((rt, 1), lambda r: (r, 0))
    return pl.pallas_call(
        finish_kernel,
        grid=(rows // rt,),
        in_specs=[
            whole,
            whole,
            whole,
            whole,
            column,
            pl.BlockSpec((1, rt // L, L), lambda r: (r, 0, 0)),
            column,
            pl.BlockSpec((1, rt // L, part), lambda r: (r, 0, 0)),
            pl.BlockSpec((1, part), lambda r: (0, 0)),
        ],
        out_specs=whole,
        out_shape=jax.ShapeDtypeStruct(x.shape, bf16),
        compiler_params=pltpu.CompilerParams(vmem_limit_bytes=16 << 20),
        name="finish",
    )(*map(in_hbm, (x, own, one, two)), rms, inner, mask, token.reshape(-1, rt // L, part), gain)


def per_device(
    hidden_in, token_ids, passage_counts, positive_doc, queries, norm_gain, w_gate, w_up, w_down
):
    row_count, part = hidden_in.shape
    width = norm_gain.shape[0]
    docs = passage_counts.shape[0]
    passes = row_count // L
    most = passes // docs
    share = queries.shape[0] // MP
    chips = lax.axis_size(("x", "z"))
    cores = lax.axis_size("core")
    mi = lax.axis_index("mp")
    core = lax.axis_index("core")
    chip = lax.axis_index(("x", "z"))
    m = mi.astype(jnp.int32).reshape(1)

    mine = lax.all_to_all(
        queries.reshape(MP, share, part), "mp", split_axis=0, concat_axis=0, tiled=True
    )
    mine = jnp.moveaxis(mine, 0, 1).reshape(share, width)
    own_positive = lax.dynamic_slice_in_dim(positive_doc, mi * share, share)
    square = jnp.sum(mine.astype(f32) ** 2, axis=1)
    square_high = square.astype(bf16)
    square_low = (square - square_high.astype(f32)).astype(bf16)
    extra = jnp.stack([own_positive.astype(bf16), square_high, square_low], axis=1)
    extra = jnp.pad(extra, ((0, 0), (0, L - 3)))
    sent = jnp.concatenate([mine, extra], axis=1)

    right, left = shifted(hidden_in, -1), shifted(hidden_in, 1)
    right, left, sent = lax.optimization_barrier((right, left, sent))
    half = row_count // 2
    high, low = shifted(left[:half], 1), shifted(right[half:], -1)
    all_q = lax.all_gather(sent, ("x", "z"), axis=0)

    live_pass = jnp.arange(passes, dtype=jnp.int32) % most < jnp.repeat(passage_counts, most)
    other_live = swapped(live_pass.astype(jnp.int32)) > 0
    live = jnp.where(
        core == 0,
        jnp.concatenate([live_pass, other_live]),
        jnp.concatenate([other_live, live_pass]),
    ).astype(f32)[:, None]
    token_live = (token_ids.reshape(passes, L) != pad_token) & live_pass[:, None]
    live_float = token_live.astype(f32)
    mask = live_float.reshape(row_count, 1)
    divisor = jnp.maximum(jnp.sum(live_float, axis=1), 1.0)[:, None]
    gain = norm_gain.reshape(MP, 1, part)

    weights = (gain, w_gate, w_up)
    acc, square, own_x = encode_near(m, hidden_in, right, left, mask, *weights)
    a, b, c, pool, rms = encode_far(m, high, low, acc, square, mask, *weights)
    pool = jnp.moveaxis(pool, 0, 1).reshape(passes, -1)

    high = pool.astype(bf16)
    low = (pool - high.astype(f32)).astype(bf16)
    branch = jnp.dot(jnp.concatenate([high, low], 0), w_down, preferred_element_type=f32)
    own_x = (jnp.arange(MP) == mi)[None, :, None].astype(f32) * own_x[:, None, :]
    summed = (branch[:passes] + branch[passes:] + own_x.reshape(passes, width)) / divisor
    summed = copies_to_all(summed.astype(bf16), ("core", "mp"), cores * MP)
    summed = summed.reshape(cores, MP, passes, width).astype(f32).sum(axis=1)
    vecs = summed.reshape(cores * passes, width).astype(bf16)
    vec_float = vecs.astype(f32)
    vec_scale = lax.rsqrt(jnp.sum(vec_float * vec_float, axis=1, keepdims=True) + unit_epsilon)

    all_q = all_q.reshape(chips * share, width + L)
    q = all_q[:, :width]
    extra = all_q[:, width:].astype(f32)
    positive = extra[:, 0]
    query_scale = lax.rsqrt(extra[:, 1] + extra[:, 2] + unit_epsilon)
    raw = contract_rows(vecs, q)
    weights = live * jnp.exp(score_scale * raw * query_scale[None, :] * vec_scale)
    k = jnp.arange(cores * passes, dtype=jnp.int32)
    doc = chip * (cores * docs) + k // most
    hit = (positive[None, :] == doc.astype(f32)[:, None]).astype(f32)
    mass = jnp.stack([jnp.sum(weights, axis=0), jnp.sum(weights * hit, axis=0)])
    mass = copies_to_all(mass.reshape(8, -1), ("x", "z"), chips).sum(axis=0).reshape(2, -1)
    total, held = mass[0], mass[1]
    loss = jnp.log(total) - jnp.log(held)
    own_loss = lax.dynamic_slice_in_dim(loss, chip * share, share)

    coef = (loss_seed * score_scale) * query_scale[None, :] * (
        weights / total[None, :] - hit * weights / held[None, :]
    )
    grad = jnp.dot(coef.astype(bf16), q, preferred_element_type=f32)
    term = jnp.sum(coef * raw, axis=1, keepdims=True)
    grad = jnp.concatenate([grad, jnp.broadcast_to(term, (cores * passes, L))], axis=1).astype(bf16)
    grad = jnp.broadcast_to(
        grad.reshape(cores, 1, passes, width + L), (cores, MP, passes, width + L)
    ).reshape(cores * MP, passes, width + L)
    grad = lax.all_to_all(grad, ("core", "mp"), split_axis=0, concat_axis=0, tiled=True)
    grad = grad.astype(f32).sum(axis=0)
    own_vec = lax.dynamic_slice_in_dim(vec_float, core * passes, passes)
    scale = lax.dynamic_slice_in_dim(vec_scale, core * passes, passes)
    change = scale * grad[:, :width] - own_vec * (scale**3 * grad[:, width : width + 1])
    token_grad = (change / divisor).astype(bf16)

    tensors = (w_gate, w_up, w_down)
    none = jnp.zeros((2 * passes, pool.shape[1]), bf16)
    high, low, g = back(m, (2,), 256, True, a, b, c, token_grad, none, *tensors)
    from_right = shifted(high, -1)
    from_left = shifted(low, 1)
    right, left = back(m, (1, 3), 512, False, a, b, c, g, none, *tensors)
    right = right.at[half:].set((right[half:].astype(f32) + from_left.astype(f32)).astype(bf16))
    left = left.at[:half].set((left[:half].astype(f32) + from_right.astype(f32)).astype(bf16))
    right, left, g = lax.optimization_barrier((right, left, g))
    right = shifted(right, 1)
    left = shifted(left, -1)
    g_high = g.astype(bf16)
    gs = jnp.concatenate([g_high, (g - g_high.astype(f32)).astype(bf16)], axis=0)
    own, s = back(m, (0,), 512, False, a, b, c, g, gs, *tensors)
    small = jnp.concatenate(
        [s.reshape(passes, L), jnp.pad(own_loss[None, :], ((0, 7), (0, L - share)))], axis=0
    )
    small = copies_to_all(small, "mp", MP)
    inner = small[:, :passes].sum(axis=0).reshape(passes // 2, 2, L) / width
    query_loss = small[:, passes, :share].reshape(MP * share)
    own_gain = lax.dynamic_slice_in_dim(norm_gain, mi * part, part)[None, :]
    own_token = lax.dynamic_slice_in_dim(token_grad, mi * part, part, axis=1).astype(f32)
    rest = (rms, inner, mask, own_token, own_gain)
    hidden_grad = finish(hidden_in, own, right, left, *rest)
    return query_loss, hidden_grad


def solution(mesh):
    shape = (4, 4, 2, MP)
    split = Mesh(mesh.devices.reshape(shape), ("x", "z", "core", "mp"))
    dp = ("x", "z", "core")
    return jax.shard_map(
        per_device,
        mesh=split,
        in_specs=(
            P(dp, "mp"),
            P(dp),
            P(dp),
            P(dp),
            P(dp, "mp"),
            P(),
            P(None, "mp"),
            P(None, "mp"),
            P("mp", None),
        ),
        out_specs=(P(dp), P(dp, "mp")),
        check_vma=False,
    )
```

```python
import functools

import jax
import jax.numpy as jnp
from jax import lax
from jax.experimental import pallas as pl
from jax.experimental.pallas import tpu as pltpu
from jax.sharding import Mesh, PartitionSpec as P

L = 128
pad_token = 128001
score_scale = 20.0
loss_seed = 4096.0
norm_epsilon = 1e-05
unit_epsilon = 1e-06
MP = 4
FT = 256
SCOPED = 40 << 20
bf16 = jnp.bfloat16
f32 = jnp.float32


def shifted(x, by):
    return lax.ppermute(x, "mp", [(i, (i + by) % MP) for i in range(MP)])


def across(left, right):
    half = left.shape[0] // 2
    return shifted(left[:half], 1), shifted(right[half:], -1)


def swapped(x):
    return lax.ppermute(x, "core", [(0, 1), (1, 0)])


def copies_to_all(x, axes, count):
    return lax.all_to_all(
        jnp.broadcast_to(x, (count, *x.shape)), axes, split_axis=0, concat_axis=0, tiled=True
    )


def in_hbm(x):
    return pltpu.with_memory_space_constraint(x, pltpu.HBM)


def contract_rows(left, right):
    return lax.dot_general(
        left, right, (((1,), (1,)), ((), ())), preferred_element_type=f32
    )


def each(count, body):
    def step(n, carry):
        body(n)
        return carry

    lax.fori_loop(0, count, step, 0)


anywhere = pl.BlockSpec(memory_space=pl.ANY)
vmem = pl.BlockSpec(memory_space=pltpu.VMEM)
smem = pl.BlockSpec(memory_space=pltpu.SMEM)


def loop_copies(copies, count):
    def start(n):
        for copy in copies(n):
            copy.start()

    each(count, start)


def weight_tiles(m, steps, part, wg_ref, wu_ref, w, sem):
    def copies(n):
        columns = pl.ds(pl.multiple_of(n * FT, FT), FT)
        return [
            pltpu.make_async_copy(
                ref.at[pl.ds(pl.multiple_of(lax.rem(m + step, MP) * part, part), part), columns],
                w.at[n, pl.ds(k * part, part), pl.ds(i * FT, FT)],
                sem.at[n, 2 * k + i],
            )
            for k, step in enumerate(steps)
            for i, ref in enumerate((wg_ref, wu_ref))
        ]

    return copies


def encode_near_kernel(steps, m_ref, *refs):
    count = len(steps)
    pieces, (gain_ref, wg_ref, wu_ref), refs = refs[:count], refs[count : count + 3], refs[count + 3 :]
    own = count == 1
    if own:
        mask_ref, acc_out, square_ref, xpool_ref = refs[:4]
        xin, xs, w, acc, in_sem, w_sem, out_sem = refs[4:]
    else:
        acc_in, square_in, acc_out, square_ref = refs[:4]
        xin, xs, w, acc, in_sem, w_sem, out_sem, acc_sem = refs[4:]
    rows, part = pieces[0].shape
    tiles = w.shape[0]
    m = m_ref[0]
    arriving = [pltpu.make_async_copy(ref, xin.at[k], in_sem.at[k]) for k, ref in enumerate(pieces)]
    for copy in arriving:
        copy.start()
    weights = weight_tiles(m, steps, part, wg_ref, wu_ref, w, w_sem)

    def inputs(n):
        more = [] if own else [pltpu.make_async_copy(acc_in.at[n], acc.at[n], acc_sem.at[n])]
        return weights(n) + more

    loop_copies(inputs, tiles)
    for copy in arriving:
        copy.wait()

    def scale(p):
        at = pl.ds(pl.multiple_of(p * L, L), L)
        total = None if own else square_in[at]
        for k, step in enumerate(steps):
            v = xin[k, at].astype(f32)
            square = jnp.sum(v * v, axis=1, keepdims=True)
            total = square if total is None else total + square
            xs[at, k * part : (k + 1) * part] = (v * gain_ref[lax.rem(m + step, MP)]).astype(bf16)
            if own:
                xpool_ref[pl.ds(p, 1)] = jnp.sum(v * mask_ref[at], axis=0, keepdims=True)
        square_ref[at] = total

    each(rows // L, scale)

    def leaving(n):
        return pltpu.make_async_copy(acc.at[n], acc_out.at[n], out_sem.at[n])

    def multiply(n):
        for copy in inputs(n):
            copy.wait()
        product = jnp.dot(xs[...], w[n], preferred_element_type=f32)
        acc[n] = product if own else acc[n] + product
        leaving(n).start()

    each(tiles, multiply)
    each(tiles, lambda n: leaving(n).wait())


def encode_near(m, steps, pieces, gain, w_gate, w_up, *rest):
    own = len(steps) == 1
    rows, part = pieces[0].shape
    width, ff = w_gate.shape
    tiles = ff // FT
    count = len(steps)
    rest = rest if own else (in_hbm(rest[0]), rest[1])
    return pl.pallas_call(
        functools.partial(encode_near_kernel, steps),
        in_specs=[smem]
        + [anywhere] * count
        + [vmem, anywhere, anywhere]
        + ([vmem] if own else [anywhere, vmem]),
        out_specs=[anywhere, vmem] + [vmem] * own,
        out_shape=[
            pltpu.HBM((tiles, rows, 2 * FT), f32),
            jax.ShapeDtypeStruct((rows, 1), f32),
        ]
        + [jax.ShapeDtypeStruct((rows // L, part), f32)] * own,
        scratch_shapes=[
            pltpu.VMEM((count, rows, part), bf16),
            pltpu.VMEM((rows, count * part), bf16),
            pltpu.VMEM((tiles, count * part, 2 * FT), bf16),
            pltpu.VMEM((tiles, rows, 2 * FT), f32),
            pltpu.SemaphoreType.DMA((count,)),
            pltpu.SemaphoreType.DMA((tiles, 2 * count)),
            pltpu.SemaphoreType.DMA((tiles,)),
        ]
        + [pltpu.SemaphoreType.DMA((tiles,))] * (not own),
        compiler_params=pltpu.CompilerParams(vmem_limit_bytes=SCOPED),
        cost_estimate=pl.CostEstimate(
            flops=count * rows * width * ff, transcendentals=0, bytes_accessed=4 * rows * width
        ),
        name="encode_near",
    )(m, *map(in_hbm, pieces), gain, in_hbm(w_gate), in_hbm(w_up), *rest)


def encode_far_kernel(
    m_ref, high_ref, low_ref, acc_ref, square_ref, mask_ref, gain_ref, wg_ref, wu_ref,
    a_out, b_out, c_out, pool_ref, rms_ref, xin, xs, w, acc, results, in_sem, w_sem, acc_sem, out_sem,
):
    rows, part = xin.shape
    half = rows // 2
    tiles = w.shape[0]
    m = m_ref[0]
    arriving = [
        pltpu.make_async_copy(ref, xin.at[pl.ds(k * half, half)], in_sem.at[k])
        for k, ref in enumerate((high_ref, low_ref))
    ]
    for copy in arriving:
        copy.start()
    weights = weight_tiles(m, (2,), part, wg_ref, wu_ref, w, w_sem)

    def inputs(n):
        return [*weights(n), pltpu.make_async_copy(acc_ref.at[n], acc.at[n], acc_sem.at[n])]

    loop_copies(inputs, tiles)
    for copy in arriving:
        copy.wait()

    def scale(p):
        at = pl.ds(pl.multiple_of(p * L, L), L)
        v = xin[at].astype(f32)
        total = square_ref[at] + jnp.sum(v * v, axis=1, keepdims=True)
        rms_ref[at] = lax.rsqrt(total / (MP * part) + norm_epsilon)
        xs[at] = (v * gain_ref[lax.rem(m + 2, MP)]).astype(bf16)

    each(rows // L, scale)

    def leaving(n):
        return [
            pltpu.make_async_copy(
                results.at[n, i],
                out.at[:, pl.ds(pl.multiple_of(n * FT, FT), FT)],
                out_sem.at[n, i],
            )
            for i, out in enumerate((a_out, b_out, c_out))
        ]

    def multiply(n):
        for copy in inputs(n):
            copy.wait()
        for r in range(2):
            at = slice(r * half, (r + 1) * half)
            both = acc[n, at] + jnp.dot(xs[at], w[n], preferred_element_type=f32)
            both *= rms_ref[at]
            gate, up = both[:, :FT], both[:, FT:]
            mask = mask_ref[at]
            sig = jax.nn.sigmoid(gate)
            up = up * mask
            b = gate * sig
            bu = b * up
            act = bu.astype(bf16).astype(f32)
            for p in range(half // L):
                q = r * (half // L) + p
                pool_ref[n, q : q + 1] = jnp.sum(act[p * L : (p + 1) * L], axis=0, keepdims=True)
            a = up * (sig + b * (1.0 - sig))
            results[n, 0, at] = a.astype(bf16)
            results[n, 1, at] = (b * mask).astype(bf16)
            results[n, 2, at] = (a * gate + bu).astype(bf16)
        for copy in leaving(n):
            copy.start()

    each(tiles, multiply)

    def wait(n):
        for copy in leaving(n):
            copy.wait()

    each(tiles, wait)


def encode_far(m, high, low, acc, square, mask, gain, w_gate, w_up):
    half, part = high.shape
    rows = 2 * half
    width, ff = w_gate.shape
    tiles = ff // FT
    return pl.pallas_call(
        encode_far_kernel,
        in_specs=[smem] + [anywhere] * 3 + [vmem] * 3 + [anywhere] * 2,
        out_specs=[anywhere] * 3 + [vmem] * 2,
        out_shape=[pltpu.HBM((rows, ff), bf16)] * 3
        + [
            jax.ShapeDtypeStruct((tiles, rows // L, FT), f32),
            jax.ShapeDtypeStruct((rows, 1), f32),
        ],
        scratch_shapes=[
            pltpu.VMEM((rows, part), bf16),
            pltpu.VMEM((rows, part), bf16),
            pltpu.VMEM((tiles, part, 2 * FT), bf16),
            pltpu.VMEM((tiles, rows, 2 * FT), f32),
            pltpu.VMEM((tiles, 3, rows, FT), bf16),
            pltpu.SemaphoreType.DMA((2,)),
            pltpu.SemaphoreType.DMA((tiles, 2)),
            pltpu.SemaphoreType.DMA((tiles,)),
            pltpu.SemaphoreType.DMA((tiles, 3)),
        ],
        compiler_params=pltpu.CompilerParams(vmem_limit_bytes=SCOPED),
        cost_estimate=pl.CostEstimate(
            flops=rows * width * ff, transcendentals=rows * ff, bytes_accessed=6 * rows * ff
        ),
        name="encode_far",
    )(m, *map(in_hbm, (high, low, acc)), square, mask, gain, in_hbm(w_gate), in_hbm(w_up))


def load_weights(m, steps, wg_ref, wu_ref, w, sem):
    part, ff = w.shape[1], wg_ref.shape[1]
    copies = []
    for k, step in enumerate(steps):
        at = pl.multiple_of(lax.rem(m + step, MP) * part, part)
        for i, ref in enumerate((wg_ref, wu_ref)):
            copies.append(
                pltpu.make_async_copy(
                    ref.at[pl.ds(at, part)], w.at[k, :, pl.ds(i * ff, ff)], sem.at[k, i]
                )
            )
    return copies


def back_kernel(steps, first, m_ref, a_ref, b_ref, c_ref, g_in, gs_ref, wg_ref, wu_ref, *refs):
    if first:
        wd_ref, *refs = refs
    count = 2 if first else len(steps)
    outs = refs[:count]
    last = not first and len(steps) == 1
    if first:
        g_ref, ab, w, in_sem, w_sem = refs[count:]
    elif last:
        s_ref, c, ab, w, in_sem, w_sem = refs[count:]
    else:
        ab, w, in_sem, w_sem = refs[count:]
    part = outs[0].shape[1]
    ff = a_ref.shape[1]
    tiles, rt, _ = ab.shape
    here = tiles // 2 if first else tiles
    weights = load_weights(m_ref[0], steps, wg_ref, wu_ref, w, w_sem)
    passes = g_in.shape[0]

    def arriving(r):
        at = pl.ds(pl.multiple_of(r * rt, rt), rt)
        copies = [
            pltpu.make_async_copy(ref.at[at], ab.at[r, :, pl.ds(i * ff, ff)], in_sem.at[r, i])
            for i, ref in enumerate((a_ref, b_ref))
        ]
        if last:
            copies.append(pltpu.make_async_copy(c_ref.at[at], c.at[r], in_sem.at[r, 2]))
        return copies

    for copy in arriving(0) + weights[:2]:
        copy.start()
    for r in range(1, tiles):
        for copy in arriving(r):
            copy.start()
    for copy in weights[2:]:
        copy.start()

    if first:

        def dact_tile(n):
            at = pl.ds(pl.multiple_of(n * FT, FT), FT)
            g_ref[:, at] = contract_rows(wd_ref[at], g_in[...]).T

        each(ff // FT, dact_tile)
        source = g_ref
    else:
        source = g_in

    def scale(r):
        for copy in arriving(r):
            copy.wait()
        lane = lax.broadcasted_iota(jnp.int32, (L, 2 * passes), 1)
        for p in range(rt // L):
            at = slice(p * L, (p + 1) * L)
            q = r * (rt // L) + p
            dact = source[pl.ds(q, 1)].astype(bf16)
            ab[r, at, :ff] = dact * ab[r, at, :ff]
            ab[r, at, ff:] = dact * ab[r, at, ff:]
            if last:
                sums = contract_rows(c[r, at], gs_ref[...])
                mine = (lane == q) | (lane == q + passes)
                s_ref[pl.ds(pl.multiple_of(q * L, L), L)] = jnp.sum(
                    jnp.where(mine, sums, 0.0), axis=1, keepdims=True
                )

    def multiply(j):
        k, r = j // tiles, lax.rem(j, tiles)

        @pl.when(k == 0)
        def _():
            scale(r)

        @pl.when(r == 0)
        def _():
            for i in range(2):
                pltpu.make_async_copy(
                    wg_ref.at[pl.ds(0, part)], w.at[k, :, pl.ds(i * ff, ff)], w_sem.at[k, i]
                ).wait()

        out = contract_rows(ab[r], w[k]).astype(bf16)
        at = pl.ds(pl.multiple_of(lax.rem(j, here) * rt, rt), rt)
        for i, ref in enumerate(outs):

            @pl.when(j // here == i)
            def _():
                ref[at] = out

    each(len(steps) * tiles, multiply)


def back(m, steps, rt, first, a, b, c, g, gs, w_gate, w_up, w_down):
    rows, ff = a.shape
    width = w_gate.shape[0]
    part = width // MP
    tiles = rows // rt
    last = not first and len(steps) == 1
    outs = [pltpu.HBM((rows // 2, part), bf16)] * 2
    if not first:
        outs = [pltpu.HBM((rows, part), bf16)] * len(steps)
    more = []
    scratch = []
    if first:
        more = [jax.ShapeDtypeStruct((g.shape[0], ff), f32)]
    elif last:
        more = [jax.ShapeDtypeStruct((rows, 1), f32)]
        scratch = [pltpu.VMEM((tiles, rt, ff), bf16)]
    return pl.pallas_call(
        functools.partial(back_kernel, steps, first),
        in_specs=[smem] + [anywhere] * 3 + [vmem] * 2 + [anywhere] * 2 + [vmem] * first,
        out_specs=[vmem] * (len(outs) + len(more)),
        out_shape=outs + more,
        scratch_shapes=scratch
        + [
            pltpu.VMEM((tiles, rt, 2 * ff), bf16),
            pltpu.VMEM((len(steps), part, 2 * ff), bf16),
            pltpu.SemaphoreType.DMA((tiles, 3)),
            pltpu.SemaphoreType.DMA((len(steps), 2)),
        ],
        compiler_params=pltpu.CompilerParams(vmem_limit_bytes=SCOPED),
        cost_estimate=pl.CostEstimate(flops=1, transcendentals=0, bytes_accessed=1),
        name="back",
    )(m, *map(in_hbm, (a, b, c)), g, gs, in_hbm(w_gate), in_hbm(w_up), *([w_down] if first else []))


def add_kernel(right_ref, left_ref, from_left_ref, from_right_ref, right_out, left_out):
    right_out[...] = (right_ref[...].astype(f32) + from_left_ref[...].astype(f32)).astype(bf16)
    left_out[...] = (left_ref[...].astype(f32) + from_right_ref[...].astype(f32)).astype(bf16)


def add_halves(right, left, from_left, from_right):
    half, part = from_left.shape
    rt = half // 2
    upper = pl.BlockSpec((rt, part), lambda r: (r, 0))
    lower = pl.BlockSpec((rt, part), lambda r: (r + 2, 0))
    return pl.pallas_call(
        add_kernel,
        grid=(2,),
        in_specs=[lower, upper, upper, upper],
        out_specs=[lower, upper],
        out_shape=[pltpu.HBM(right.shape, bf16)] * 2,
        input_output_aliases={0: 0, 1: 1},
        compiler_params=pltpu.CompilerParams(vmem_limit_bytes=8 << 20),
        cost_estimate=pl.CostEstimate(flops=1, transcendentals=0, bytes_accessed=1),
        name="add_halves",
    )(in_hbm(right), in_hbm(left), from_left, from_right)


def finish_kernel(
    x_ref, own_ref, one_ref, two_ref, rms_ref, inner_ref, mask_ref, token_ref, gain_ref, out_ref
):
    rms = rms_ref[...]
    eye = lax.broadcasted_iota(jnp.int32, (L, L), 0) == lax.broadcasted_iota(jnp.int32, (L, L), 1)
    inner = jnp.concatenate(
        [
            jnp.sum(jnp.where(eye, inner_ref[0, p : p + 1], 0.0), axis=1, keepdims=True)
            for p in range(out_ref.shape[0] // L)
        ],
        axis=0,
    )
    normed = own_ref[...].astype(f32) + one_ref[...].astype(f32) + two_ref[...].astype(f32)
    grad = rms * gain_ref[...] * normed - x_ref[...].astype(f32) * (rms * rms * inner)
    mask = mask_ref[...]
    for p in range(out_ref.shape[0] // L):
        part = slice(p * L, (p + 1) * L)
        out_ref[part] = (grad[part] + mask[part] * token_ref[0, p : p + 1]).astype(bf16)


def finish(x, own, one, two, rms, inner, mask, token, gain):
    rows, part = x.shape
    rt = 256
    whole = pl.BlockSpec((rt, part), lambda r: (r, 0))
    column = pl.BlockSpec((rt, 1), lambda r: (r, 0))
    return pl.pallas_call(
        finish_kernel,
        grid=(rows // rt,),
        in_specs=[
            whole,
            whole,
            whole,
            whole,
            column,
            pl.BlockSpec((1, rt // L, L), lambda r: (r, 0, 0)),
            column,
            pl.BlockSpec((1, rt // L, part), lambda r: (r, 0, 0)),
            pl.BlockSpec((1, part), lambda r: (0, 0)),
        ],
        out_specs=whole,
        out_shape=jax.ShapeDtypeStruct(x.shape, bf16),
        compiler_params=pltpu.CompilerParams(vmem_limit_bytes=16 << 20),
        name="finish",
    )(in_hbm(x), in_hbm(own), one, two, rms, inner, mask, token.reshape(-1, rt // L, part), gain)


def per_device(
    hidden_in, token_ids, passage_counts, positive_doc, queries, norm_gain, w_gate, w_up, w_down
):
    row_count, part = hidden_in.shape
    width = norm_gain.shape[0]
    docs = passage_counts.shape[0]
    passes = row_count // L
    most = passes // docs
    share = queries.shape[0] // MP
    chips = lax.axis_size(("x", "z"))
    cores = lax.axis_size("core")
    mi = lax.axis_index("mp")
    core = lax.axis_index("core")
    chip = lax.axis_index(("x", "z"))
    m = mi.astype(jnp.int32).reshape(1)

    mine = lax.all_to_all(
        queries.reshape(MP, share, part), "mp", split_axis=0, concat_axis=0, tiled=True
    )
    mine = jnp.moveaxis(mine, 0, 1).reshape(share, width)
    own_positive = lax.dynamic_slice_in_dim(positive_doc, mi * share, share)
    square = jnp.sum(mine.astype(f32) ** 2, axis=1)
    square_high = square.astype(bf16)
    square_low = (square - square_high.astype(f32)).astype(bf16)
    extra = jnp.stack([own_positive.astype(bf16), square_high, square_low], axis=1)
    extra = jnp.pad(extra, ((0, 0), (0, L - 3)))
    sent = jnp.concatenate([mine, extra], axis=1)

    right, left = shifted(hidden_in, -1), shifted(hidden_in, 1)
    live_pass = jnp.arange(passes, dtype=jnp.int32) % most < jnp.repeat(passage_counts, most)
    token_live = (token_ids.reshape(passes, L) != pad_token) & live_pass[:, None]
    live_float = token_live.astype(f32)
    mask = live_float.reshape(row_count, 1)
    weights = (norm_gain.reshape(MP, 1, part), w_gate, w_up)
    acc, square, own_x = encode_near(m, (0,), (hidden_in,), *weights, mask)
    right, left, sent, acc = lax.optimization_barrier((right, left, sent, acc))
    half = row_count // 2
    high, low = shifted(left[:half], 1), shifted(right[half:], -1)
    all_q = lax.all_gather(sent, ("x", "z"), axis=0)

    other_live = swapped(live_pass.astype(jnp.int32)) > 0
    live = jnp.where(
        core == 0,
        jnp.concatenate([live_pass, other_live]),
        jnp.concatenate([other_live, live_pass]),
    ).astype(f32)[:, None]
    divisor = jnp.maximum(jnp.sum(live_float, axis=1), 1.0)[:, None]

    acc, square = encode_near(m, (1, 3), (right, left), *weights, acc, square)
    a, b, c, pool, rms = encode_far(m, high, low, acc, square, mask, *weights)
    pool = jnp.moveaxis(pool, 0, 1).reshape(passes, -1)

    high = pool.astype(bf16)
    low = (pool - high.astype(f32)).astype(bf16)
    branch = jnp.dot(jnp.concatenate([high, low], 0), w_down, preferred_element_type=f32)
    own_x = (jnp.arange(MP) == mi)[None, :, None].astype(f32) * own_x[:, None, :]
    summed = (branch[:passes] + branch[passes:] + own_x.reshape(passes, width)) / divisor
    summed = copies_to_all(summed.astype(bf16), ("core", "mp"), cores * MP)
    summed = summed.reshape(cores, MP, passes, width).astype(f32).sum(axis=1)
    vecs = summed.reshape(cores * passes, width).astype(bf16)
    vec_float = vecs.astype(f32)
    vec_scale = lax.rsqrt(jnp.sum(vec_float * vec_float, axis=1, keepdims=True) + unit_epsilon)

    all_q = all_q.reshape(chips * share, width + L)
    q = all_q[:, :width]
    extra = all_q[:, width:].astype(f32)
    positive = extra[:, 0]
    query_scale = lax.rsqrt(extra[:, 1] + extra[:, 2] + unit_epsilon)
    raw = contract_rows(vecs, q)
    weights = live * jnp.exp(score_scale * raw * query_scale[None, :] * vec_scale)
    k = jnp.arange(cores * passes, dtype=jnp.int32)
    doc = chip * (cores * docs) + k // most
    hit = (positive[None, :] == doc.astype(f32)[:, None]).astype(f32)
    mass = jnp.stack([jnp.sum(weights, axis=0), jnp.sum(weights * hit, axis=0)])
    mass = copies_to_all(mass.reshape(8, -1), ("x", "z"), chips).sum(axis=0).reshape(2, -1)
    total, held = mass[0], mass[1]
    loss = jnp.log(total) - jnp.log(held)
    own_loss = lax.dynamic_slice_in_dim(loss, chip * share, share)

    coef = (loss_seed * score_scale) * query_scale[None, :] * (
        weights / total[None, :] - hit * weights / held[None, :]
    )
    grad = jnp.dot(coef.astype(bf16), q, preferred_element_type=f32)
    term = jnp.sum(coef * raw, axis=1, keepdims=True)
    grad = jnp.concatenate([grad, jnp.broadcast_to(term, (cores * passes, L))], axis=1).astype(bf16)
    grad = jnp.broadcast_to(
        grad.reshape(cores, 1, passes, width + L), (cores, MP, passes, width + L)
    ).reshape(cores * MP, passes, width + L)
    grad = lax.all_to_all(grad, ("core", "mp"), split_axis=0, concat_axis=0, tiled=True)
    grad = grad.astype(f32).sum(axis=0)
    own_vec = lax.dynamic_slice_in_dim(vec_float, core * passes, passes)
    scale = lax.dynamic_slice_in_dim(vec_scale, core * passes, passes)
    change = scale * grad[:, :width] - own_vec * (scale**3 * grad[:, width : width + 1])
    token_grad = (change / divisor).astype(bf16)

    tensors = (w_gate, w_up, w_down)
    none = jnp.zeros((2 * passes, pool.shape[1]), bf16)
    high, low, g = back(m, (2,), 256, True, a, b, c, token_grad, none, *tensors)
    from_right = shifted(high, -1)
    from_left = shifted(low, 1)
    right, left = back(m, (1, 3), 512, False, a, b, c, g, none, *tensors)
    right, left = add_halves(right, left, from_left, from_right)
    right, left, g = lax.optimization_barrier((right, left, g))
    right = shifted(right, 1)
    left = shifted(left, -1)
    g_high = g.astype(bf16)
    gs = jnp.concatenate([g_high, (g - g_high.astype(f32)).astype(bf16)], axis=0)
    own, s = back(m, (0,), 512, False, a, b, c, g, gs, *tensors)
    small = jnp.concatenate(
        [s.reshape(passes, L), jnp.pad(own_loss[None, :], ((0, 7), (0, L - share)))], axis=0
    )
    small = copies_to_all(small, "mp", MP)
    inner = small[:, :passes].sum(axis=0).reshape(passes // 2, 2, L) / width
    query_loss = small[:, passes, :share].reshape(MP * share)
    own_gain = lax.dynamic_slice_in_dim(norm_gain, mi * part, part)[None, :]
    own_token = lax.dynamic_slice_in_dim(token_grad, mi * part, part, axis=1).astype(f32)
    rest = (rms, inner, mask, own_token, own_gain)
    hidden_grad = finish(hidden_in, own, right, left, *rest)
    return query_loss, hidden_grad


def solution(mesh):
    shape = (4, 4, 2, MP)
    split = Mesh(mesh.devices.reshape(shape), ("x", "z", "core", "mp"))
    dp = ("x", "z", "core")
    return jax.shard_map(
        per_device,
        mesh=split,
        in_specs=(
            P(dp, "mp"),
            P(dp),
            P(dp),
            P(dp),
            P(dp, "mp"),
            P(),
            P(None, "mp"),
            P(None, "mp"),
            P("mp", None),
        ),
        out_specs=(P(dp), P(dp, "mp")),
        check_vma=False,
    )
```

```python
import functools

import jax
import jax.numpy as jnp
from jax import lax
from jax.experimental import pallas as pl
from jax.experimental.pallas import tpu as pltpu
from jax.sharding import Mesh, PartitionSpec as P

L = 128
pad_token = 128001
score_scale = 20.0
loss_seed = 4096.0
norm_epsilon = 1e-05
unit_epsilon = 1e-06
MP = 4
FT = 256
SCOPED = 40 << 20
bf16 = jnp.bfloat16
f32 = jnp.float32


def shifted(x, by):
    return lax.ppermute(x, "mp", [(i, (i + by) % MP) for i in range(MP)])


def across(left, right):
    half = left.shape[0] // 2
    return shifted(left[:half], 1), shifted(right[half:], -1)


def swapped(x):
    return lax.ppermute(x, "core", [(0, 1), (1, 0)])


def copies_to_all(x, axes, count):
    return lax.all_to_all(
        jnp.broadcast_to(x, (count, *x.shape)), axes, split_axis=0, concat_axis=0, tiled=True
    )


def in_hbm(x):
    return pltpu.with_memory_space_constraint(x, pltpu.HBM)


def contract_rows(left, right):
    return lax.dot_general(
        left, right, (((1,), (1,)), ((), ())), preferred_element_type=f32
    )


def each(count, body):
    def step(n, carry):
        body(n)
        return carry

    lax.fori_loop(0, count, step, 0)


anywhere = pl.BlockSpec(memory_space=pl.ANY)
vmem = pl.BlockSpec(memory_space=pltpu.VMEM)
smem = pl.BlockSpec(memory_space=pltpu.SMEM)


def loop_copies(copies, count):
    def start(n):
        for copy in copies(n):
            copy.start()

    each(count, start)


def weight_tiles(m, steps, part, wg_ref, wu_ref, w, sem):
    def copies(n):
        columns = pl.ds(pl.multiple_of(n * FT, FT), FT)
        return [
            pltpu.make_async_copy(
                ref.at[pl.ds(pl.multiple_of(lax.rem(m + step, MP) * part, part), part), columns],
                w.at[n, pl.ds(k * part, part), pl.ds(i * FT, FT)],
                sem.at[n, 2 * k + i],
            )
            for k, step in enumerate(steps)
            for i, ref in enumerate((wg_ref, wu_ref))
        ]

    return copies


def encode_near_kernel(steps, m_ref, *refs):
    count = len(steps)
    pieces, (gain_ref, wg_ref, wu_ref), refs = refs[:count], refs[count : count + 3], refs[count + 3 :]
    own = count == 1
    if own:
        mask_ref, acc_out, square_ref, xpool_ref = refs[:4]
        xin, xs, w, acc, in_sem, w_sem, out_sem = refs[4:]
    else:
        acc_in, square_in, acc_out, square_ref = refs[:4]
        xin, xs, w, acc, in_sem, w_sem, out_sem, acc_sem = refs[4:]
    rows, part = pieces[0].shape
    tiles = w.shape[0]
    m = m_ref[0]
    arriving = [pltpu.make_async_copy(ref, xin.at[k], in_sem.at[k]) for k, ref in enumerate(pieces)]
    for copy in arriving:
        copy.start()
    weights = weight_tiles(m, steps, part, wg_ref, wu_ref, w, w_sem)

    def inputs(n):
        more = [] if own else [pltpu.make_async_copy(acc_in.at[n], acc.at[n], acc_sem.at[n])]
        return weights(n) + more

    loop_copies(inputs, tiles)
    for copy in arriving:
        copy.wait()

    def scale(p):
        at = pl.ds(pl.multiple_of(p * L, L), L)
        total = None if own else square_in[at]
        for k, step in enumerate(steps):
            v = xin[k, at].astype(f32)
            square = jnp.sum(v * v, axis=1, keepdims=True)
            total = square if total is None else total + square
            xs[at, k * part : (k + 1) * part] = (v * gain_ref[lax.rem(m + step, MP)]).astype(bf16)
            if own:
                xpool_ref[pl.ds(p, 1)] = jnp.sum(v * mask_ref[at], axis=0, keepdims=True)
        square_ref[at] = total

    each(rows // L, scale)

    def leaving(n):
        return pltpu.make_async_copy(acc.at[n], acc_out.at[n], out_sem.at[n])

    def multiply(n):
        for copy in inputs(n):
            copy.wait()
        product = jnp.dot(xs[...], w[n], preferred_element_type=f32)
        acc[n] = product if own else acc[n] + product
        leaving(n).start()

    each(tiles, multiply)
    each(tiles, lambda n: leaving(n).wait())


def encode_near(m, steps, pieces, gain, w_gate, w_up, *rest):
    own = len(steps) == 1
    rows, part = pieces[0].shape
    width, ff = w_gate.shape
    tiles = ff // FT
    count = len(steps)
    rest = rest if own else (in_hbm(rest[0]), rest[1])
    return pl.pallas_call(
        functools.partial(encode_near_kernel, steps),
        in_specs=[smem]
        + [anywhere] * count
        + [vmem, anywhere, anywhere]
        + ([vmem] if own else [anywhere, vmem]),
        out_specs=[anywhere, vmem] + [vmem] * own,
        out_shape=[
            pltpu.HBM((tiles, rows, 2 * FT), f32),
            jax.ShapeDtypeStruct((rows, 1), f32),
        ]
        + [jax.ShapeDtypeStruct((rows // L, part), f32)] * own,
        scratch_shapes=[
            pltpu.VMEM((count, rows, part), bf16),
            pltpu.VMEM((rows, count * part), bf16),
            pltpu.VMEM((tiles, count * part, 2 * FT), bf16),
            pltpu.VMEM((tiles, rows, 2 * FT), f32),
            pltpu.SemaphoreType.DMA((count,)),
            pltpu.SemaphoreType.DMA((tiles, 2 * count)),
            pltpu.SemaphoreType.DMA((tiles,)),
        ]
        + [pltpu.SemaphoreType.DMA((tiles,))] * (not own),
        compiler_params=pltpu.CompilerParams(vmem_limit_bytes=SCOPED),
        cost_estimate=pl.CostEstimate(
            flops=count * rows * width * ff, transcendentals=0, bytes_accessed=4 * rows * width
        ),
        name="encode_near",
    )(m, *map(in_hbm, pieces), gain, in_hbm(w_gate), in_hbm(w_up), *rest)


def encode_far_kernel(
    m_ref, high_ref, low_ref, acc_ref, square_ref, mask_ref, gain_ref, wg_ref, wu_ref,
    a_out, b_out, c_out, pool_ref, rms_ref, xin, xs, w, acc, results, in_sem, w_sem, acc_sem, out_sem,
):
    rows, part = xin.shape
    half = rows // 2
    tiles = w.shape[0]
    m = m_ref[0]
    arriving = [
        pltpu.make_async_copy(ref, xin.at[pl.ds(k * half, half)], in_sem.at[k])
        for k, ref in enumerate((high_ref, low_ref))
    ]
    for copy in arriving:
        copy.start()
    weights = weight_tiles(m, (2,), part, wg_ref, wu_ref, w, w_sem)

    def inputs(n):
        return [*weights(n), pltpu.make_async_copy(acc_ref.at[n], acc.at[n], acc_sem.at[n])]

    loop_copies(inputs, tiles)
    for copy in arriving:
        copy.wait()

    def scale(p):
        at = pl.ds(pl.multiple_of(p * L, L), L)
        v = xin[at].astype(f32)
        total = square_ref[at] + jnp.sum(v * v, axis=1, keepdims=True)
        rms_ref[at] = lax.rsqrt(total / (MP * part) + norm_epsilon)
        xs[at] = (v * gain_ref[lax.rem(m + 2, MP)]).astype(bf16)

    each(rows // L, scale)

    def leaving(n):
        return [
            pltpu.make_async_copy(
                results.at[n, i],
                out.at[:, pl.ds(pl.multiple_of(n * FT, FT), FT)],
                out_sem.at[n, i],
            )
            for i, out in enumerate((a_out, b_out, c_out))
        ]

    def multiply(n):
        for copy in inputs(n):
            copy.wait()
        for r in range(2):
            at = slice(r * half, (r + 1) * half)
            both = acc[n, at] + jnp.dot(xs[at], w[n], preferred_element_type=f32)
            both *= rms_ref[at]
            gate, up = both[:, :FT], both[:, FT:]
            mask = mask_ref[at]
            sig = jax.nn.sigmoid(gate)
            up = up * mask
            b = gate * sig
            bu = b * up
            act = bu.astype(bf16).astype(f32)
            for p in range(half // L):
                q = r * (half // L) + p
                pool_ref[n, q : q + 1] = jnp.sum(act[p * L : (p + 1) * L], axis=0, keepdims=True)
            a = up * (sig + b * (1.0 - sig))
            results[n, 0, at] = a.astype(bf16)
            results[n, 1, at] = (b * mask).astype(bf16)
            results[n, 2, at] = (a * gate + bu).astype(bf16)
        for copy in leaving(n):
            copy.start()

    each(tiles, multiply)

    def wait(n):
        for copy in leaving(n):
            copy.wait()

    each(tiles, wait)


def encode_far(m, high, low, acc, square, mask, gain, w_gate, w_up):
    half, part = high.shape
    rows = 2 * half
    width, ff = w_gate.shape
    tiles = ff // FT
    return pl.pallas_call(
        encode_far_kernel,
        in_specs=[smem] + [anywhere] * 3 + [vmem] * 3 + [anywhere] * 2,
        out_specs=[anywhere] * 3 + [vmem] * 2,
        out_shape=[pltpu.HBM((rows, ff), bf16)] * 3
        + [
            jax.ShapeDtypeStruct((tiles, rows // L, FT), f32),
            jax.ShapeDtypeStruct((rows, 1), f32),
        ],
        scratch_shapes=[
            pltpu.VMEM((rows, part), bf16),
            pltpu.VMEM((rows, part), bf16),
            pltpu.VMEM((tiles, part, 2 * FT), bf16),
            pltpu.VMEM((tiles, rows, 2 * FT), f32),
            pltpu.VMEM((tiles, 3, rows, FT), bf16),
            pltpu.SemaphoreType.DMA((2,)),
            pltpu.SemaphoreType.DMA((tiles, 2)),
            pltpu.SemaphoreType.DMA((tiles,)),
            pltpu.SemaphoreType.DMA((tiles, 3)),
        ],
        compiler_params=pltpu.CompilerParams(vmem_limit_bytes=SCOPED),
        cost_estimate=pl.CostEstimate(
            flops=rows * width * ff, transcendentals=rows * ff, bytes_accessed=6 * rows * ff
        ),
        name="encode_far",
    )(m, *map(in_hbm, (high, low, acc)), square, mask, gain, in_hbm(w_gate), in_hbm(w_up))


def load_weights(m, steps, wg_ref, wu_ref, w, sem):
    part, ff = w.shape[1], wg_ref.shape[1]
    copies = []
    for k, step in enumerate(steps):
        at = pl.multiple_of(lax.rem(m + step, MP) * part, part)
        for i, ref in enumerate((wg_ref, wu_ref)):
            copies.append(
                pltpu.make_async_copy(
                    ref.at[pl.ds(at, part)], w.at[k, :, pl.ds(i * ff, ff)], sem.at[k, i]
                )
            )
    return copies


def back_kernel(steps, first, m_ref, a_ref, b_ref, c_ref, g_in, gs_ref, wg_ref, wu_ref, *refs):
    if first:
        wd_ref, *refs = refs
    count = 2 if first else len(steps)
    outs = refs[:count]
    last = not first and len(steps) == 1
    if first:
        g_ref, ab, w, in_sem, w_sem = refs[count:]
    elif last:
        s_ref, c, ab, w, in_sem, w_sem = refs[count:]
    else:
        ab, w, in_sem, w_sem = refs[count:]
    part = outs[0].shape[1]
    ff = a_ref.shape[1]
    tiles, rt, _ = ab.shape
    here = tiles // 2 if first else tiles
    weights = load_weights(m_ref[0], steps, wg_ref, wu_ref, w, w_sem)
    passes = g_in.shape[0]

    def arriving(r):
        at = pl.ds(pl.multiple_of(r * rt, rt), rt)
        copies = [
            pltpu.make_async_copy(ref.at[at], ab.at[r, :, pl.ds(i * ff, ff)], in_sem.at[r, i])
            for i, ref in enumerate((a_ref, b_ref))
        ]
        if last:
            copies.append(pltpu.make_async_copy(c_ref.at[at], c.at[r], in_sem.at[r, 2]))
        return copies

    for copy in arriving(0) + weights[:2]:
        copy.start()
    for r in range(1, tiles):
        for copy in arriving(r):
            copy.start()
    for copy in weights[2:]:
        copy.start()

    if first:

        step = ff // 2

        def dact_tile(n):
            at = pl.ds(pl.multiple_of(n * step, L), step)
            g_ref[:, at] = contract_rows(wd_ref[at], g_in[...]).T

        each(2, dact_tile)
        source = g_ref
    else:
        source = g_in

    def scale(r):
        for copy in arriving(r):
            copy.wait()
        lane = lax.broadcasted_iota(jnp.int32, (L, 2 * passes), 1)
        for p in range(rt // L):
            at = slice(p * L, (p + 1) * L)
            q = r * (rt // L) + p
            dact = source[pl.ds(q, 1)].astype(bf16)
            ab[r, at, :ff] = dact * ab[r, at, :ff]
            ab[r, at, ff:] = dact * ab[r, at, ff:]
            if last:
                sums = contract_rows(c[r, at], gs_ref[...])
                mine = (lane == q) | (lane == q + passes)
                s_ref[pl.ds(pl.multiple_of(q * L, L), L)] = jnp.sum(
                    jnp.where(mine, sums, 0.0), axis=1, keepdims=True
                )

    def multiply(j):
        k, r = j // tiles, lax.rem(j, tiles)

        @pl.when(k == 0)
        def _():
            scale(r)

        @pl.when(r == 0)
        def _():
            for i in range(2):
                pltpu.make_async_copy(
                    wg_ref.at[pl.ds(0, part)], w.at[k, :, pl.ds(i * ff, ff)], w_sem.at[k, i]
                ).wait()

        out = contract_rows(ab[r], w[k]).astype(bf16)
        at = pl.ds(pl.multiple_of(lax.rem(j, here) * rt, rt), rt)
        for i, ref in enumerate(outs):

            @pl.when(j // here == i)
            def _():
                ref[at] = out

    each(len(steps) * tiles, multiply)


def back(m, steps, rt, first, a, b, c, g, gs, w_gate, w_up, w_down):
    rows, ff = a.shape
    width = w_gate.shape[0]
    part = width // MP
    tiles = rows // rt
    last = not first and len(steps) == 1
    outs = [pltpu.HBM((rows // 2, part), bf16)] * 2
    if not first:
        outs = [pltpu.HBM((rows, part), bf16)] * len(steps)
    more = []
    scratch = []
    if first:
        more = [jax.ShapeDtypeStruct((g.shape[0], ff), f32)]
    elif last:
        more = [jax.ShapeDtypeStruct((rows, 1), f32)]
        scratch = [pltpu.VMEM((tiles, rt, ff), bf16)]
    return pl.pallas_call(
        functools.partial(back_kernel, steps, first),
        in_specs=[smem] + [anywhere] * 3 + [vmem] * 2 + [anywhere] * 2 + [vmem] * first,
        out_specs=[vmem] * (len(outs) + len(more)),
        out_shape=outs + more,
        scratch_shapes=scratch
        + [
            pltpu.VMEM((tiles, rt, 2 * ff), bf16),
            pltpu.VMEM((len(steps), part, 2 * ff), bf16),
            pltpu.SemaphoreType.DMA((tiles, 3)),
            pltpu.SemaphoreType.DMA((len(steps), 2)),
        ],
        compiler_params=pltpu.CompilerParams(vmem_limit_bytes=SCOPED),
        cost_estimate=pl.CostEstimate(flops=1, transcendentals=0, bytes_accessed=1),
        name="back",
    )(m, *map(in_hbm, (a, b, c)), g, gs, in_hbm(w_gate), in_hbm(w_up), *([w_down] if first else []))


def add_kernel(right_ref, left_ref, from_left_ref, from_right_ref, right_out, left_out):
    right_out[...] = (right_ref[...].astype(f32) + from_left_ref[...].astype(f32)).astype(bf16)
    left_out[...] = (left_ref[...].astype(f32) + from_right_ref[...].astype(f32)).astype(bf16)


def add_halves(right, left, from_left, from_right):
    half, part = from_left.shape
    upper = pl.BlockSpec((half, part), lambda r: (0, 0))
    lower = pl.BlockSpec((half, part), lambda r: (1, 0))
    return pl.pallas_call(
        add_kernel,
        grid=(1,),
        in_specs=[lower, upper, upper, upper],
        out_specs=[lower, upper],
        out_shape=[pltpu.HBM(right.shape, bf16)] * 2,
        input_output_aliases={0: 0, 1: 1},
        compiler_params=pltpu.CompilerParams(vmem_limit_bytes=8 << 20),
        cost_estimate=pl.CostEstimate(flops=1, transcendentals=0, bytes_accessed=1),
        name="add_halves",
    )(in_hbm(right), in_hbm(left), from_left, from_right)


def finish_kernel(
    x_ref, own_ref, one_ref, two_ref, rms_ref, inner_ref, mask_ref, token_ref, gain_ref, out_ref
):
    rms = rms_ref[...]
    eye = lax.broadcasted_iota(jnp.int32, (L, L), 0) == lax.broadcasted_iota(jnp.int32, (L, L), 1)
    inner = jnp.concatenate(
        [
            jnp.sum(jnp.where(eye, inner_ref[0, p : p + 1], 0.0), axis=1, keepdims=True)
            for p in range(out_ref.shape[0] // L)
        ],
        axis=0,
    )
    normed = own_ref[...].astype(f32) + one_ref[...].astype(f32) + two_ref[...].astype(f32)
    grad = rms * gain_ref[...] * normed - x_ref[...].astype(f32) * (rms * rms * inner)
    mask = mask_ref[...]
    for p in range(out_ref.shape[0] // L):
        part = slice(p * L, (p + 1) * L)
        out_ref[part] = (grad[part] + mask[part] * token_ref[0, p : p + 1]).astype(bf16)


def finish(x, own, one, two, rms, inner, mask, token, gain):
    rows, part = x.shape
    rt = 512
    whole = pl.BlockSpec((rt, part), lambda r: (r, 0))
    column = pl.BlockSpec((rt, 1), lambda r: (r, 0))
    return pl.pallas_call(
        finish_kernel,
        grid=(rows // rt,),
        in_specs=[
            whole,
            whole,
            whole,
            whole,
            column,
            pl.BlockSpec((1, rt // L, L), lambda r: (r, 0, 0)),
            column,
            pl.BlockSpec((1, rt // L, part), lambda r: (r, 0, 0)),
            pl.BlockSpec((1, part), lambda r: (0, 0)),
        ],
        out_specs=whole,
        out_shape=jax.ShapeDtypeStruct(x.shape, bf16),
        compiler_params=pltpu.CompilerParams(vmem_limit_bytes=16 << 20),
        name="finish",
    )(in_hbm(x), in_hbm(own), one, two, rms, inner, mask, token.reshape(-1, rt // L, part), gain)


def per_device(
    hidden_in, token_ids, passage_counts, positive_doc, queries, norm_gain, w_gate, w_up, w_down
):
    row_count, part = hidden_in.shape
    width = norm_gain.shape[0]
    docs = passage_counts.shape[0]
    passes = row_count // L
    most = passes // docs
    share = queries.shape[0] // MP
    chips = lax.axis_size(("x", "z"))
    cores = lax.axis_size("core")
    mi = lax.axis_index("mp")
    core = lax.axis_index("core")
    chip = lax.axis_index(("x", "z"))
    m = mi.astype(jnp.int32).reshape(1)

    def share_of(k):
        return lax.dynamic_slice_in_dim(queries, lax.rem(mi + k, MP) * share, share)

    mine = jnp.stack(
        [
            share_of(0),
            shifted(share_of(3), -1),
            shifted(share_of(2), 2),
            shifted(share_of(1), 1),
        ]
    )
    mine = lax.dynamic_slice_in_dim(jnp.concatenate([mine, mine], axis=0), MP - mi, MP)
    mine = jnp.moveaxis(mine, 0, 1).reshape(share, width)
    own_positive = lax.dynamic_slice_in_dim(positive_doc, mi * share, share)
    square = jnp.sum(mine.astype(f32) ** 2, axis=1)
    square_high = square.astype(bf16)
    square_low = (square - square_high.astype(f32)).astype(bf16)
    extra = jnp.stack([own_positive.astype(bf16), square_high, square_low], axis=1)
    extra = jnp.pad(extra, ((0, 0), (0, L - 3)))
    sent = jnp.concatenate([mine, extra], axis=1)

    right, left = shifted(hidden_in, -1), shifted(hidden_in, 1)
    live_pass = jnp.arange(passes, dtype=jnp.int32) % most < jnp.repeat(passage_counts, most)
    token_live = (token_ids.reshape(passes, L) != pad_token) & live_pass[:, None]
    live_float = token_live.astype(f32)
    mask = live_float.reshape(row_count, 1)
    weights = (norm_gain.reshape(MP, 1, part), w_gate, w_up)
    acc, square, own_x = encode_near(m, (0,), (hidden_in,), *weights, mask)
    right, left, sent, acc = lax.optimization_barrier((right, left, sent, acc))
    half = row_count // 2
    high, low = shifted(left[:half], 1), shifted(right[half:], -1)
    all_q = lax.all_gather(sent, ("x", "z"), axis=0)

    other_live = swapped(live_pass.astype(jnp.int32)) > 0
    live = jnp.where(
        core == 0,
        jnp.concatenate([live_pass, other_live]),
        jnp.concatenate([other_live, live_pass]),
    ).astype(f32)[:, None]
    divisor = jnp.maximum(jnp.sum(live_float, axis=1), 1.0)[:, None]

    acc, square = encode_near(m, (1, 3), (right, left), *weights, acc, square)
    a, b, c, pool, rms = encode_far(m, high, low, acc, square, mask, *weights)
    pool = jnp.moveaxis(pool, 0, 1).reshape(passes, -1)

    high = pool.astype(bf16)
    low = (pool - high.astype(f32)).astype(bf16)
    branch = jnp.dot(jnp.concatenate([high, low], 0), w_down, preferred_element_type=f32)
    own_x = (jnp.arange(MP) == mi)[None, :, None].astype(f32) * own_x[:, None, :]
    summed = (branch[:passes] + branch[passes:] + own_x.reshape(passes, width)) / divisor
    summed = copies_to_all(summed.astype(bf16), ("core", "mp"), cores * MP)
    summed = summed.reshape(cores, MP, passes, width).astype(f32).sum(axis=1)
    vecs = summed.reshape(cores * passes, width).astype(bf16)
    vec_float = vecs.astype(f32)
    vec_scale = lax.rsqrt(jnp.sum(vec_float * vec_float, axis=1, keepdims=True) + unit_epsilon)

    all_q = all_q.reshape(chips * share, width + L)
    q = all_q[:, :width]
    extra = all_q[:, width:].astype(f32)
    positive = extra[:, 0]
    query_scale = lax.rsqrt(extra[:, 1] + extra[:, 2] + unit_epsilon)
    raw = contract_rows(vecs, q)
    weights = live * jnp.exp(score_scale * raw * query_scale[None, :] * vec_scale)
    k = jnp.arange(cores * passes, dtype=jnp.int32)
    doc = chip * (cores * docs) + k // most
    hit = (positive[None, :] == doc.astype(f32)[:, None]).astype(f32)
    mass = jnp.stack([jnp.sum(weights, axis=0), jnp.sum(weights * hit, axis=0)])
    mass = copies_to_all(mass.reshape(8, -1), ("x", "z"), chips).sum(axis=0).reshape(2, -1)
    total, held = mass[0], mass[1]
    loss = jnp.log(total) - jnp.log(held)
    own_loss = lax.dynamic_slice_in_dim(loss, chip * share, share)

    coef = (loss_seed * score_scale) * query_scale[None, :] * (
        weights / total[None, :] - hit * weights / held[None, :]
    )
    grad = jnp.dot(coef.astype(bf16), q, preferred_element_type=f32)
    term = jnp.sum(coef * raw, axis=1, keepdims=True)
    grad = jnp.concatenate([grad, jnp.broadcast_to(term, (cores * passes, L))], axis=1).astype(bf16)
    grad = jnp.broadcast_to(
        grad.reshape(cores, 1, passes, width + L), (cores, MP, passes, width + L)
    ).reshape(cores * MP, passes, width + L)
    grad = lax.all_to_all(grad, ("core", "mp"), split_axis=0, concat_axis=0, tiled=True)
    grad = grad.astype(f32).sum(axis=0)
    own_vec = lax.dynamic_slice_in_dim(vec_float, core * passes, passes)
    scale = lax.dynamic_slice_in_dim(vec_scale, core * passes, passes)
    change = scale * grad[:, :width] - own_vec * (scale**3 * grad[:, width : width + 1])
    token_grad = (change / divisor).astype(bf16)

    tensors = (w_gate, w_up, w_down)
    none = jnp.zeros((2 * passes, pool.shape[1]), bf16)
    high, low, g = back(m, (2,), 512, True, a, b, c, token_grad, none, *tensors)
    from_right = shifted(high, -1)
    from_left = shifted(low, 1)
    right, left = back(m, (1, 3), 512, False, a, b, c, g, none, *tensors)
    right, left = add_halves(right, left, from_left, from_right)
    right, left, g = lax.optimization_barrier((right, left, g))
    right = shifted(right, 1)
    left = shifted(left, -1)
    g_high = g.astype(bf16)
    gs = jnp.concatenate([g_high, (g - g_high.astype(f32)).astype(bf16)], axis=0)
    own, s = back(m, (0,), 512, False, a, b, c, g, gs, *tensors)
    small = jnp.concatenate(
        [s.reshape(passes, L), jnp.pad(own_loss[None, :], ((0, 7), (0, L - share)))], axis=0
    )
    small = copies_to_all(small, "mp", MP)
    inner = small[:, :passes].sum(axis=0).reshape(passes // 4, 4, L) / width
    query_loss = small[:, passes, :share].reshape(MP * share)
    own_gain = lax.dynamic_slice_in_dim(norm_gain, mi * part, part)[None, :]
    own_token = lax.dynamic_slice_in_dim(token_grad, mi * part, part, axis=1).astype(f32)
    rest = (rms, inner, mask, own_token, own_gain)
    hidden_grad = finish(hidden_in, own, right, left, *rest)
    return query_loss, hidden_grad


def solution(mesh):
    shape = (4, 4, 2, MP)
    split = Mesh(mesh.devices.reshape(shape), ("x", "z", "core", "mp"))
    dp = ("x", "z", "core")
    return jax.shard_map(
        per_device,
        mesh=split,
        in_specs=(
            P(dp, "mp"),
            P(dp),
            P(dp),
            P(dp),
            P(dp, "mp"),
            P(),
            P(None, "mp"),
            P(None, "mp"),
            P("mp", None),
        ),
        out_specs=(P(dp), P(dp, "mp")),
        check_vma=False,
    )
```

```python
import functools

import jax
import jax.numpy as jnp
from jax import lax
from jax.experimental import pallas as pl
from jax.experimental.pallas import tpu as pltpu
from jax.sharding import Mesh, PartitionSpec as P

L = 128
pad_token = 128001
score_scale = 20.0
loss_seed = 4096.0
norm_epsilon = 1e-05
unit_epsilon = 1e-06
MP = 4
FT = 256
SCOPED = 40 << 20
bf16 = jnp.bfloat16
f32 = jnp.float32


def shifted(x, by):
    return lax.ppermute(x, "mp", [(i, (i + by) % MP) for i in range(MP)])


def across(left, right):
    half = left.shape[0] // 2
    return shifted(left[:half], 1), shifted(right[half:], -1)


def swapped(x):
    return lax.ppermute(x, "core", [(0, 1), (1, 0)])


def copies_to_all(x, axes, count):
    return lax.all_to_all(
        jnp.broadcast_to(x, (count, *x.shape)), axes, split_axis=0, concat_axis=0, tiled=True
    )


def in_hbm(x):
    return pltpu.with_memory_space_constraint(x, pltpu.HBM)


def contract_rows(left, right):
    return lax.dot_general(
        left, right, (((1,), (1,)), ((), ())), preferred_element_type=f32
    )


def each(count, body):
    def step(n, carry):
        body(n)
        return carry

    lax.fori_loop(0, count, step, 0)


anywhere = pl.BlockSpec(memory_space=pl.ANY)
vmem = pl.BlockSpec(memory_space=pltpu.VMEM)
smem = pl.BlockSpec(memory_space=pltpu.SMEM)


def loop_copies(copies, count):
    def start(n):
        for copy in copies(n):
            copy.start()

    each(count, start)


def weight_tiles(m, steps, part, wg_ref, wu_ref, w, sem):
    def copies(n):
        columns = pl.ds(pl.multiple_of(n * FT, FT), FT)
        return [
            pltpu.make_async_copy(
                ref.at[pl.ds(pl.multiple_of(lax.rem(m + step, MP) * part, part), part), columns],
                w.at[n, pl.ds(k * part, part), pl.ds(i * FT, FT)],
                sem.at[n, 2 * k + i],
            )
            for k, step in enumerate(steps)
            for i, ref in enumerate((wg_ref, wu_ref))
        ]

    return copies


def encode_near_kernel(steps, m_ref, *refs):
    count = len(steps)
    pieces, (gain_ref, wg_ref, wu_ref), refs = refs[:count], refs[count : count + 3], refs[count + 3 :]
    own = count == 1
    if own:
        mask_ref, acc_out, square_ref, xpool_ref = refs[:4]
        xin, xs, w, acc, in_sem, w_sem, out_sem = refs[4:]
    else:
        acc_in, square_in, acc_out, square_ref = refs[:4]
        xin, xs, w, acc, in_sem, w_sem, out_sem, acc_sem = refs[4:]
    rows, part = pieces[0].shape
    tiles = w.shape[0]
    m = m_ref[0]
    arriving = [pltpu.make_async_copy(ref, xin.at[k], in_sem.at[k]) for k, ref in enumerate(pieces)]
    for copy in arriving:
        copy.start()
    weights = weight_tiles(m, steps, part, wg_ref, wu_ref, w, w_sem)

    def inputs(n):
        more = [] if own else [pltpu.make_async_copy(acc_in.at[n], acc.at[n], acc_sem.at[n])]
        return weights(n) + more

    loop_copies(inputs, tiles)
    for copy in arriving:
        copy.wait()

    def scale(p):
        at = pl.ds(pl.multiple_of(p * L, L), L)
        total = None if own else square_in[at]
        for k, step in enumerate(steps):
            v = xin[k, at].astype(f32)
            square = jnp.sum(v * v, axis=1, keepdims=True)
            total = square if total is None else total + square
            xs[at, k * part : (k + 1) * part] = (v * gain_ref[lax.rem(m + step, MP)]).astype(bf16)
            if own:
                xpool_ref[pl.ds(p, 1)] = jnp.sum(v * mask_ref[at], axis=0, keepdims=True)
        square_ref[at] = total

    each(rows // L, scale)

    def leaving(n):
        return pltpu.make_async_copy(acc.at[n], acc_out.at[n], out_sem.at[n])

    def multiply(n):
        for copy in inputs(n):
            copy.wait()
        product = jnp.dot(xs[...], w[n], preferred_element_type=f32)
        acc[n] = product if own else acc[n] + product
        leaving(n).start()

    each(tiles, multiply)
    each(tiles, lambda n: leaving(n).wait())


def encode_near(m, steps, pieces, gain, w_gate, w_up, *rest):
    own = len(steps) == 1
    rows, part = pieces[0].shape
    width, ff = w_gate.shape
    tiles = ff // FT
    count = len(steps)
    rest = rest if own else (in_hbm(rest[0]), rest[1])
    return pl.pallas_call(
        functools.partial(encode_near_kernel, steps),
        in_specs=[smem]
        + [anywhere] * count
        + [vmem, anywhere, anywhere]
        + ([vmem] if own else [anywhere, vmem]),
        out_specs=[anywhere, vmem] + [vmem] * own,
        out_shape=[
            pltpu.HBM((tiles, rows, 2 * FT), f32),
            jax.ShapeDtypeStruct((rows, 1), f32),
        ]
        + [jax.ShapeDtypeStruct((rows // L, part), f32)] * own,
        scratch_shapes=[
            pltpu.VMEM((count, rows, part), bf16),
            pltpu.VMEM((rows, count * part), bf16),
            pltpu.VMEM((tiles, count * part, 2 * FT), bf16),
            pltpu.VMEM((tiles, rows, 2 * FT), f32),
            pltpu.SemaphoreType.DMA((count,)),
            pltpu.SemaphoreType.DMA((tiles, 2 * count)),
            pltpu.SemaphoreType.DMA((tiles,)),
        ]
        + [pltpu.SemaphoreType.DMA((tiles,))] * (not own),
        compiler_params=pltpu.CompilerParams(vmem_limit_bytes=SCOPED),
        cost_estimate=pl.CostEstimate(
            flops=count * rows * width * ff, transcendentals=0, bytes_accessed=4 * rows * width
        ),
        name="encode_near",
    )(m, *map(in_hbm, pieces), gain, in_hbm(w_gate), in_hbm(w_up), *rest)


def encode_far_kernel(
    m_ref, high_ref, low_ref, acc_ref, square_ref, mask_ref, gain_ref, wg_ref, wu_ref,
    a_out, b_out, c_out, pool_ref, rms_ref, xin, xs, w, acc, results, in_sem, w_sem, acc_sem, out_sem,
):
    rows, part = xin.shape
    half = rows // 2
    tiles = w.shape[0]
    m = m_ref[0]
    arriving = [
        pltpu.make_async_copy(ref, xin.at[pl.ds(k * half, half)], in_sem.at[k])
        for k, ref in enumerate((high_ref, low_ref))
    ]
    for copy in arriving:
        copy.start()
    weights = weight_tiles(m, (2,), part, wg_ref, wu_ref, w, w_sem)

    def inputs(n):
        return [*weights(n), pltpu.make_async_copy(acc_ref.at[n], acc.at[n], acc_sem.at[n])]

    loop_copies(inputs, tiles)
    for copy in arriving:
        copy.wait()

    def scale(p):
        at = pl.ds(pl.multiple_of(p * L, L), L)
        v = xin[at].astype(f32)
        total = square_ref[at] + jnp.sum(v * v, axis=1, keepdims=True)
        rms_ref[at] = lax.rsqrt(total / (MP * part) + norm_epsilon)
        xs[at] = (v * gain_ref[lax.rem(m + 2, MP)]).astype(bf16)

    each(rows // L, scale)

    def leaving(n):
        return [
            pltpu.make_async_copy(
                results.at[n, i],
                out.at[:, pl.ds(pl.multiple_of(n * FT, FT), FT)],
                out_sem.at[n, i],
            )
            for i, out in enumerate((a_out, b_out, c_out))
        ]

    def multiply(n):
        for copy in inputs(n):
            copy.wait()
        for r in range(2):
            at = slice(r * half, (r + 1) * half)
            both = acc[n, at] + jnp.dot(xs[at], w[n], preferred_element_type=f32)
            both *= rms_ref[at]
            gate, up = both[:, :FT], both[:, FT:]
            mask = mask_ref[at]
            sig = jax.nn.sigmoid(gate)
            up = up * mask
            b = gate * sig
            bu = b * up
            act = bu.astype(bf16).astype(f32)
            for p in range(half // L):
                q = r * (half // L) + p
                pool_ref[n, q : q + 1] = jnp.sum(act[p * L : (p + 1) * L], axis=0, keepdims=True)
            a = up * (sig + b * (1.0 - sig))
            results[n, 0, at] = a.astype(bf16)
            results[n, 1, at] = (b * mask).astype(bf16)
            results[n, 2, at] = (a * gate + bu).astype(bf16)
        for copy in leaving(n):
            copy.start()

    each(tiles, multiply)

    def wait(n):
        for copy in leaving(n):
            copy.wait()

    each(tiles, wait)


def encode_far(m, high, low, acc, square, mask, gain, w_gate, w_up):
    half, part = high.shape
    rows = 2 * half
    width, ff = w_gate.shape
    tiles = ff // FT
    return pl.pallas_call(
        encode_far_kernel,
        in_specs=[smem] + [anywhere] * 3 + [vmem] * 3 + [anywhere] * 2,
        out_specs=[anywhere] * 3 + [vmem] * 2,
        out_shape=[pltpu.HBM((rows, ff), bf16)] * 3
        + [
            jax.ShapeDtypeStruct((tiles, rows // L, FT), f32),
            jax.ShapeDtypeStruct((rows, 1), f32),
        ],
        scratch_shapes=[
            pltpu.VMEM((rows, part), bf16),
            pltpu.VMEM((rows, part), bf16),
            pltpu.VMEM((tiles, part, 2 * FT), bf16),
            pltpu.VMEM((tiles, rows, 2 * FT), f32),
            pltpu.VMEM((tiles, 3, rows, FT), bf16),
            pltpu.SemaphoreType.DMA((2,)),
            pltpu.SemaphoreType.DMA((tiles, 2)),
            pltpu.SemaphoreType.DMA((tiles,)),
            pltpu.SemaphoreType.DMA((tiles, 3)),
        ],
        compiler_params=pltpu.CompilerParams(vmem_limit_bytes=SCOPED),
        cost_estimate=pl.CostEstimate(
            flops=rows * width * ff, transcendentals=rows * ff, bytes_accessed=6 * rows * ff
        ),
        name="encode_far",
    )(m, *map(in_hbm, (high, low, acc)), square, mask, gain, in_hbm(w_gate), in_hbm(w_up))


def load_weights(m, steps, wg_ref, wu_ref, w, sem):
    part, ff = w.shape[1], wg_ref.shape[1]
    copies = []
    for k, step in enumerate(steps):
        at = pl.multiple_of(lax.rem(m + step, MP) * part, part)
        for i, ref in enumerate((wg_ref, wu_ref)):
            copies.append(
                pltpu.make_async_copy(
                    ref.at[pl.ds(at, part)], w.at[k, :, pl.ds(i * ff, ff)], sem.at[k, i]
                )
            )
    return copies


def back_kernel(steps, first, m_ref, a_ref, b_ref, c_ref, g_in, gs_ref, wg_ref, wu_ref, *refs):
    if first:
        wd_ref, *refs = refs
    count = 2 if first else len(steps)
    outs = refs[:count]
    last = not first and len(steps) == 1
    if first:
        g_ref, ab, w, in_sem, w_sem = refs[count:]
    elif last:
        s_ref, c, ab, w, in_sem, w_sem = refs[count:]
    else:
        ab, w, in_sem, w_sem = refs[count:]
    part = outs[0].shape[1]
    ff = a_ref.shape[1]
    tiles, rt, _ = ab.shape
    here = tiles // 2 if first else tiles
    weights = load_weights(m_ref[0], steps, wg_ref, wu_ref, w, w_sem)
    passes = g_in.shape[0]

    def arriving(r):
        at = pl.ds(pl.multiple_of(r * rt, rt), rt)
        copies = [
            pltpu.make_async_copy(ref.at[at], ab.at[r, :, pl.ds(i * ff, ff)], in_sem.at[r, i])
            for i, ref in enumerate((a_ref, b_ref))
        ]
        if last:
            copies.append(pltpu.make_async_copy(c_ref.at[at], c.at[r], in_sem.at[r, 2]))
        return copies

    for copy in arriving(0) + weights[:2]:
        copy.start()
    for r in range(1, tiles):
        for copy in arriving(r):
            copy.start()
    for copy in weights[2:]:
        copy.start()

    if first:

        step = ff // 2

        def dact_tile(n):
            at = pl.ds(pl.multiple_of(n * step, L), step)
            g_ref[:, at] = contract_rows(wd_ref[at], g_in[...]).T

        each(2, dact_tile)
        source = g_ref
    else:
        source = g_in

    def scale(r):
        for copy in arriving(r):
            copy.wait()
        lane = lax.broadcasted_iota(jnp.int32, (L, 2 * passes), 1)
        for p in range(rt // L):
            at = slice(p * L, (p + 1) * L)
            q = r * (rt // L) + p
            dact = source[pl.ds(q, 1)].astype(bf16)
            ab[r, at, :ff] = dact * ab[r, at, :ff]
            ab[r, at, ff:] = dact * ab[r, at, ff:]
            if last:
                sums = contract_rows(c[r, at], gs_ref[...])
                mine = (lane == q) | (lane == q + passes)
                s_ref[pl.ds(pl.multiple_of(q * L, L), L)] = jnp.sum(
                    jnp.where(mine, sums, 0.0), axis=1, keepdims=True
                )

    def multiply(j):
        k, r = j // tiles, lax.rem(j, tiles)

        @pl.when(k == 0)
        def _():
            scale(r)

        @pl.when(r == 0)
        def _():
            for i in range(2):
                pltpu.make_async_copy(
                    wg_ref.at[pl.ds(0, part)], w.at[k, :, pl.ds(i * ff, ff)], w_sem.at[k, i]
                ).wait()

        out = contract_rows(ab[r], w[k]).astype(bf16)
        at = pl.ds(pl.multiple_of(lax.rem(j, here) * rt, rt), rt)
        for i, ref in enumerate(outs):

            @pl.when(j // here == i)
            def _():
                ref[at] = out

    each(len(steps) * tiles, multiply)


def back(m, steps, rt, first, a, b, c, g, gs, w_gate, w_up, w_down):
    rows, ff = a.shape
    width = w_gate.shape[0]
    part = width // MP
    tiles = rows // rt
    last = not first and len(steps) == 1
    outs = [pltpu.HBM((rows // 2, part), bf16)] * 2
    if not first:
        outs = [pltpu.HBM((rows, part), bf16)] * len(steps)
    more = []
    scratch = []
    if first:
        more = [jax.ShapeDtypeStruct((g.shape[0], ff), f32)]
    elif last:
        more = [jax.ShapeDtypeStruct((rows, 1), f32)]
        scratch = [pltpu.VMEM((tiles, rt, ff), bf16)]
    return pl.pallas_call(
        functools.partial(back_kernel, steps, first),
        in_specs=[smem] + [anywhere] * 3 + [vmem] * 2 + [anywhere] * 2 + [vmem] * first,
        out_specs=[vmem] * (len(outs) + len(more)),
        out_shape=outs + more,
        scratch_shapes=scratch
        + [
            pltpu.VMEM((tiles, rt, 2 * ff), bf16),
            pltpu.VMEM((len(steps), part, 2 * ff), bf16),
            pltpu.SemaphoreType.DMA((tiles, 3)),
            pltpu.SemaphoreType.DMA((len(steps), 2)),
        ],
        compiler_params=pltpu.CompilerParams(vmem_limit_bytes=SCOPED),
        cost_estimate=pl.CostEstimate(flops=1, transcendentals=0, bytes_accessed=1),
        name="back",
    )(m, *map(in_hbm, (a, b, c)), g, gs, in_hbm(w_gate), in_hbm(w_up), *([w_down] if first else []))


def add_kernel(right_ref, left_ref, from_left_ref, from_right_ref, right_out, left_out):
    right_out[...] = (right_ref[...].astype(f32) + from_left_ref[...].astype(f32)).astype(bf16)
    left_out[...] = (left_ref[...].astype(f32) + from_right_ref[...].astype(f32)).astype(bf16)


def add_halves(right, left, from_left, from_right):
    half, part = from_left.shape
    rt = half // 2
    upper = pl.BlockSpec((rt, part), lambda r: (r, 0))
    lower = pl.BlockSpec((rt, part), lambda r: (r + 2, 0))
    return pl.pallas_call(
        add_kernel,
        grid=(2,),
        in_specs=[lower, upper, upper, upper],
        out_specs=[lower, upper],
        out_shape=[pltpu.HBM(right.shape, bf16)] * 2,
        input_output_aliases={0: 0, 1: 1},
        compiler_params=pltpu.CompilerParams(vmem_limit_bytes=8 << 20),
        cost_estimate=pl.CostEstimate(flops=1, transcendentals=0, bytes_accessed=1),
        name="add_halves",
    )(in_hbm(right), in_hbm(left), from_left, from_right)


def finish_kernel(
    x_ref, own_ref, one_ref, two_ref, rms_ref, inner_ref, mask_ref, token_ref, gain_ref, out_ref
):
    rms = rms_ref[...]
    eye = lax.broadcasted_iota(jnp.int32, (L, L), 0) == lax.broadcasted_iota(jnp.int32, (L, L), 1)
    inner = jnp.concatenate(
        [
            jnp.sum(jnp.where(eye, inner_ref[0, p : p + 1], 0.0), axis=1, keepdims=True)
            for p in range(out_ref.shape[0] // L)
        ],
        axis=0,
    )
    normed = own_ref[...].astype(f32) + one_ref[...].astype(f32) + two_ref[...].astype(f32)
    grad = rms * gain_ref[...] * normed - x_ref[...].astype(f32) * (rms * rms * inner)
    mask = mask_ref[...]
    for p in range(out_ref.shape[0] // L):
        part = slice(p * L, (p + 1) * L)
        out_ref[part] = (grad[part] + mask[part] * token_ref[0, p : p + 1]).astype(bf16)


def finish(x, own, one, two, rms, inner, mask, token, gain):
    rows, part = x.shape
    rt = 512
    whole = pl.BlockSpec((rt, part), lambda r: (r, 0))
    column = pl.BlockSpec((rt, 1), lambda r: (r, 0))
    return pl.pallas_call(
        finish_kernel,
        grid=(rows // rt,),
        in_specs=[
            whole,
            whole,
            whole,
            whole,
            column,
            pl.BlockSpec((1, rt // L, L), lambda r: (r, 0, 0)),
            column,
            pl.BlockSpec((1, rt // L, part), lambda r: (r, 0, 0)),
            pl.BlockSpec((1, part), lambda r: (0, 0)),
        ],
        out_specs=whole,
        out_shape=jax.ShapeDtypeStruct(x.shape, bf16),
        compiler_params=pltpu.CompilerParams(vmem_limit_bytes=16 << 20),
        name="finish",
    )(in_hbm(x), in_hbm(own), one, two, rms, inner, mask, token.reshape(-1, rt // L, part), gain)


def per_device(
    hidden_in, token_ids, passage_counts, positive_doc, queries, norm_gain, w_gate, w_up, w_down
):
    row_count, part = hidden_in.shape
    width = norm_gain.shape[0]
    docs = passage_counts.shape[0]
    passes = row_count // L
    most = passes // docs
    share = queries.shape[0] // MP
    chips = lax.axis_size(("x", "z"))
    cores = lax.axis_size("core")
    mi = lax.axis_index("mp")
    core = lax.axis_index("core")
    chip = lax.axis_index(("x", "z"))
    m = mi.astype(jnp.int32).reshape(1)

    def share_of(k):
        return lax.dynamic_slice_in_dim(queries, lax.rem(mi + k, MP) * share, share)

    opposite = shifted(share_of(2), 2)
    from_right, from_left = shifted(share_of(3), -1), shifted(share_of(1), 1)
    mine = jnp.stack([share_of(0), from_right, opposite, from_left])
    mine = lax.dynamic_slice_in_dim(jnp.concatenate([mine, mine], axis=0), MP - mi, MP)
    mine = jnp.moveaxis(mine, 0, 1).reshape(share, width)
    own_positive = lax.dynamic_slice_in_dim(positive_doc, mi * share, share)
    square = jnp.sum(mine.astype(f32) ** 2, axis=1)
    square_high = square.astype(bf16)
    square_low = (square - square_high.astype(f32)).astype(bf16)
    extra = jnp.stack([own_positive.astype(bf16), square_high, square_low], axis=1)
    extra = jnp.pad(extra, ((0, 0), (0, L - 3)))
    sent = jnp.concatenate([mine, extra], axis=1)

    right, left = shifted(hidden_in, -1), shifted(hidden_in, 1)
    live_pass = jnp.arange(passes, dtype=jnp.int32) % most < jnp.repeat(passage_counts, most)
    token_live = (token_ids.reshape(passes, L) != pad_token) & live_pass[:, None]
    live_float = token_live.astype(f32)
    mask = live_float.reshape(row_count, 1)
    weights = (norm_gain.reshape(MP, 1, part), w_gate, w_up)
    acc, square, own_x = encode_near(m, (0,), (hidden_in,), *weights, mask)
    right, left, sent, acc = lax.optimization_barrier((right, left, sent, acc))
    half = row_count // 2
    high, low = shifted(left[:half], 1), shifted(right[half:], -1)
    all_q = lax.all_gather(sent, ("x", "z"), axis=0)

    other_live = swapped(live_pass.astype(jnp.int32)) > 0
    live = jnp.where(
        core == 0,
        jnp.concatenate([live_pass, other_live]),
        jnp.concatenate([other_live, live_pass]),
    ).astype(f32)[:, None]
    divisor = jnp.maximum(jnp.sum(live_float, axis=1), 1.0)[:, None]

    acc, square = encode_near(m, (1, 3), (right, left), *weights, acc, square)
    a, b, c, pool, rms = encode_far(m, high, low, acc, square, mask, *weights)
    pool = jnp.moveaxis(pool, 0, 1).reshape(passes, -1)

    high = pool.astype(bf16)
    low = (pool - high.astype(f32)).astype(bf16)
    branch = jnp.dot(jnp.concatenate([high, low], 0), w_down, preferred_element_type=f32)
    own_x = (jnp.arange(MP) == mi)[None, :, None].astype(f32) * own_x[:, None, :]
    summed = (branch[:passes] + branch[passes:] + own_x.reshape(passes, width)) / divisor
    summed = copies_to_all(summed.astype(bf16), ("core", "mp"), cores * MP)
    summed = summed.reshape(cores, MP, passes, width).astype(f32).sum(axis=1)
    vecs = summed.reshape(cores * passes, width).astype(bf16)
    vec_float = vecs.astype(f32)
    vec_scale = lax.rsqrt(jnp.sum(vec_float * vec_float, axis=1, keepdims=True) + unit_epsilon)

    all_q = all_q.reshape(chips * share, width + L)
    q = all_q[:, :width]
    extra = all_q[:, width:].astype(f32)
    positive = extra[:, 0]
    query_scale = lax.rsqrt(extra[:, 1] + extra[:, 2] + unit_epsilon)
    raw = contract_rows(vecs, q)
    weights = live * jnp.exp(score_scale * raw * query_scale[None, :] * vec_scale)
    k = jnp.arange(cores * passes, dtype=jnp.int32)
    doc = chip * (cores * docs) + k // most
    hit = (positive[None, :] == doc.astype(f32)[:, None]).astype(f32)
    mass = jnp.stack([jnp.sum(weights, axis=0), jnp.sum(weights * hit, axis=0)])
    mass = copies_to_all(mass.reshape(8, -1), ("x", "z"), chips).sum(axis=0).reshape(2, -1)
    total, held = mass[0], mass[1]
    loss = jnp.log(total) - jnp.log(held)
    own_loss = lax.dynamic_slice_in_dim(loss, chip * share, share)

    coef = (loss_seed * score_scale) * query_scale[None, :] * (
        weights / total[None, :] - hit * weights / held[None, :]
    )
    grad = jnp.dot(coef.astype(bf16), q, preferred_element_type=f32)
    term = jnp.sum(coef * raw, axis=1, keepdims=True)
    grad = jnp.concatenate([grad, jnp.broadcast_to(term, (cores * passes, L))], axis=1).astype(bf16)
    grad = jnp.broadcast_to(
        grad.reshape(cores, 1, passes, width + L), (cores, MP, passes, width + L)
    ).reshape(cores * MP, passes, width + L)
    grad = lax.all_to_all(grad, ("core", "mp"), split_axis=0, concat_axis=0, tiled=True)
    grad = grad.astype(f32).sum(axis=0)
    own_vec = lax.dynamic_slice_in_dim(vec_float, core * passes, passes)
    scale = lax.dynamic_slice_in_dim(vec_scale, core * passes, passes)
    change = scale * grad[:, :width] - own_vec * (scale**3 * grad[:, width : width + 1])
    token_grad = (change / divisor).astype(bf16)

    tensors = (w_gate, w_up, w_down)
    none = jnp.zeros((2 * passes, pool.shape[1]), bf16)
    high, low, g = back(m, (2,), 512, True, a, b, c, token_grad, none, *tensors)
    from_right = shifted(high, -1)
    from_left = shifted(low, 1)
    right, left = back(m, (1, 3), 512, False, a, b, c, g, none, *tensors)
    right, left = add_halves(right, left, from_left, from_right)
    right, left, g = lax.optimization_barrier((right, left, g))
    right = shifted(right, 1)
    left = shifted(left, -1)
    g_high = g.astype(bf16)
    gs = jnp.concatenate([g_high, (g - g_high.astype(f32)).astype(bf16)], axis=0)
    own, s = back(m, (0,), 512, False, a, b, c, g, gs, *tensors)
    small = jnp.concatenate(
        [s.reshape(passes, L), jnp.pad(own_loss[None, :], ((0, 7), (0, L - share)))], axis=0
    )
    small = copies_to_all(small, "mp", MP)
    inner = small[:, :passes].sum(axis=0).reshape(passes // 4, 4, L) / width
    query_loss = small[:, passes, :share].reshape(MP * share)
    own_gain = lax.dynamic_slice_in_dim(norm_gain, mi * part, part)[None, :]
    own_token = lax.dynamic_slice_in_dim(token_grad, mi * part, part, axis=1).astype(f32)
    rest = (rms, inner, mask, own_token, own_gain)
    hidden_grad = finish(hidden_in, own, right, left, *rest)
    return query_loss, hidden_grad


def solution(mesh):
    shape = (4, 4, 2, MP)
    split = Mesh(mesh.devices.reshape(shape), ("x", "z", "core", "mp"))
    dp = ("x", "z", "core")
    return jax.shard_map(
        per_device,
        mesh=split,
        in_specs=(
            P(dp, "mp"),
            P(dp),
            P(dp),
            P(dp),
            P(dp, "mp"),
            P(),
            P(None, "mp"),
            P(None, "mp"),
            P("mp", None),
        ),
        out_specs=(P(dp), P(dp, "mp")),
        check_vma=False,
    )
```
